256 devices in a mesh: leaf: 32 (over x, y, core), front: 8 (over z).
Axes of the slice: x: 4, y: 4, z: 8, core: 2. Of those that a mesh axis runs over, the one named last changes fastest.
Arguments:
- child_updates: float32 [32768, 1024], P('leaf', 'front'), as said below
- initial_one: float32 [32768, 2048], P('leaf', 'front'), as said below
- initial_two: float32 [16384, 2048], P('leaf', 'front'), as said below
- pattern_one: int32 [16, 16, 16], replicated, may hold values 0 or 1
- pattern_two: int32 [8, 16, 16], replicated, may hold values 0 or 1
- parent_map_one: int32 [16, 2, 16], replicated, may hold values from 0 to 15, each once within a row
- parent_map_two: int32 [8, 2, 16], replicated, may hold values from 0 to 15, each once within a row
Outputs:
- factor_one: float32 [32768, 1024], P('leaf', 'front')
- factor_two: float32 [16384, 1024], P('leaf', 'front')
- schur_two: float32 [8192, 1024], P('leaf', 'front')
The draws below stay inside these ranges and needn't reach their ends.
Inputs may be any that keep to these rules, and one draw needn't show every extreme that they name: `parent_map_one`: each row is a permutation of 0 to 15; only its first 8 entries are used. `parent_map_two`: each row is a permutation of 0 to 15; only its first 8 entries are used. `initial_one`: each 2048 x 2048 front block is symmetric, and positive definite after any symmetric block mask. `initial_two`: each 2048 x 2048 front block is symmetric, and positive definite after any symmetric block mask. `child_updates`: each 1024 x 1024 matrix is symmetric positive definite.
All inputs are finite; a program needn't handle non-finite values.
Results may differ from the reference program's by a relative error of at most 0.0003.
Values sent between devices are 32-bit elements; how exact they have to be, the bound alone decides.
No kernel may reach another device: no remote copies, remote signals or barrier semaphores. Data moves between devices by JAX's collectives and lax.ppermute only.
A program may use at most 128 MiB of HBM per device.

```python
import math
import jax
import jax.numpy as jnp
from jax import lax

BLK = 128
SEP = 1024
UPD = 1024
FR = 2048
FB = 16
LEAVES = 32
FRONTS_ONE = 16
FRONTS_TWO = 8


def symmetric_fronts(key, front_count, order, diag_base):
    key_off, key_diag = jax.random.split(key)
    off_part = 0.7 * jax.random.normal(key_off, (front_count, order, order), jnp.float32)
    diag_part = diag_base + jax.random.uniform(key_diag, (front_count, order), jnp.float32, 0.0, 2.0)
    off_part = off_part / math.sqrt(order)
    sym_part = (off_part + jnp.swapaxes(off_part, 1, 2)) / math.sqrt(2.0)
    return sym_part + diag_part[:, :, None] * jnp.eye(order, dtype=jnp.float32)[None, :, :]


def coupled_updates(key, count, order):
    key_base, key_shift = jax.random.split(key)
    base = jax.random.normal(key_base, (count, order, order), jnp.float32)
    shift = 0.5 + jax.random.uniform(key_shift, (count, order), jnp.float32, 0.0, 0.25)
    product = jnp.einsum('lik,ljk->lij', base, base, precision=lax.Precision.HIGHEST) / order
    product = 0.5 * (product + jnp.swapaxes(product, 1, 2))
    return product + shift[:, :, None] * jnp.eye(order, dtype=jnp.float32)[None, :, :]


def draw_child_updates(key, part):
    return coupled_updates(jax.random.fold_in(key, 11), LEAVES, UPD).reshape(LEAVES * UPD, UPD)


def draw_initial_one(key, part):
    return symmetric_fronts(jax.random.fold_in(key, 12), FRONTS_ONE, FR, 2.0).reshape(FRONTS_ONE * FR, FR)


def draw_initial_two(key, part):
    return symmetric_fronts(jax.random.fold_in(key, 13), FRONTS_TWO, FR, 2.0).reshape(FRONTS_TWO * FR, FR)


def plant(entries, rng, low, high):
    longest = entries.shape.index(max(entries.shape))
    spots = []
    for shift in (0, 1):
        where = [jax.random.randint(jax.random.fold_in(rng, axis), (), 0, length) for axis, length in enumerate(entries.shape)]
        where[longest] = (where[longest] + shift) % entries.shape[longest]
        spots.append(tuple(where))
    return entries.at[spots[0]].set(low).at[spots[1]].set(high)


def setup_inputs(seed: int = 0) -> dict:
    streams_of = jax.random.split(jax.random.key(seed), 8)
    return {
        "child_updates": draw_child_updates(jax.random.fold_in(streams_of[7], 71), 0),
        "initial_one": draw_initial_one(jax.random.fold_in(streams_of[7], 71), 0),
        "initial_two": draw_initial_two(jax.random.fold_in(streams_of[7], 71), 0),
        "pattern_one": plant((jax.random.randint(streams_of[3], (FRONTS_ONE, FB, FB), 0, 2) < 1).astype(jnp.int32), jax.random.fold_in(streams_of[3], 1), 0, 1),
        "pattern_two": plant((jax.random.randint(streams_of[4], (FRONTS_TWO, FB, FB), 0, 2) < 1).astype(jnp.int32), jax.random.fold_in(streams_of[4], 1), 0, 1),
        "parent_map_one": jax.vmap(lambda own: jax.random.permutation(own, FB))(jax.random.split(streams_of[5], FRONTS_ONE * 2)).reshape((FRONTS_ONE, 2, FB)).astype(jnp.int32),
        "parent_map_two": jax.vmap(lambda own: jax.random.permutation(own, FB))(jax.random.split(streams_of[6], FRONTS_TWO * 2)).reshape((FRONTS_TWO, 2, FB)).astype(jnp.int32),
    }


HIGHEST = lax.Precision.HIGHEST

def one_front(inputs):
    initial, pattern, parent_map, children = inputs
    front_blocks = FR // BLK
    keep_blocks = (pattern == 1) | (pattern.T == 1) | jnp.eye(front_blocks, dtype=bool)
    keep_mask = jnp.repeat(jnp.repeat(keep_blocks, BLK, 0), BLK, 1).astype(jnp.float32)
    assembled = initial * keep_mask
    for child_side in range(2):
        block_map = parent_map[child_side, :UPD // BLK]
        row_index = (block_map[:, None] * BLK + jnp.arange(BLK, dtype=jnp.int32)[None, :]).reshape(-1)
        assembled = assembled.at[row_index[:, None], row_index[None, :]].add(children[child_side])
    blocked = assembled.reshape(front_blocks, BLK, front_blocks, BLK)
    corner = blocked[0::2, :, 0::2, :].reshape(SEP, SEP)
    lower_part = blocked[1::2, :, 0::2, :].reshape(UPD, SEP)
    trailing = blocked[1::2, :, 1::2, :].reshape(UPD, UPD)
    chol_block = jnp.linalg.cholesky(corner)
    below = jax.scipy.linalg.solve_triangular(chol_block, lower_part.T, lower=True).T
    schur_part = trailing - jnp.dot(below, below.T, precision=HIGHEST)
    factor_part = jnp.stack([chol_block.reshape(SEP // BLK, BLK, SEP), below.reshape(UPD // BLK, BLK, SEP)], axis=1).reshape(FR, SEP)
    return (factor_part, schur_part)

def one_level(initial, pattern, parent_map, children):
    front_count = pattern.shape[0]
    return lax.map(one_front, (initial.reshape(front_count, FR, FR), pattern, parent_map, children.reshape(front_count, 2, UPD, UPD)))

def reference(child_updates, initial_one, initial_two, pattern_one, pattern_two, parent_map_one, parent_map_two):
    factor_first, schur_first = one_level(initial_one, pattern_one, parent_map_one, child_updates)
    factor_second, schur_second = one_level(initial_two, pattern_two, parent_map_two, schur_first)
    return (factor_first.reshape(-1, SEP), factor_second.reshape(-1, SEP), schur_second.reshape(-1, UPD))
```

```python
import jax
import jax.numpy as jnp
from jax import lax
from jax.experimental import pallas as pl
from jax.experimental.pallas import tpu as pltpu
from jax.sharding import Mesh, PartitionSpec as P

BLK = 128
NB = 8
FB = 16
F32 = jnp.float32
BF16 = jnp.bfloat16
VMEM = pl.BlockSpec(memory_space=pltpu.VMEM)
SMEM = pl.BlockSpec(memory_space=pltpu.SMEM)
PARAMS = pltpu.CompilerParams(vmem_limit_bytes=58 * 1024 * 1024)
LEAF = ("x", "yh", "yl", "core")


def shape(*dims):
    return jax.ShapeDtypeStruct(dims, F32)


def packed_index(row, col):
    return col * NB - col * (col - 1) // 2 + row - col


def across(piece):
    return jnp.broadcast_to(piece, (8, BLK))


def factor_block(block):
    sub = lax.broadcasted_iota(jnp.int32, (8, BLK), 0)
    lane = lax.broadcasted_iota(jnp.int32, (8, BLK), 1)
    rows = [block[8 * g : 8 * g + 8] for g in range(16)]
    diag = jnp.zeros((8, BLK), F32)
    for t in range(16):
        cols = {}
        for b in range(8):
            for g in range(t, 16):
                cols[b, g] = across(rows[g][:, 8 * t + b : 8 * t + b + 1])
        for b in range(8):
            here = lane == 8 * t + b
            pivot = across(cols[b, t][b : b + 1])
            scale = lax.rsqrt(pivot)
            diag = jnp.where(here, pivot * scale, diag)
            low = {g: cols[b, g] * scale for g in range(t, 16)}
            for later in range(b + 1, 8):
                weight = across(low[t][later : later + 1])
                for g in range(t, 16):
                    cols[later, g] = cols[later, g] - low[g] * weight
            row = jnp.where(here, scale, across(rows[t][b : b + 1]) * scale)
            lower = jnp.where(here, 0.0, rows[t]) - low[t] * row
            rows[t] = jnp.where(sub == b, row, jnp.where(sub > b, lower, rows[t]))
            for g in range(t + 1, 16):
                rows[g] = jnp.where(here, 0.0, rows[g]) - low[g] * row
    full = jnp.concatenate(rows, 0)
    row_id = lax.broadcasted_iota(jnp.int32, (BLK, BLK), 0)
    col_id = lax.broadcasted_iota(jnp.int32, (BLK, BLK), 1)
    on_diag = jnp.broadcast_to(diag[0:1], (BLK, BLK))
    upper = jnp.where(col_id > row_id, full, jnp.where(col_id == row_id, on_diag, 0.0))
    return upper.T, jnp.where(col_id <= row_id, full, 0.0)


def halves(value):
    high = value.astype(BF16)
    return high, (value - high.astype(F32)).astype(BF16)


def dot_nt(left, right):
    return lax.dot_general(
        left, right, (((1,), (1,)), ((), ())), preferred_element_type=F32
    )


def dot_split(left, right):
    left_high, left_low = halves(left)
    right_high, right_low = halves(right)
    return dot_nt(
        jnp.concatenate([left_high, left_high, left_low], 1),
        jnp.concatenate([right_high, right_low, right_high], 1),
    )


def factor_corner(work, chol, inverse):
    order = NB * BLK

    def one_panel(step, carry):
        first = pl.multiple_of(step * BLK, BLK)
        lower, lower_inverse = factor_block(work[step, pl.ds(first, BLK), :])
        chol[step, pl.ds(first, BLK), :] = lower
        inverse[step] = lower_inverse
        for j in range(NB - 1):

            @pl.when(step == j)
            def _():
                start = BLK * (j + 1)
                panel = dot_split(work[j, start:, :], inverse[j])
                chol[j, start:, :] = panel
                high, low = halves(panel)
                left = jnp.concatenate([high, high, low], 1)
                right = jnp.concatenate([high, low, high], 1)
                for k in range(j + 1, NB, 2):
                    wide = min(2, NB - k)
                    top = BLK * k - start
                    update = dot_nt(left[top:], right[top : top + wide * BLK])
                    for w in range(wide):
                        work[k + w, BLK * k :, :] = (
                            work[k + w, BLK * k :, :] - update[:, w * BLK : (w + 1) * BLK]
                        )

        return carry

    for j in range(1, NB):
        chol[j, : j * BLK, :] = jnp.zeros((j * BLK, BLK), F32)
    lax.fori_loop(0, NB, one_panel, 0)


def solve_rows(right_side, chol, inverse, solved, solved_high, solved_low):
    for p in range(0, NB, 2):
        first, second = right_side(p), right_side(p + 1)
        if p:
            depth = range(p)
            left_high = jnp.concatenate([solved_high[k] for k in depth], 1)
            left_low = jnp.concatenate([solved_low[k] for k in depth], 1)
            right = jnp.concatenate([chol[k, p * BLK : (p + 2) * BLK, :] for k in depth], 1)
            right_high, right_low = halves(right)
            update = (
                dot_nt(left_high, right_high)
                + dot_nt(left_high, right_low)
                + dot_nt(left_low, right_high)
            )
            first = first - update[:, :BLK]
            second = second - update[:, BLK:]
        first = dot_split(first, inverse[p])
        second = second - dot_split(first, chol[p, (p + 1) * BLK : (p + 2) * BLK, :])
        second = dot_split(second, inverse[p + 1])
        for k, value in ((p, first), (p + 1, second)):
            solved[k] = value
            solved_high[k], solved_low[k] = halves(value)


def place_of(block_map, front, child, slots):
    for m in range(FB):
        slots[child, m] = -1
    for i in range(NB):
        slots[child, block_map[front, child, i]] = i


def kept(pattern, front, row, col):
    return (pattern[front, row, col] == 1) | (pattern[front, col, row] == 1) | (row == col)


def pack_kernel(ids, map_one, pattern_two, child, initial_two, packed, sep_two, row_two, tail_two):
    front_one, side, z, front_two, sub = ids[0], ids[1], ids[2], ids[3], ids[4]
    packed[...] = jnp.zeros_like(packed)
    for i in range(NB):
        packed[map_one[front_one, side, i]] = child[i * BLK : (i + 1) * BLK, :].T
    for r in range(4):
        for w in range(2):
            keep = kept(pattern_two, front_two, 4 * sub + r, 2 * z + w)
            tile = initial_two[r * BLK : (r + 1) * BLK, w * BLK : (w + 1) * BLK]
            tile = jnp.where(keep, tile, 0.0)
            if w == 0:
                sep_two[r % 2 * 2 + r // 2] = tile
            elif r % 2 == 0:
                row_two[r // 2] = tile.T
            else:
                tail_two[r // 2] = tile


def assemble_kernel(
    ids, map_one, pattern_one, own, other, initial, corner, lower, trailing, slots
):
    front_one, side, z = ids[0], ids[1], ids[2]
    place_of(map_one, front_one, 0, slots)
    place_of(map_one, front_one, 1, slots)
    for r in range(NB):
        row = NB * side + r
        for w in range(2):
            if r % 2 == 0 and w == 1:
                continue
            out = (lower if w == 0 else trailing) if r % 2 else corner
            keep = kept(pattern_one, front_one, row, 2 * z + w)
            tile = initial[r * BLK : (r + 1) * BLK, w * BLK : (w + 1) * BLK]
            out[r // 2] = jnp.where(keep, tile, 0.0)
            for source, child in ((own, side), (other, 1 - side)):
                index = slots[child, row]

                @pl.when(index >= 0)
                def _():
                    out[r // 2] = out[r // 2] + source[index, w]


def chol_kernel(ids, own, other, chol, inverse, work):
    side = ids[1]
    half = NB // 2 * BLK
    work[:, pl.ds(pl.multiple_of(side * half, half), half), :] = own[...]
    work[:, pl.ds(pl.multiple_of((1 - side) * half, half), half), :] = other[...]
    factor_corner(work, chol, inverse)


def rest_kernel(
    ids,
    chol,
    inverse,
    lower_own,
    lower_other,
    trail_own,
    trail_other,
    factor,
    packed,
    lower,
    solved,
    solved_high,
    solved_low,
    trail,
):
    side, z = ids[1], ids[2]
    half = NB // 2 * BLK
    for ref, own, other in ((lower, lower_own, lower_other), (trail, trail_own, trail_other)):
        ref[:, pl.ds(pl.multiple_of(side * half, half), half), :] = own[...]
        ref[:, pl.ds(pl.multiple_of((1 - side) * half, half), half), :] = other[...]
    solve_rows(lambda k: lower[k], chol, inverse, solved, solved_high, solved_low)
    for p in range(0, NB, 2):
        high = jnp.concatenate([solved_high[k, p * BLK :, :] for k in range(NB)], 1)
        low = jnp.concatenate([solved_low[k, p * BLK :, :] for k in range(NB)], 1)
        wide_high, wide_low = high[: 2 * BLK], low[: 2 * BLK]
        update = dot_nt(high, wide_high) + dot_nt(high, wide_low) + dot_nt(low, wide_high)
        for w in range(2):
            for i in range(p + w, NB):
                packed[packed_index(i, p + w)] = (
                    trail[p + w, i * BLK : (i + 1) * BLK, :]
                    - update[(i - p) * BLK : (i - p + 1) * BLK, w * BLK : (w + 1) * BLK]
                )
    for r in range(NB):
        source = solved if r % 2 else chol
        start = pl.multiple_of((side * (NB // 2) + r // 2) * BLK, BLK)
        factor[r * BLK : (r + 1) * BLK, :] = source[z, pl.ds(start, BLK), :]


def second_kernel(
    ids,
    map_two,
    corner_own,
    corner_yl,
    corner_core,
    corner_both,
    lower_own,
    row_own,
    row_yl,
    row_core,
    row_both,
    tail,
    child_half_own,
    child_half_other,
    child_far_own,
    child_far_other,
    factor,
    schur,
    work,
    chol,
    inverse,
    lower,
    solved,
    solved_high,
    solved_low,
    trail,
    slots,
):
    side, z, front, sub = ids[1], ids[2], ids[3], ids[4]
    mine = sub // 2
    for ref, yl, core in (
        (corner_own, mine, side),
        (corner_yl, 1 - mine, side),
        (corner_core, mine, 1 - side),
        (corner_both, 1 - mine, 1 - side),
    ):
        start = pl.multiple_of((yl * 2 + core) * 2 * BLK, 2 * BLK)
        work[:, pl.ds(start, 2 * BLK), :] = ref[...]
    lower[:, : 2 * BLK, :] = lower_own[...]
    for ref, yl, core in (
        (row_own, mine, side),
        (row_yl, 1 - mine, side),
        (row_core, mine, 1 - side),
        (row_both, 1 - mine, 1 - side),
    ):
        at = (yl * 2 + core) * 2
        for b in range(2):
            lower[at + b, 2 * BLK :, :] = ref[b]
    for r in range(2):
        trail[r] = tail[r]
    place_of(map_two, front, 0, slots)
    place_of(map_two, front, 1, slots)
    wanted = (2 * sub, 2 * sub + 1, z)

    for child in range(2):
        near = mine == child

        for i in range(NB):
            for k in range(i + 1):
                index = packed_index(i, k)
                half_id, at = divmod(index, 18)
                row, col = map_two[front, child, i], map_two[front, child, k]
                row_half, col_half = row // 2, col // 2
                row_odd, col_odd = row % 2, col % 2

                def block():
                    from_near = jnp.where(
                        side == half_id, child_half_own[at], child_half_other[at]
                    )
                    from_far = jnp.where(side == half_id, child_far_own[at], child_far_other[at])
                    return jnp.where(near, from_near, from_far)

                @pl.when((row_odd == 0) & (col_odd == 0) & (row_half >= col_half))
                def _():
                    start = pl.multiple_of(row_half * BLK, BLK)
                    work[col_half, pl.ds(start, BLK), :] += block()

                @pl.when((row_odd == 0) & (col_odd == 0) & (row_half < col_half))
                def _():
                    start = pl.multiple_of(col_half * BLK, BLK)
                    work[row_half, pl.ds(start, BLK), :] += block().T

                @pl.when((row_odd == 1) & (col_odd == 0))
                def _():
                    for slot, target in enumerate(wanted):

                        @pl.when(row_half == target)
                        def _():
                            lower[col_half, slot * BLK : (slot + 1) * BLK, :] += block()

                @pl.when((row_odd == 0) & (col_odd == 1))
                def _():
                    for slot, target in enumerate(wanted):

                        @pl.when(col_half == target)
                        def _():
                            lower[row_half, slot * BLK : (slot + 1) * BLK, :] += block().T

                @pl.when((row_odd == 1) & (col_odd == 1))
                def _():
                    for slot in range(2):

                        @pl.when((row_half == wanted[slot]) & (col_half == z))
                        def _():
                            trail[slot] += block()

                        if i != k:

                            @pl.when((col_half == wanted[slot]) & (row_half == z))
                            def _():
                                trail[slot] += block().T

    factor_corner(work, chol, inverse)
    solve_rows(lambda k: lower[k], chol, inverse, solved, solved_high, solved_low)
    high = jnp.concatenate([solved_high[k] for k in range(NB)], 1)
    low = jnp.concatenate([solved_low[k] for k in range(NB)], 1)
    left_high, left_low = high[: 2 * BLK], low[: 2 * BLK]
    right_high, right_low = high[2 * BLK :], low[2 * BLK :]
    update = (
        dot_nt(left_high, right_high)
        + dot_nt(left_high, right_low)
        + dot_nt(left_low, right_high)
    )
    for r in range(2):
        schur[r * BLK : (r + 1) * BLK, :] = trail[r] - update[r * BLK : (r + 1) * BLK, :]
        start = pl.multiple_of((2 * sub + r) * BLK, BLK)
        factor[2 * r * BLK : (2 * r + 1) * BLK, :] = chol[z, pl.ds(start, BLK), :]
        factor[(2 * r + 1) * BLK : (2 * r + 2) * BLK, :] = solved[z, r * BLK : (r + 1) * BLK, :]


def call(kernel, name, outs, specs, args, scratch=()):
    return pl.pallas_call(
        kernel,
        name=name,
        out_shape=outs,
        in_specs=specs,
        out_specs=[VMEM] * len(outs),
        scratch_shapes=list(scratch),
        compiler_params=PARAMS,
    )(*args)


def swap(value, axis):
    return lax.ppermute(value, axis, [(0, 1), (1, 0)])


def per_device(
    child_updates,
    initial_one,
    initial_two,
    pattern_one,
    pattern_two,
    parent_map_one,
    parent_map_two,
):
    x, yh, yl = lax.axis_index("x"), lax.axis_index("yh"), lax.axis_index("yl")
    core, z = lax.axis_index("core"), lax.axis_index("front")
    ids = jnp.stack([x * 4 + yh * 2 + yl, core, z, x * 2 + yh, yl * 2 + core]).astype(jnp.int32)
    panel = (NB, NB * BLK, BLK)

    packed, sep_two, row_two, tail_two = call(
        pack_kernel,
        "pack",
        [shape(FB, BLK, BLK), shape(4, BLK, BLK), shape(2, BLK, BLK), shape(2, BLK, BLK)],
        [SMEM, SMEM, SMEM, VMEM, VMEM],
        (ids, parent_map_one, pattern_two, child_updates, initial_two),
    )
    own = lax.all_to_all(packed.reshape(NB, 2, BLK, BLK), "front", 0, 0, tiled=True)
    other = swap(own, "core")
    corner, lower, trailing = call(
        assemble_kernel,
        "assemble",
        [shape(4, BLK, BLK)] * 3,
        [SMEM, SMEM, SMEM, VMEM, VMEM, VMEM],
        (ids, parent_map_one, pattern_one, own, other, initial_one),
        [pltpu.SMEM((2, FB), jnp.int32)],
    )

    def spread(value):
        flat = value.reshape(-1, BLK)
        return lax.all_gather(flat, "front", axis=0, tiled=False)

    corner_all = spread(corner)
    chol, inverse = call(
        chol_kernel,
        "chol",
        [shape(*panel), shape(NB, BLK, BLK)],
        [SMEM, VMEM, VMEM],
        (ids, corner_all, swap(corner_all, "core")),
        [pltpu.VMEM(panel, F32)],
    )
    lower_all = spread(lower)
    trail_all = spread(trailing)
    factor_one, schur_one = call(
        rest_kernel,
        "rest",
        [shape(NB * BLK, BLK), shape(36, BLK, BLK)],
        [SMEM] + [VMEM] * 6,
        (
            ids,
            chol,
            inverse,
            lower_all,
            swap(lower_all, "core"),
            trail_all,
            swap(trail_all, "core"),
        ),
        [pltpu.VMEM(panel, F32)] * 2
        + [pltpu.VMEM(panel, BF16)] * 2
        + [pltpu.VMEM(panel, F32)],
    )

    gathered_two = spread(sep_two)
    corner_near = gathered_two[:, : 2 * BLK]
    lower_near = gathered_two[:, 2 * BLK :]
    corner_yl = swap(corner_near, "yl")
    row_yl = swap(row_two, "yl")

    half_near = jnp.where(core == 0, schur_one[:18], schur_one[18:])
    half_far = swap(half_near, "yl")
    far_other = swap(half_far, "core")
    near_other = jnp.where(core == 0, schur_one[18:], schur_one[:18])
    factor_two, schur_two = call(
        second_kernel,
        "second",
        [shape(4 * BLK, BLK), shape(2 * BLK, BLK)],
        [SMEM, SMEM] + [VMEM] * 14,
        (
            ids,
            parent_map_two,
            corner_near,
            corner_yl,
            swap(corner_near, "core"),
            swap(corner_yl, "core"),
            lower_near,
            row_two,
            row_yl,
            swap(row_two, "core"),
            swap(row_yl, "core"),
            tail_two,
            half_near,
            near_other,
            half_far,
            far_other,
        ),
        [
            pltpu.VMEM(panel, F32),
            pltpu.VMEM(panel, F32),
            pltpu.VMEM((NB, BLK, BLK), F32),
            pltpu.VMEM((NB, 3 * BLK, BLK), F32),
            pltpu.VMEM((NB, 3 * BLK, BLK), F32),
            pltpu.VMEM((NB, 3 * BLK, BLK), BF16),
            pltpu.VMEM((NB, 3 * BLK, BLK), BF16),
            pltpu.VMEM((2, BLK, BLK), F32),
            pltpu.SMEM((2, FB), jnp.int32),
        ],
    )
    return factor_one, factor_two, schur_two


def solution(mesh):
    cut = Mesh(mesh.devices.reshape(4, 2, 2, 2, 8), LEAF + ("front",))
    tile = P(LEAF, "front")
    return jax.shard_map(
        per_device,
        mesh=cut,
        in_specs=(tile, tile, tile, P(), P(), P(), P()),
        out_specs=(tile, tile, tile),
        check_vma=False,
    )
```

```python
import jax
import jax.numpy as jnp
from jax import lax
from jax.experimental import pallas as pl
from jax.experimental.pallas import tpu as pltpu
from jax.sharding import Mesh, PartitionSpec as P

BLK = 128
NB = 8
FB = 16
F32 = jnp.float32
BF16 = jnp.bfloat16
VMEM = pl.BlockSpec(memory_space=pltpu.VMEM)
SMEM = pl.BlockSpec(memory_space=pltpu.SMEM)
ANY = pl.BlockSpec(memory_space=pl.ANY)
HALF = BLK // 2
CORNER_ROWS = 2 * BLK + HALF
CHILD_ROWS = 4 * BLK + HALF
LOWER_ROWS = 4 * BLK
PARAMS = pltpu.CompilerParams(vmem_limit_bytes=58 * 1024 * 1024)
LEAF = ("x", "yh", "yl", "core")


def shape(*dims):
    return jax.ShapeDtypeStruct(dims, F32)


def packed_index(row, col):
    return col * NB - col * (col - 1) // 2 + row - col


def across(piece):
    return jnp.broadcast_to(piece, (8, BLK))


def factor_block(block):
    sub = lax.broadcasted_iota(jnp.int32, (8, BLK), 0)
    lane = lax.broadcasted_iota(jnp.int32, (8, BLK), 1)
    rows = [block[8 * g : 8 * g + 8] for g in range(16)]
    diag = jnp.zeros((8, BLK), F32)
    for t in range(16):
        cols = {}
        for b in range(8):
            for g in range(t, 16):
                cols[b, g] = across(rows[g][:, 8 * t + b : 8 * t + b + 1])
        for b in range(8):
            here = lane == 8 * t + b
            pivot = across(cols[b, t][b : b + 1])
            scale = lax.rsqrt(pivot)
            diag = jnp.where(here, pivot * scale, diag)
            low = {g: cols[b, g] * scale for g in range(t, 16)}
            for later in range(b + 1, 8):
                weight = across(low[t][later : later + 1])
                for g in range(t, 16):
                    cols[later, g] = cols[later, g] - low[g] * weight
            row = jnp.where(here, scale, across(rows[t][b : b + 1]) * scale)
            lower = jnp.where(here, 0.0, rows[t]) - low[t] * row
            rows[t] = jnp.where(sub == b, row, jnp.where(sub > b, lower, rows[t]))
            for g in range(t + 1, 16):
                rows[g] = jnp.where(here, 0.0, rows[g]) - low[g] * row
    full = jnp.concatenate(rows, 0)
    row_id = lax.broadcasted_iota(jnp.int32, (BLK, BLK), 0)
    col_id = lax.broadcasted_iota(jnp.int32, (BLK, BLK), 1)
    on_diag = jnp.broadcast_to(diag[0:1], (BLK, BLK))
    upper = jnp.where(col_id > row_id, full, jnp.where(col_id == row_id, on_diag, 0.0))
    return upper.T, jnp.where(col_id <= row_id, full, 0.0)


def halves(value):
    high = value.astype(BF16)
    return high, (value - high.astype(F32)).astype(BF16)


def dot_nt(left, right):
    return lax.dot_general(
        left, right, (((1,), (1,)), ((), ())), preferred_element_type=F32
    )


def dot_split(left, right):
    left_high, left_low = halves(left)
    right_high, right_low = halves(right)
    return dot_nt(
        jnp.concatenate([left_high, left_high, left_low], 1),
        jnp.concatenate([right_high, right_low, right_high], 1),
    )


def factor_corner(work, chol, inverse):
    order = NB * BLK

    def one_panel(step, carry):
        first = pl.multiple_of(step * BLK, BLK)
        lower, lower_inverse = factor_block(work[step, pl.ds(first, BLK), :])
        chol[step, pl.ds(first, BLK), :] = lower
        inverse[step] = lower_inverse
        for j in range(NB - 1):

            @pl.when(step == j)
            def _():
                start = BLK * (j + 1)
                panel = dot_split(work[j, start:, :], inverse[j])
                chol[j, start:, :] = panel
                high, low = halves(panel)
                left = jnp.concatenate([high, high, low], 1)
                right = jnp.concatenate([high, low, high], 1)
                for k in range(j + 1, NB, 2):
                    wide = min(2, NB - k)
                    top = BLK * k - start
                    update = dot_nt(left[top:], right[top : top + wide * BLK])
                    for w in range(wide):
                        work[k + w, BLK * k :, :] = (
                            work[k + w, BLK * k :, :] - update[:, w * BLK : (w + 1) * BLK]
                        )

        return carry

    for j in range(1, NB):
        chol[j, : j * BLK, :] = jnp.zeros((j * BLK, BLK), F32)
    lax.fori_loop(0, NB, one_panel, 0)


def solve_rows(right_side, chol, inverse, solved, solved_high, solved_low):
    for p in range(0, NB, 2):
        first, second = right_side(p), right_side(p + 1)
        if p:
            depth = range(p)
            left_high = jnp.concatenate([solved_high[k] for k in depth], 1)
            left_low = jnp.concatenate([solved_low[k] for k in depth], 1)
            right = jnp.concatenate([chol[k, p * BLK : (p + 2) * BLK, :] for k in depth], 1)
            right_high, right_low = halves(right)
            update = (
                dot_nt(left_high, right_high)
                + dot_nt(left_high, right_low)
                + dot_nt(left_low, right_high)
            )
            first = first - update[:, :BLK]
            second = second - update[:, BLK:]
        first = dot_split(first, inverse[p])
        second = second - dot_split(first, chol[p, (p + 1) * BLK : (p + 2) * BLK, :])
        second = dot_split(second, inverse[p + 1])
        for k, value in ((p, first), (p + 1, second)):
            solved[k] = value
            solved_high[k], solved_low[k] = halves(value)


def kept(pattern, front, row, col):
    return (pattern[front, row, col] == 1) | (pattern[front, col, row] == 1) | (row == col)


def first_turn(core, z):
    return jnp.where((core == 0) & (z >= 4), 1, 0)


def send_blocks(tile, core, z, out):
    base = NB // 2 * core
    for turn in range(2):
        local = (z + first_turn(core, z) + turn) % 4
        block = tile[local]
        at = turn * BLK

        @pl.when(base + local >= z)
        def _():
            out[at : at + BLK, :] = block

        @pl.when(base + local < z)
        def _():
            out[at : at + BLK, :] = block.T

    block = tile[(z + 2) % 4]

    @pl.when(z % 4 < 2)
    def _():
        out[2 * BLK :, :] = block[:HALF, :]

    @pl.when(z % 4 >= 2)
    def _():
        out[2 * BLK :, :] = block.T[HALF:, :]


def static_blocks():
    where = {}
    for core in range(2):
        for z in range(NB):
            turn0 = 1 if core == 0 and z >= 4 else 0
            for turn in range(2):
                row = 4 * core + (z + turn0 + turn) % 4
                where[max(row, z), min(row, z)] = [(core * NB + z, turn * BLK, BLK)]
            if z // 4 == core:
                row = 4 * core + (z + 2) % 4
                key = (max(row, z), min(row, z))
                entry = (core * NB + z, 2 * BLK, HALF)
                known = where.setdefault(key, [])
                if z % 4 < 2:
                    known.insert(0, entry)
                else:
                    known.append(entry)
    return where


def send_child(child, z, out):
    for turn in range(4):
        row = (z + turn) % NB
        at = turn * BLK
        block = child[pl.ds(pl.multiple_of(row * BLK, BLK), BLK), :]

        @pl.when(row >= z)
        def _():
            out[at : at + BLK, :] = block

        @pl.when(row < z)
        def _():
            out[at : at + BLK, :] = block.T

    row = (z + 4) % NB
    block = child[pl.ds(pl.multiple_of(row * BLK, BLK), BLK), :]

    @pl.when(row > z)
    def _():
        out[4 * BLK :, :] = block[:HALF, :]

    @pl.when(row < z)
    def _():
        out[4 * BLK :, :] = block.T[HALF:, :]


def child_blocks():
    where = {}
    for z in range(NB):
        for turn in range(4):
            row = (z + turn) % NB
            where[max(row, z), min(row, z)] = [(z, turn * BLK, BLK)]
        row = (z + 4) % NB
        known = where.setdefault((max(row, z), min(row, z)), [])
        known.insert(0 if row > z else 1, (z, 4 * BLK, HALF))
    return where


def gathered_parts(children):
    where = child_blocks()

    def parts(child, i, k):
        return [children[child * NB + z, row : row + rows, :] for z, row, rows in where[i, k]]

    return parts


def packed_parts(children):
    def parts(child, i, k):
        half_id, at = divmod(packed_index(i, k), 18)
        return [children[child, half_id, at]]

    return parts


def turned(parts):
    block = parts[0] if len(parts) == 1 else jnp.concatenate(parts, 0)
    return block.T


def accumulate(ref, lead, start, parts):
    for part in parts:
        rows = part.shape[0]
        at = start if isinstance(start, int) else pl.multiple_of(start, HALF)
        ref[lead, pl.ds(at, rows), :] += part
        start = start + rows


def for_each_block(block_map, front, visit):
    def one_child(child, carry):
        for i in range(NB):
            for k in range(i + 1):
                visit(child, i, k, block_map[front, child, i], block_map[front, child, k])
        return carry

    lax.fori_loop(0, 2, one_child, 0)


def add_separators(block_map, front, parts, work):
    def visit(child, i, k, row, col):
        both = (row % 2 == 0) & (col % 2 == 0)

        @pl.when(both & (row >= col))
        def _():
            accumulate(work, col // 2, row // 2 * BLK, parts(child, i, k))

        if i != k:

            @pl.when(both & (row < col))
            def _():
                accumulate(work, row // 2, col // 2 * BLK, [turned(parts(child, i, k))])

    for_each_block(block_map, front, visit)


def masked_tile(initial, pattern, front, row, local, col):
    keep = kept(pattern, front, row, col)
    return jnp.where(keep, initial[local * BLK : (local + 1) * BLK, :], 0.0)


def pack_kernel(ids, pattern_one, child, initial, merged, columns, tile, sem):
    front_one, side, z = ids[0], ids[1], ids[2]
    copy = pltpu.make_async_copy(initial.at[:, :BLK], columns, sem)
    copy.start()
    send_child(child, z, merged.at[:CHILD_ROWS, :])
    copy.wait()
    for r in range(4):
        tile[r] = masked_tile(columns, pattern_one, front_one, NB * side + 2 * r, 2 * r, 2 * z)
    send_blocks(tile, side, z, merged.at[CHILD_ROWS:, :])


def mask_kernel(
    ids,
    pattern_one,
    pattern_two,
    initial_one,
    initial_two,
    merged,
    corner_two,
    lower_two,
    row_two,
    tail_two,
    tile,
):
    front_one, side, z, front_two, sub = ids[0], ids[1], ids[2], ids[3], ids[4]
    first, second = initial_one.at[:, :BLK], initial_one.at[:, BLK:]
    for r in range(4):
        row = NB * side + 2 * r + 1
        merged[r * BLK : (r + 1) * BLK, :] = masked_tile(
            first, pattern_one, front_one, row, 2 * r + 1, 2 * z
        )
        tile[r] = masked_tile(second, pattern_one, front_one, row, 2 * r + 1, 2 * z + 1)
    send_blocks(tile, side, z, merged.at[LOWER_ROWS:, :])
    for r in range(4):
        for w in range(2):
            columns = initial_two.at[:, w * BLK : (w + 1) * BLK]
            block = masked_tile(columns, pattern_two, front_two, 4 * sub + r, r, 2 * z + w)
            at = slice(r // 2 * BLK, (r // 2 + 1) * BLK)
            if w == 0:
                (corner_two if r % 2 == 0 else lower_two)[at, :] = block
            elif r % 2 == 0:
                row_two[at, :] = block.T
            else:
                tail_two[r // 2] = block


def chol_kernel(ids, block_map, gathered, chol, inverse, work, children, sems):
    front = ids[0]
    bulk = pltpu.make_async_copy(gathered.at[:, :CHILD_ROWS, :], children, sems.at[0])
    bulk.start()
    copies = []
    for (row, col), parts in static_blocks().items():
        start = row * BLK
        for piece, at, rows in parts:
            copies.append(
                pltpu.make_async_copy(
                    gathered.at[piece, CHILD_ROWS + at : CHILD_ROWS + at + rows, :],
                    work.at[col, start : start + rows, :],
                    sems.at[1 + len(copies)],
                )
            )
            start += rows
    for copy in copies:
        copy.start()
    for copy in copies:
        copy.wait()
    bulk.wait()
    add_separators(block_map, front, gathered_parts(children), work)
    factor_corner(work, chol, inverse)


def rest_kernel(
    ids,
    block_map,
    chol,
    inverse,
    gathered,
    merged,
    factor,
    mine,
    other,
    children,
    lower,
    solved,
    solved_high,
    solved_low,
    trail,
    sems,
):
    front, side, z = ids[0], ids[1], ids[2]
    half = NB // 2 * BLK
    copies = [pltpu.make_async_copy(gathered.at[:, :CHILD_ROWS, :], children, sems.at[0])]
    for core in range(2):
        copies.append(
            pltpu.make_async_copy(
                merged.at[core * NB : (core + 1) * NB, :LOWER_ROWS, :],
                lower.at[:, core * half : (core + 1) * half, :],
                sems.at[1 + core],
            )
        )
    for (row, col), parts in static_blocks().items():
        start = 0
        for piece, at, rows in parts:
            copies.append(
                pltpu.make_async_copy(
                    merged.at[piece, LOWER_ROWS + at : LOWER_ROWS + at + rows, :],
                    trail.at[packed_index(row, col), start : start + rows, :],
                    sems.at[len(copies)],
                )
            )
            start += rows
    for copy in copies:
        copy.start()
    for copy in copies:
        copy.wait()
    parts = gathered_parts(children)

    def visit(child, i, k, row, col):
        row_odd, col_odd = row % 2 == 1, col % 2 == 1
        row_half, col_half = row // 2, col // 2

        @pl.when(row_odd & ~col_odd)
        def _():
            accumulate(lower, col_half, row_half * BLK, parts(child, i, k))

        @pl.when(~row_odd & col_odd)
        def _():
            accumulate(lower, row_half, col_half * BLK, [turned(parts(child, i, k))])

        @pl.when(row_odd & col_odd & (row >= col))
        def _():
            accumulate(trail, packed_index(row_half, col_half), 0, parts(child, i, k))

        if i != k:

            @pl.when(row_odd & col_odd & (row < col))
            def _():
                index = packed_index(col_half, row_half)
                accumulate(trail, index, 0, [turned(parts(child, i, k))])

    for_each_block(block_map, front, visit)
    solve_rows(lambda k: lower[k], chol, inverse, solved, solved_high, solved_low)
    for p in range(0, NB, 2):
        high = jnp.concatenate([solved_high[k, p * BLK :, :] for k in range(NB)], 1)
        low = jnp.concatenate([solved_low[k, p * BLK :, :] for k in range(NB)], 1)
        wide_high, wide_low = high[: 2 * BLK], low[: 2 * BLK]
        update = dot_nt(high, wide_high) + dot_nt(high, wide_low) + dot_nt(low, wide_high)
        for w in range(2):
            for i in range(p + w, NB):
                index = packed_index(i, p + w)
                half_id, at = divmod(index, 18)
                block = trail[index] - update[
                    (i - p) * BLK : (i - p + 1) * BLK, w * BLK : (w + 1) * BLK
                ]

                @pl.when(side == half_id)
                def _():
                    mine[at] = block

                @pl.when(side != half_id)
                def _():
                    other[at] = block

    for r in range(NB):
        source = solved if r % 2 else chol
        start = pl.multiple_of((side * (NB // 2) + r // 2) * BLK, BLK)
        factor[r * BLK : (r + 1) * BLK, :] = source[z, pl.ds(start, BLK), :]


def fetch_children(side, mine, refs, children, sems):
    near_mine, near_other, far_mine, far_other = refs
    copies = []
    for n, (ref, child, half) in enumerate(
        (
            (near_mine, mine, side),
            (near_other, mine, 1 - side),
            (far_mine, 1 - mine, side),
            (far_other, 1 - mine, 1 - side),
        )
    ):
        copies.append(pltpu.make_async_copy(ref, children.at[child, half], sems.at[n]))
        copies[-1].start()
    return copies


def chol_two_kernel(
    ids,
    block_map,
    gathered,
    near_mine,
    near_other,
    far_mine,
    far_other,
    chol,
    inverse,
    work,
    children,
    sems,
):
    side, front, sub = ids[1], ids[3], ids[4]
    copies = fetch_children(
        side, sub // 2, (near_mine, near_other, far_mine, far_other), children, sems
    )
    for core in range(2):
        for n, y in ((0, sub // 2), (1, 1 - sub // 2)):
            start = pl.multiple_of(2 * (2 * y + core) * BLK, BLK)
            copies.append(
                pltpu.make_async_copy(
                    gathered.at[core * NB : (core + 1) * NB, 2 * n * BLK : 2 * (n + 1) * BLK, :],
                    work.at[:, pl.ds(start, 2 * BLK), :],
                    sems.at[4 + 2 * core + n],
                )
            )
            copies[-1].start()
    for copy in copies:
        copy.wait()
    add_separators(block_map, front, packed_parts(children), work)
    factor_corner(work, chol, inverse)


def tail_kernel(
    ids,
    map_two,
    chol,
    inverse,
    lower_near,
    rows_all,
    tail,
    near_mine,
    near_other,
    far_mine,
    far_other,
    factor,
    schur,
    children,
    lower,
    solved,
    solved_high,
    solved_low,
    trail,
    sems,
):
    side, z, front, sub = ids[1], ids[2], ids[3], ids[4]
    mine = sub // 2
    copies = fetch_children(
        side, mine, (near_mine, near_other, far_mine, far_other), children, sems
    )
    lower[:, : 2 * BLK, :] = lower_near[...]
    for s in range(4):
        for b in range(2):
            lower[2 * s + b, 2 * BLK :, :] = rows_all[s, b * BLK : (b + 1) * BLK, :]
    trail[...] = tail[...]
    for copy in copies:
        copy.wait()
    wanted = (2 * sub, 2 * sub + 1, z)

    def one_child(child, carry):
        for i in range(NB):
            for k in range(i + 1):
                half_id, at = divmod(packed_index(i, k), 18)
                row, col = map_two[front, child, i], map_two[front, child, k]
                row_half, col_half = row // 2, col // 2
                row_odd, col_odd = row % 2 == 1, col % 2 == 1

                @pl.when(row_odd & ~col_odd)
                def _():
                    for slot, target in enumerate(wanted):

                        @pl.when(row_half == target)
                        def _():
                            lower[col_half, slot * BLK : (slot + 1) * BLK, :] += children[
                                child, half_id, at
                            ]

                @pl.when(~row_odd & col_odd)
                def _():
                    for slot, target in enumerate(wanted):

                        @pl.when(col_half == target)
                        def _():
                            lower[row_half, slot * BLK : (slot + 1) * BLK, :] += children[
                                child, half_id, at
                            ].T

                @pl.when(row_odd & col_odd)
                def _():
                    for slot in range(2):

                        @pl.when((row_half == wanted[slot]) & (col_half == z))
                        def _():
                            trail[slot] += children[child, half_id, at]

                        if i != k:

                            @pl.when((col_half == wanted[slot]) & (row_half == z))
                            def _():
                                trail[slot] += children[child, half_id, at].T

        return carry

    lax.fori_loop(0, 2, one_child, 0)
    solve_rows(lambda k: lower[k], chol, inverse, solved, solved_high, solved_low)
    high = jnp.concatenate([solved_high[k] for k in range(NB)], 1)
    low = jnp.concatenate([solved_low[k] for k in range(NB)], 1)
    left_high, left_low = high[: 2 * BLK], low[: 2 * BLK]
    right_high, right_low = high[2 * BLK :], low[2 * BLK :]
    update = (
        dot_nt(left_high, right_high)
        + dot_nt(left_high, right_low)
        + dot_nt(left_low, right_high)
    )
    for r in range(2):
        schur[r * BLK : (r + 1) * BLK, :] = trail[r] - update[r * BLK : (r + 1) * BLK, :]
        start = pl.multiple_of((2 * sub + r) * BLK, BLK)
        factor[2 * r * BLK : (2 * r + 1) * BLK, :] = chol[z, pl.ds(start, BLK), :]
        factor[(2 * r + 1) * BLK : (2 * r + 2) * BLK, :] = solved[z, r * BLK : (r + 1) * BLK, :]


def call(kernel, name, outs, specs, args, scratch=(), flops=0):
    return pl.pallas_call(
        kernel,
        name=name,
        out_shape=outs,
        in_specs=specs,
        out_specs=[VMEM] * len(outs),
        scratch_shapes=list(scratch),
        compiler_params=PARAMS,
        cost_estimate=pl.CostEstimate(flops=flops, bytes_accessed=flops // 400, transcendentals=0)
        if flops
        else None,
    )(*args)


def swap(value, axis):
    return lax.ppermute(value, axis, [(0, 1), (1, 0)])


def per_device(
    child_updates,
    initial_one,
    initial_two,
    pattern_one,
    pattern_two,
    parent_map_one,
    parent_map_two,
):
    x, yh, yl = lax.axis_index("x"), lax.axis_index("yh"), lax.axis_index("yl")
    core, z = lax.axis_index("core"), lax.axis_index("front")
    ids = jnp.stack([x * 4 + yh * 2 + yl, core, z, x * 2 + yh, yl * 2 + core]).astype(jnp.int32)
    panel = (NB, NB * BLK, BLK)
    block = (BLK, BLK)

    (sent,) = call(
        pack_kernel,
        "pack",
        [shape(CHILD_ROWS + CORNER_ROWS, BLK)],
        [SMEM, SMEM, VMEM, ANY],
        (ids, pattern_one, child_updates, initial_one),
        [pltpu.VMEM((NB * BLK, BLK), F32), pltpu.VMEM((4, *block), F32), pltpu.SemaphoreType.DMA],
    )
    gathered = lax.all_gather(sent, ("core", "front"), axis=0, tiled=False)
    ids_mask, _ = lax.optimization_barrier((ids, sent))
    merged, corner_two, lower_two, row_two, tail_two = call(
        mask_kernel,
        "mask",
        [
            shape(LOWER_ROWS + CORNER_ROWS, BLK),
            shape(2 * BLK, BLK),
            shape(2 * BLK, BLK),
            shape(2 * BLK, BLK),
            shape(2, *block),
        ],
        [SMEM, SMEM, SMEM, VMEM, VMEM],
        (ids_mask, pattern_one, pattern_two, initial_one, initial_two),
        [pltpu.VMEM((4, *block), F32)],
    )
    corner_two = jnp.concatenate([corner_two, swap(corner_two, "yl")], 0)
    rows_all = lax.all_gather(row_two, ("yl", "core"), axis=0, tiled=False)
    merged, gathered, corner_two, rows_all = lax.optimization_barrier(
        (merged, gathered, corner_two, rows_all)
    )
    merged_all = lax.all_gather(merged, ("core", "front"), axis=0, tiled=False)
    children_one = pltpu.VMEM((2 * NB, CHILD_ROWS, BLK), F32)
    chol, inverse = call(
        chol_kernel,
        "chol",
        [shape(*panel), shape(NB, *block)],
        [SMEM, SMEM, ANY],
        (ids, parent_map_one, gathered),
        [pltpu.VMEM(panel, F32), children_one, pltpu.SemaphoreType.DMA((64,))],
        flops=40_000_000_000,
    )
    lower_two, _ = lax.optimization_barrier((lower_two, gathered))
    gathered_two = lax.all_gather(corner_two, ("core", "front"), axis=0, tiled=False)
    lower_near = lax.all_gather(lower_two, "front", axis=0, tiled=False)
    factor_one, near_mine, near_other = call(
        rest_kernel,
        "rest",
        [shape(NB * BLK, BLK), shape(18, *block), shape(18, *block)],
        [SMEM, SMEM, VMEM, VMEM, ANY, ANY],
        (ids, parent_map_one, chol, inverse, gathered, merged_all),
        [children_one]
        + [pltpu.VMEM(panel, F32)] * 2
        + [pltpu.VMEM(panel, BF16)] * 2
        + [pltpu.VMEM((36, *block), F32), pltpu.SemaphoreType.DMA((64,))],
        flops=15_000_000_000,
    )
    far_mine = swap(near_mine, "yl")
    far_other = swap(far_mine, "core")
    packed = (near_mine, near_other, far_mine, far_other)
    children = pltpu.VMEM((2, 2, 18, *block), F32)
    chol, inverse = call(
        chol_two_kernel,
        "chol_two",
        [shape(*panel), shape(NB, *block)],
        [SMEM, SMEM] + [ANY] * 5,
        (ids, parent_map_two, gathered_two, *packed),
        [pltpu.VMEM(panel, F32), children, pltpu.SemaphoreType.DMA((8,))],
        flops=40_000_000_000,
    )
    rows = (NB, 3 * BLK, BLK)
    factor_two, schur_two = call(
        tail_kernel,
        "tail",
        [shape(4 * BLK, BLK), shape(2 * BLK, BLK)],
        [SMEM, SMEM] + [VMEM] * 5 + [ANY] * 4,
        (ids, parent_map_two, chol, inverse, lower_near, rows_all, tail_two, *packed),
        [
            children,
            pltpu.VMEM(rows, F32),
            pltpu.VMEM(rows, F32),
            pltpu.VMEM(rows, BF16),
            pltpu.VMEM(rows, BF16),
            pltpu.VMEM((2, *block), F32),
            pltpu.SemaphoreType.DMA((4,)),
        ],
    )
    return factor_one, factor_two, schur_two


def solution(mesh):
    cut = Mesh(mesh.devices.reshape(4, 2, 2, 2, 8), LEAF + ("front",))
    tile = P(LEAF, "front")
    return jax.shard_map(
        per_device,
        mesh=cut,
        in_specs=(tile, tile, tile, P(), P(), P(), P()),
        out_specs=(tile, tile, tile),
        check_vma=False,
    )
```

```python
import jax
import jax.numpy as jnp
from jax import lax
from jax.experimental import pallas as pl
from jax.experimental.pallas import tpu as pltpu
from jax.sharding import Mesh, PartitionSpec as P

BLK = 128
NB = 8
FB = 16
F32 = jnp.float32
BF16 = jnp.bfloat16
VMEM = pl.BlockSpec(memory_space=pltpu.VMEM)
SMEM = pl.BlockSpec(memory_space=pltpu.SMEM)
ANY = pl.BlockSpec(memory_space=pl.ANY)
HALF = BLK // 2
CORNER_ROWS = 2 * BLK + HALF
CHILD_ROWS = 4 * BLK + HALF
LOWER_ROWS = 4 * BLK
PARAMS = pltpu.CompilerParams(vmem_limit_bytes=58 * 1024 * 1024)
LEAF = ("x", "yh", "yl", "core")


def shape(*dims):
    return jax.ShapeDtypeStruct(dims, F32)


def packed_index(row, col):
    return col * NB - col * (col - 1) // 2 + row - col


def across(piece):
    return jnp.broadcast_to(piece, (8, BLK))


def lane_columns(rows, t):
    return [across(rows[:, 8 * t + b : 8 * t + b + 1]) for b in range(8)]


def factor_eights(rows, first, last):
    sub = lax.broadcasted_iota(jnp.int32, (8, BLK), 0)
    lane = lax.broadcasted_iota(jnp.int32, (8, BLK), 1)
    diag = jnp.zeros((8, BLK), F32)
    outs = []
    following = lane_columns(rows[first], first)
    for t in range(first, last):
        head = following
        below = {g: lane_columns(rows[g], t) for g in range(t + 1, last)}
        if t + 1 < last:
            following = lane_columns(rows[t + 1], t + 1)
        scale, weight = [], {}
        for b in range(8):
            pivot = across(head[b][b : b + 1])
            scale.append(lax.rsqrt(pivot))
            diag = jnp.where(lane == 8 * t + b, pivot * scale[b], diag)
            low = head[b] * scale[b]
            for a in range(b + 1, 8):
                weight[a, b] = across(low[a : a + 1])
                head[a] = head[a] - low * weight[a, b]
        inside = (lane >= 8 * t) & (lane < 8 * t + 8)
        pivots = []
        for b in range(8):
            unit = jnp.where(lane == 8 * t + b, 1.0, 0.0)
            row = jnp.where(inside, unit, across(rows[t][b : b + 1]))
            for a in range(b):
                row = row - weight[b, a] * pivots[a]
            pivots.append(row * scale[b])
        for g in range(t + 1, last):
            lows = []
            for b in range(8):
                column = below[g][b]
                for a in range(b):
                    column = column - lows[a] * weight[b, a]
                lows.append(column * scale[b])
            if g == t + 1:
                for b in range(8):
                    for a in range(8):
                        following[a] = following[a] - lows[b] * across(lows[b][a : a + 1])
            group = jnp.where(inside, 0.0, rows[g])
            for b in range(8):
                group = group - lows[b] * pivots[b]
            rows[g] = group
        group = pivots[7]
        for b in range(6, -1, -1):
            group = jnp.where(sub == b, pivots[b], group)
        rows[t] = group
        for a in range(1, 8):
            column = weight[a, a - 1]
            for b in range(a - 2, -1, -1):
                column = jnp.where(sub == b, weight[a, b], column)
            group = jnp.where((lane == 8 * t + a) & (sub < a), column, group)
        outs.append(group)
    return outs, diag


def factor_block(block):
    rows = [block[8 * g : 8 * g + 8] for g in range(16)]
    outs, diag = factor_eights(rows, 0, 8)
    lane = lax.broadcasted_iota(jnp.int32, (8, BLK), 1)
    row_id = lax.broadcasted_iota(jnp.int32, (BLK // 2, BLK), 0)
    col_id = lax.broadcasted_iota(jnp.int32, (BLK // 2, BLK), 1)
    left = jnp.concatenate(rows[:8], 0)
    right = jnp.where((col_id > row_id) & (col_id < BLK // 2), 0.0, left)
    left_high, left_low = halves(left)
    right_high, right_low = halves(right)
    update = lax.dot_general(
        jnp.concatenate([left_high, left_high, left_low], 0),
        jnp.concatenate([right_high, right_low, right_high], 0),
        (((0,), (0,)), ((), ())),
        preferred_element_type=F32,
    )
    for g in range(8, 16):
        rows[g] = jnp.where(lane < BLK // 2, 0.0, rows[g]) - update[8 * g : 8 * g + 8]
    more, more_diag = factor_eights(rows, 8, 16)
    full = jnp.concatenate(outs + more, 0)
    row_id = lax.broadcasted_iota(jnp.int32, (BLK, BLK), 0)
    col_id = lax.broadcasted_iota(jnp.int32, (BLK, BLK), 1)
    on_diag = jnp.broadcast_to((diag + more_diag)[0:1], (BLK, BLK))
    upper = jnp.where(col_id > row_id, full, jnp.where(col_id == row_id, on_diag, 0.0))
    return upper.T, jnp.where(col_id <= row_id, full, 0.0)


def halves(value):
    high = value.astype(BF16)
    return high, (value - high.astype(F32)).astype(BF16)


def dot_nt(left, right):
    return lax.dot_general(
        left, right, (((1,), (1,)), ((), ())), preferred_element_type=F32
    )


def dot_split(left, right):
    left_high, left_low = halves(left)
    right_high, right_low = halves(right)
    return dot_nt(
        jnp.concatenate([left_high, left_high, left_low], 1),
        jnp.concatenate([right_high, right_low, right_high], 1),
    )


def factor_corner(work, chol, inverse):
    order = NB * BLK

    def one_panel(step, carry):
        first = pl.multiple_of(step * BLK, BLK)
        lower, lower_inverse = factor_block(work[step, pl.ds(first, BLK), :])
        chol[step, pl.ds(first, BLK), :] = lower
        inverse[step] = lower_inverse
        for j in range(NB - 1):

            @pl.when(step == j)
            def _():
                start = BLK * (j + 1)
                panel = dot_split(work[j, start:, :], inverse[j])
                chol[j, start:, :] = panel
                high, low = halves(panel)
                left = jnp.concatenate([high, high, low], 1)
                right = jnp.concatenate([high, low, high], 1)
                for k in range(j + 1, NB, 2):
                    wide = min(2, NB - k)
                    top = BLK * k - start
                    update = dot_nt(left[top:], right[top : top + wide * BLK])
                    for w in range(wide):
                        work[k + w, BLK * k :, :] = (
                            work[k + w, BLK * k :, :] - update[:, w * BLK : (w + 1) * BLK]
                        )

        return carry

    for j in range(1, NB):
        chol[j, : j * BLK, :] = jnp.zeros((j * BLK, BLK), F32)
    lax.fori_loop(0, NB, one_panel, 0)


def solve_rows(right_side, chol, inverse, solved, solved_high, solved_low):
    for p in range(0, NB, 2):
        first, second = right_side(p), right_side(p + 1)
        if p:
            depth = range(p)
            left_high = jnp.concatenate([solved_high[k] for k in depth], 1)
            left_low = jnp.concatenate([solved_low[k] for k in depth], 1)
            right = jnp.concatenate([chol[k, p * BLK : (p + 2) * BLK, :] for k in depth], 1)
            right_high, right_low = halves(right)
            update = (
                dot_nt(left_high, right_high)
                + dot_nt(left_high, right_low)
                + dot_nt(left_low, right_high)
            )
            first = first - update[:, :BLK]
            second = second - update[:, BLK:]
        first = dot_split(first, inverse[p])
        second = second - dot_split(first, chol[p, (p + 1) * BLK : (p + 2) * BLK, :])
        second = dot_split(second, inverse[p + 1])
        for k, value in ((p, first), (p + 1, second)):
            solved[k] = value
            solved_high[k], solved_low[k] = halves(value)


def kept(pattern, front, row, col):
    return (pattern[front, row, col] == 1) | (pattern[front, col, row] == 1) | (row == col)


def first_turn(core, z):
    return jnp.where((core == 0) & (z >= 4), 1, 0)


def send_blocks(tile, core, z, out):
    base = NB // 2 * core
    for turn in range(2):
        local = (z + first_turn(core, z) + turn) % 4
        block = tile[local]
        at = turn * BLK

        @pl.when(base + local >= z)
        def _():
            out[at : at + BLK, :] = block

        @pl.when(base + local < z)
        def _():
            out[at : at + BLK, :] = block.T

    block = tile[(z + 2) % 4]

    @pl.when(z % 4 < 2)
    def _():
        out[2 * BLK :, :] = block[:HALF, :]

    @pl.when(z % 4 >= 2)
    def _():
        out[2 * BLK :, :] = block.T[HALF:, :]


def static_blocks():
    where = {}
    for core in range(2):
        for z in range(NB):
            turn0 = 1 if core == 0 and z >= 4 else 0
            for turn in range(2):
                row = 4 * core + (z + turn0 + turn) % 4
                where[max(row, z), min(row, z)] = [(core * NB + z, turn * BLK, BLK)]
            if z // 4 == core:
                row = 4 * core + (z + 2) % 4
                key = (max(row, z), min(row, z))
                entry = (core * NB + z, 2 * BLK, HALF)
                known = where.setdefault(key, [])
                if z % 4 < 2:
                    known.insert(0, entry)
                else:
                    known.append(entry)
    return where


def send_child(child, z, out):
    for turn in range(4):
        row = (z + turn) % NB
        at = turn * BLK
        block = child[pl.ds(pl.multiple_of(row * BLK, BLK), BLK), :]

        @pl.when(row >= z)
        def _():
            out[at : at + BLK, :] = block

        @pl.when(row < z)
        def _():
            out[at : at + BLK, :] = block.T

    row = (z + 4) % NB
    block = child[pl.ds(pl.multiple_of(row * BLK, BLK), BLK), :]

    @pl.when(row > z)
    def _():
        out[4 * BLK :, :] = block[:HALF, :]

    @pl.when(row < z)
    def _():
        out[4 * BLK :, :] = block.T[HALF:, :]


def child_copies(gathered, children, sems):
    return [
        pltpu.make_async_copy(
            gathered.at[:, :CHILD_ROWS, :], children.at[:, :CHILD_ROWS, :], sems.at[0]
        )
    ] + [
        pltpu.make_async_copy(
            gathered.at[child * NB + 4 : child * NB + 8, 4 * BLK : CHILD_ROWS, :],
            children.at[child * NB : child * NB + 4, CHILD_ROWS:, :],
            sems.at[1 + child],
        )
        for child in range(2)
    ]


def each_gathered(block_map, front, children, visit):
    def one(n, carry):
        child, m = n // 36, n % 36
        z = jnp.where(m < 32, m // 4, m - 32)
        turn = jnp.where(m < 32, m % 4, 4)
        other = (z + turn) % NB
        row = block_map[front, child, jnp.maximum(z, other)]
        col = block_map[front, child, jnp.minimum(z, other)]
        start = pl.multiple_of(turn * BLK, BLK)
        visit(row, col, lambda: children[child * NB + z, pl.ds(start, BLK), :])
        return carry

    lax.fori_loop(0, 72, one, 0)


def each_packed(block_map, front, children, visit):
    def one_child(child, carry):
        def one_col(k, carry):
            def one_row(i, carry):
                row, col = block_map[front, child, i], block_map[front, child, k]
                index = packed_index(i, k)
                visit(row, col, lambda: children[child, index])
                return carry

            return lax.fori_loop(k, NB, one_row, carry)

        return lax.fori_loop(0, NB, one_col, carry)

    lax.fori_loop(0, 2, one_child, 0)


def add_at(ref, lead, block_row, block):
    place = pl.ds(pl.multiple_of(block_row * BLK, BLK), BLK)
    ref[lead, place, :] = ref[lead, place, :] + block


def separators_into(work):
    def visit(row, col, block):
        both = (row % 2 == 0) & (col % 2 == 0)

        @pl.when(both & (row >= col))
        def _():
            add_at(work, col // 2, row // 2, block())

        @pl.when(both & (row < col))
        def _():
            add_at(work, row // 2, col // 2, block().T)

    return visit


def masked_tile(initial, pattern, front, row, local, col):
    keep = kept(pattern, front, row, col)
    return jnp.where(keep, initial[local * BLK : (local + 1) * BLK, :], 0.0)


def pack_kernel(ids, pattern_one, child, initial, merged, columns, tile, sem):
    front_one, side, z = ids[0], ids[1], ids[2]
    copy = pltpu.make_async_copy(initial.at[:, :BLK], columns, sem)
    copy.start()
    send_child(child, z, merged.at[:CHILD_ROWS, :])
    copy.wait()
    for r in range(4):
        tile[r] = masked_tile(columns, pattern_one, front_one, NB * side + 2 * r, 2 * r, 2 * z)
    send_blocks(tile, side, z, merged.at[CHILD_ROWS:, :])


def mask_kernel(
    ids,
    pattern_one,
    pattern_two,
    initial_one,
    initial_two,
    merged,
    corner_two,
    lower_two,
    row_two,
    tail_two,
    tile,
):
    front_one, side, z, front_two, sub = ids[0], ids[1], ids[2], ids[3], ids[4]
    first, second = initial_one.at[:, :BLK], initial_one.at[:, BLK:]
    for r in range(4):
        row = NB * side + 2 * r + 1
        merged[r * BLK : (r + 1) * BLK, :] = masked_tile(
            first, pattern_one, front_one, row, 2 * r + 1, 2 * z
        )
        tile[r] = masked_tile(second, pattern_one, front_one, row, 2 * r + 1, 2 * z + 1)
    send_blocks(tile, side, z, merged.at[LOWER_ROWS:, :])
    for r in range(4):
        for w in range(2):
            columns = initial_two.at[:, w * BLK : (w + 1) * BLK]
            block = masked_tile(columns, pattern_two, front_two, 4 * sub + r, r, 2 * z + w)
            at = slice(r // 2 * BLK, (r // 2 + 1) * BLK)
            if w == 0:
                (corner_two if r % 2 == 0 else lower_two)[at, :] = block
            elif r % 2 == 0:
                row_two[at, :] = block.T
            else:
                tail_two[r // 2] = block


def chol_kernel(ids, block_map, gathered, chol, inverse, work, children, sems):
    front = ids[0]
    copies = child_copies(gathered, children, sems)
    for (row, col), parts in static_blocks().items():
        start = row * BLK
        for piece, at, rows in parts:
            copies.append(
                pltpu.make_async_copy(
                    gathered.at[piece, CHILD_ROWS + at : CHILD_ROWS + at + rows, :],
                    work.at[col, start : start + rows, :],
                    sems.at[len(copies)],
                )
            )
            start += rows
    for copy in copies:
        copy.start()
    for copy in copies:
        copy.wait()
    each_gathered(block_map, front, children, separators_into(work))
    factor_corner(work, chol, inverse)


def rest_kernel(
    ids,
    block_map,
    chol,
    inverse,
    gathered,
    merged,
    factor,
    mine,
    other,
    children,
    lower,
    solved,
    solved_high,
    solved_low,
    trail,
    sems,
):
    front, side, z = ids[0], ids[1], ids[2]
    half = NB // 2 * BLK
    copies = child_copies(gathered, children, sems)
    for core in range(2):
        copies.append(
            pltpu.make_async_copy(
                merged.at[core * NB : (core + 1) * NB, :LOWER_ROWS, :],
                lower.at[:, core * half : (core + 1) * half, :],
                sems.at[3 + core],
            )
        )
    for (row, col), parts in static_blocks().items():
        start = 0
        for piece, at, rows in parts:
            copies.append(
                pltpu.make_async_copy(
                    merged.at[piece, LOWER_ROWS + at : LOWER_ROWS + at + rows, :],
                    trail.at[packed_index(row, col), start : start + rows, :],
                    sems.at[len(copies)],
                )
            )
            start += rows
    for copy in copies:
        copy.start()
    for copy in copies:
        copy.wait()

    def visit(row, col, block):
        row_odd, col_odd = row % 2 == 1, col % 2 == 1
        row_half, col_half = row // 2, col // 2

        @pl.when(row_odd & ~col_odd)
        def _():
            add_at(lower, col_half, row_half, block())

        @pl.when(~row_odd & col_odd)
        def _():
            add_at(lower, row_half, col_half, block().T)

        @pl.when(row_odd & col_odd & (row >= col))
        def _():
            add_at(trail, packed_index(row_half, col_half), 0, block())

        @pl.when(row_odd & col_odd & (row < col))
        def _():
            add_at(trail, packed_index(col_half, row_half), 0, block().T)

    each_gathered(block_map, front, children, visit)
    solve_rows(lambda k: lower[k], chol, inverse, solved, solved_high, solved_low)
    for p in range(0, NB, 2):
        high = jnp.concatenate([solved_high[k, p * BLK :, :] for k in range(NB)], 1)
        low = jnp.concatenate([solved_low[k, p * BLK :, :] for k in range(NB)], 1)
        wide_high, wide_low = high[: 2 * BLK], low[: 2 * BLK]
        update = dot_nt(high, wide_high) + dot_nt(high, wide_low) + dot_nt(low, wide_high)
        for w in range(2):
            for i in range(p + w, NB):
                index = packed_index(i, p + w)
                trail[index] = (
                    trail[index]
                    - update[(i - p) * BLK : (i - p + 1) * BLK, w * BLK : (w + 1) * BLK]
                )
    outs = [
        pltpu.make_async_copy(trail.at[pl.ds(18 * side, 18)], mine, sems.at[0]),
        pltpu.make_async_copy(trail.at[pl.ds(18 * (1 - side), 18)], other, sems.at[1]),
    ]
    for copy in outs:
        copy.start()
    for r in range(NB):
        source = solved if r % 2 else chol
        start = pl.multiple_of((side * (NB // 2) + r // 2) * BLK, BLK)
        factor[r * BLK : (r + 1) * BLK, :] = source[z, pl.ds(start, BLK), :]
    for copy in outs:
        copy.wait()


def fetch_children(side, mine, refs, children, sems):
    near_mine, near_other, far_mine, far_other = refs
    copies = []
    for n, (ref, child, half) in enumerate(
        (
            (near_mine, mine, side),
            (near_other, mine, 1 - side),
            (far_mine, 1 - mine, side),
            (far_other, 1 - mine, 1 - side),
        )
    ):
        copies.append(pltpu.make_async_copy(ref, children.at[child, pl.ds(18 * half, 18)], sems.at[n]))
        copies[-1].start()
    return copies


def chol_two_kernel(
    ids,
    block_map,
    gathered,
    near_mine,
    near_other,
    far_mine,
    far_other,
    chol,
    inverse,
    work,
    children,
    sems,
):
    side, front, sub = ids[1], ids[3], ids[4]
    copies = fetch_children(
        side, sub // 2, (near_mine, near_other, far_mine, far_other), children, sems
    )
    for core in range(2):
        for n, y in ((0, sub // 2), (1, 1 - sub // 2)):
            start = pl.multiple_of(2 * (2 * y + core) * BLK, BLK)
            copies.append(
                pltpu.make_async_copy(
                    gathered.at[core * NB : (core + 1) * NB, 2 * n * BLK : 2 * (n + 1) * BLK, :],
                    work.at[:, pl.ds(start, 2 * BLK), :],
                    sems.at[4 + 2 * core + n],
                )
            )
            copies[-1].start()
    for copy in copies:
        copy.wait()
    each_packed(block_map, front, children, separators_into(work))
    factor_corner(work, chol, inverse)


def tail_kernel(
    ids,
    map_two,
    chol,
    inverse,
    lower_near,
    rows_all,
    tail,
    near_mine,
    near_other,
    far_mine,
    far_other,
    factor,
    schur,
    children,
    lower,
    solved,
    solved_high,
    solved_low,
    trail,
    sems,
):
    side, z, front, sub = ids[1], ids[2], ids[3], ids[4]
    mine = sub // 2
    copies = fetch_children(
        side, mine, (near_mine, near_other, far_mine, far_other), children, sems
    )
    lower[:, : 2 * BLK, :] = lower_near[...]
    for s in range(4):
        for b in range(2):
            lower[2 * s + b, 2 * BLK :, :] = rows_all[s, b * BLK : (b + 1) * BLK, :]
    trail[...] = tail[...]
    for copy in copies:
        copy.wait()
    wanted = (2 * sub, 2 * sub + 1, z)

    def visit(row, col, block):
        row_half, col_half = row // 2, col // 2
        row_odd, col_odd = row % 2 == 1, col % 2 == 1
        for slot, target in enumerate(wanted):

            @pl.when(row_odd & ~col_odd & (row_half == target))
            def _():
                add_at(lower, col_half, slot, block())

            @pl.when(~row_odd & col_odd & (col_half == target))
            def _():
                add_at(lower, row_half, slot, block().T)

        for slot in range(2):

            @pl.when(row_odd & col_odd & (row_half == wanted[slot]) & (col_half == z))
            def _():
                trail[slot] = trail[slot] + block()

            @pl.when(
                row_odd & col_odd & (row != col) & (col_half == wanted[slot]) & (row_half == z)
            )
            def _():
                trail[slot] = trail[slot] + block().T

    each_packed(map_two, front, children, visit)
    solve_rows(lambda k: lower[k], chol, inverse, solved, solved_high, solved_low)
    high = jnp.concatenate([solved_high[k] for k in range(NB)], 1)
    low = jnp.concatenate([solved_low[k] for k in range(NB)], 1)
    left_high, left_low = high[: 2 * BLK], low[: 2 * BLK]
    right_high, right_low = high[2 * BLK :], low[2 * BLK :]
    update = (
        dot_nt(left_high, right_high)
        + dot_nt(left_high, right_low)
        + dot_nt(left_low, right_high)
    )
    for r in range(2):
        schur[r * BLK : (r + 1) * BLK, :] = trail[r] - update[r * BLK : (r + 1) * BLK, :]
        start = pl.multiple_of((2 * sub + r) * BLK, BLK)
        factor[2 * r * BLK : (2 * r + 1) * BLK, :] = chol[z, pl.ds(start, BLK), :]
        factor[(2 * r + 1) * BLK : (2 * r + 2) * BLK, :] = solved[z, r * BLK : (r + 1) * BLK, :]


def call(kernel, name, outs, specs, args, scratch=(), flops=0, out_specs=None):
    return pl.pallas_call(
        kernel,
        name=name,
        out_shape=outs,
        in_specs=specs,
        out_specs=out_specs or [VMEM] * len(outs),
        scratch_shapes=list(scratch),
        compiler_params=PARAMS,
        cost_estimate=pl.CostEstimate(flops=flops, bytes_accessed=flops // 400, transcendentals=0)
        if flops
        else None,
    )(*args)


def swap(value, axis):
    return lax.ppermute(value, axis, [(0, 1), (1, 0)])


def per_device(
    child_updates,
    initial_one,
    initial_two,
    pattern_one,
    pattern_two,
    parent_map_one,
    parent_map_two,
):
    x, yh, yl = lax.axis_index("x"), lax.axis_index("yh"), lax.axis_index("yl")
    core, z = lax.axis_index("core"), lax.axis_index("front")
    ids = jnp.stack([x * 4 + yh * 2 + yl, core, z, x * 2 + yh, yl * 2 + core]).astype(jnp.int32)
    panel = (NB, NB * BLK, BLK)
    block = (BLK, BLK)

    (sent,) = call(
        pack_kernel,
        "pack",
        [shape(CHILD_ROWS + CORNER_ROWS, BLK)],
        [SMEM, SMEM, VMEM, ANY],
        (ids, pattern_one, child_updates, initial_one),
        [pltpu.VMEM((NB * BLK, BLK), F32), pltpu.VMEM((4, *block), F32), pltpu.SemaphoreType.DMA],
    )
    gathered = lax.all_gather(sent, ("core", "front"), axis=0, tiled=False)
    ids_mask, _ = lax.optimization_barrier((ids, sent))
    merged, corner_two, lower_two, row_two, tail_two = call(
        mask_kernel,
        "mask",
        [
            shape(LOWER_ROWS + CORNER_ROWS, BLK),
            shape(2 * BLK, BLK),
            shape(2 * BLK, BLK),
            shape(2 * BLK, BLK),
            shape(2, *block),
        ],
        [SMEM, SMEM, SMEM, VMEM, VMEM],
        (ids_mask, pattern_one, pattern_two, initial_one, initial_two),
        [pltpu.VMEM((4, *block), F32)],
    )
    corner_two = jnp.concatenate([corner_two, swap(corner_two, "yl")], 0)
    rows_all = lax.all_gather(row_two, ("yl", "core"), axis=0, tiled=False)
    merged, gathered, corner_two, rows_all = lax.optimization_barrier(
        (merged, gathered, corner_two, rows_all)
    )
    merged_all = lax.all_gather(merged, ("core", "front"), axis=0, tiled=False)
    children_one = pltpu.VMEM((2 * NB, 5 * BLK, BLK), F32)
    chol, inverse = call(
        chol_kernel,
        "chol",
        [shape(*panel), shape(NB, *block)],
        [SMEM, SMEM, ANY],
        (ids, parent_map_one, gathered),
        [pltpu.VMEM(panel, F32), children_one, pltpu.SemaphoreType.DMA((64,))],
        flops=40_000_000_000,
    )
    lower_two, _ = lax.optimization_barrier((lower_two, gathered))
    gathered_two = lax.all_gather(corner_two, ("core", "front"), axis=0, tiled=False)
    lower_near = lax.all_gather(lower_two, "front", axis=0, tiled=False)
    factor_one, near_mine, near_other = call(
        rest_kernel,
        "rest",
        [shape(NB * BLK, BLK), shape(18, *block), shape(18, *block)],
        [SMEM, SMEM, VMEM, VMEM, ANY, ANY],
        (ids, parent_map_one, chol, inverse, gathered, merged_all),
        [children_one]
        + [pltpu.VMEM(panel, F32)] * 2
        + [pltpu.VMEM(panel, BF16)] * 2
        + [pltpu.VMEM((36, *block), F32), pltpu.SemaphoreType.DMA((64,))],
        flops=15_000_000_000,
        out_specs=[VMEM, ANY, ANY],
    )
    far_mine = swap(near_mine, "yl")
    far_other = swap(far_mine, "core")
    packed = (near_mine, near_other, far_mine, far_other)
    children = pltpu.VMEM((2, 36, *block), F32)
    chol, inverse = call(
        chol_two_kernel,
        "chol_two",
        [shape(*panel), shape(NB, *block)],
        [SMEM, SMEM] + [ANY] * 5,
        (ids, parent_map_two, gathered_two, *packed),
        [pltpu.VMEM(panel, F32), children, pltpu.SemaphoreType.DMA((8,))],
        flops=40_000_000_000,
    )
    rows = (NB, 3 * BLK, BLK)
    factor_two, schur_two = call(
        tail_kernel,
        "tail",
        [shape(4 * BLK, BLK), shape(2 * BLK, BLK)],
        [SMEM, SMEM] + [VMEM] * 5 + [ANY] * 4,
        (ids, parent_map_two, chol, inverse, lower_near, rows_all, tail_two, *packed),
        [
            children,
            pltpu.VMEM(rows, F32),
            pltpu.VMEM(rows, F32),
            pltpu.VMEM(rows, BF16),
            pltpu.VMEM(rows, BF16),
            pltpu.VMEM((2, *block), F32),
            pltpu.SemaphoreType.DMA((4,)),
        ],
    )
    return factor_one, factor_two, schur_two


def solution(mesh):
    cut = Mesh(mesh.devices.reshape(4, 2, 2, 2, 8), LEAF + ("front",))
    tile = P(LEAF, "front")
    return jax.shard_map(
        per_device,
        mesh=cut,
        in_specs=(tile, tile, tile, P(), P(), P(), P()),
        out_specs=(tile, tile, tile),
        check_vma=False,
    )
```

```python
import jax
import jax.numpy as jnp
from jax import lax
from jax.experimental import pallas as pl
from jax.experimental.pallas import tpu as pltpu
from jax.sharding import Mesh, PartitionSpec as P

BLK = 128
NB = 8
FB = 16
F32 = jnp.float32
BF16 = jnp.bfloat16
VMEM = pl.BlockSpec(memory_space=pltpu.VMEM)
SMEM = pl.BlockSpec(memory_space=pltpu.SMEM)
ANY = pl.BlockSpec(memory_space=pl.ANY)
HALF = BLK // 2
CORNER_ROWS = 2 * BLK + HALF
CHILD_ROWS = 4 * BLK + HALF
LOWER_ROWS = 4 * BLK
PARAMS = pltpu.CompilerParams(vmem_limit_bytes=58 * 1024 * 1024)
LEAF = ("x", "yh", "yl", "core")


def shape(*dims):
    return jax.ShapeDtypeStruct(dims, F32)


def packed_index(row, col):
    return col * NB - col * (col - 1) // 2 + row - col


def across(piece):
    return jnp.broadcast_to(piece, (8, BLK))


def lane_columns(rows, t):
    return [across(rows[:, 8 * t + b : 8 * t + b + 1]) for b in range(8)]


def factor_eights(rows, first, last):
    sub = lax.broadcasted_iota(jnp.int32, (8, BLK), 0)
    lane = lax.broadcasted_iota(jnp.int32, (8, BLK), 1)
    diag = jnp.zeros((8, BLK), F32)
    outs = []
    following = lane_columns(rows[first], first)
    for t in range(first, last):
        head = following
        below = {g: lane_columns(rows[g], t) for g in range(t + 1, last)}
        if t + 1 < last:
            following = lane_columns(rows[t + 1], t + 1)
        scale, weight = [], {}
        for b in range(8):
            pivot = across(head[b][b : b + 1])
            scale.append(lax.rsqrt(pivot))
            diag = jnp.where(lane == 8 * t + b, pivot * scale[b], diag)
            low = head[b] * scale[b]
            for a in range(b + 1, 8):
                weight[a, b] = across(low[a : a + 1])
                head[a] = head[a] - low * weight[a, b]
        inside = (lane >= 8 * t) & (lane < 8 * t + 8)
        pivots = []
        for b in range(8):
            unit = jnp.where(lane == 8 * t + b, 1.0, 0.0)
            row = jnp.where(inside, unit, across(rows[t][b : b + 1]))
            for a in range(b):
                row = row - weight[b, a] * pivots[a]
            pivots.append(row * scale[b])
        for g in range(t + 1, last):
            lows = []
            for b in range(8):
                column = below[g][b]
                for a in range(b):
                    column = column - lows[a] * weight[b, a]
                lows.append(column * scale[b])
            if g == t + 1:
                for b in range(8):
                    for a in range(8):
                        following[a] = following[a] - lows[b] * across(lows[b][a : a + 1])
            group = jnp.where(inside, 0.0, rows[g])
            for b in range(8):
                group = group - lows[b] * pivots[b]
            rows[g] = group
        group = pivots[7]
        for b in range(6, -1, -1):
            group = jnp.where(sub == b, pivots[b], group)
        rows[t] = group
        for a in range(1, 8):
            column = weight[a, a - 1]
            for b in range(a - 2, -1, -1):
                column = jnp.where(sub == b, weight[a, b], column)
            group = jnp.where((lane == 8 * t + a) & (sub < a), column, group)
        outs.append(group)
    return outs, diag


def factor_block(block):
    rows = [block[8 * g : 8 * g + 8] for g in range(16)]
    outs, diag = factor_eights(rows, 0, 8)
    lane = lax.broadcasted_iota(jnp.int32, (8, BLK), 1)
    row_id = lax.broadcasted_iota(jnp.int32, (BLK // 2, BLK), 0)
    col_id = lax.broadcasted_iota(jnp.int32, (BLK // 2, BLK), 1)
    left = jnp.concatenate(rows[:8], 0)
    right = jnp.where((col_id > row_id) & (col_id < BLK // 2), 0.0, left)
    left_high, left_low = halves(left)
    right_high, right_low = halves(right)
    update = lax.dot_general(
        jnp.concatenate([left_high, left_high, left_low], 0),
        jnp.concatenate([right_high, right_low, right_high], 0),
        (((0,), (0,)), ((), ())),
        preferred_element_type=F32,
    )
    for g in range(8, 16):
        rows[g] = jnp.where(lane < BLK // 2, 0.0, rows[g]) - update[8 * g : 8 * g + 8]
    more, more_diag = factor_eights(rows, 8, 16)
    full = jnp.concatenate(outs + more, 0)
    row_id = lax.broadcasted_iota(jnp.int32, (BLK, BLK), 0)
    col_id = lax.broadcasted_iota(jnp.int32, (BLK, BLK), 1)
    on_diag = jnp.broadcast_to((diag + more_diag)[0:1], (BLK, BLK))
    upper = jnp.where(col_id > row_id, full, jnp.where(col_id == row_id, on_diag, 0.0))
    return upper.T, jnp.where(col_id <= row_id, full, 0.0)


def halves(value):
    high = value.astype(BF16)
    return high, (value - high.astype(F32)).astype(BF16)


def dot_nt(left, right):
    return lax.dot_general(
        left, right, (((1,), (1,)), ((), ())), preferred_element_type=F32
    )


def dot_split(left, right):
    left_high, left_low = halves(left)
    right_high, right_low = halves(right)
    return dot_nt(
        jnp.concatenate([left_high, left_high, left_low], 1),
        jnp.concatenate([right_high, right_low, right_high], 1),
    )


def factor_corner(work, chol, inverse):
    order = NB * BLK

    def one_panel(step, carry):
        first = pl.multiple_of(step * BLK, BLK)
        lower, lower_inverse = factor_block(work[step, pl.ds(first, BLK), :])
        chol[step, pl.ds(first, BLK), :] = lower
        inverse[step] = lower_inverse
        for j in range(NB - 1):

            @pl.when(step == j)
            def _():
                start = BLK * (j + 1)
                panel = dot_split(work[j, start:, :], inverse[j])
                chol[j, start:, :] = panel
                high, low = halves(panel)
                left = jnp.concatenate([high, high, low], 1)
                right = jnp.concatenate([high, low, high], 1)
                for k in range(j + 1, NB, 2):
                    wide = min(2, NB - k)
                    top = BLK * k - start
                    update = dot_nt(left[top:], right[top : top + wide * BLK])
                    for w in range(wide):
                        work[k + w, BLK * k :, :] = (
                            work[k + w, BLK * k :, :] - update[:, w * BLK : (w + 1) * BLK]
                        )

        return carry

    for j in range(1, NB):
        chol[j, : j * BLK, :] = jnp.zeros((j * BLK, BLK), F32)
    lax.fori_loop(0, NB, one_panel, 0)


def solve_rows(right_side, chol, inverse, solved, solved_high, solved_low):
    for p in range(0, NB, 2):
        value = right_side(p)
        if p:
            depth = range(p)
            left_high = jnp.concatenate([solved_high[k] for k in depth], 1)
            left_low = jnp.concatenate([solved_low[k] for k in depth], 1)
            right = jnp.concatenate([chol[k, p * BLK : (p + 2) * BLK, :] for k in depth], 1)
            right_high, right_low = halves(right)
            value = value - (
                dot_nt(left_high, right_high)
                + dot_nt(left_high, right_low)
                + dot_nt(left_low, right_high)
            )
        between = chol[p, (p + 1) * BLK : (p + 2) * BLK, :]
        corner = -dot_split(inverse[p + 1], dot_split(inverse[p].T, between))
        pair_inverse = jnp.concatenate(
            [
                jnp.concatenate([inverse[p], jnp.zeros((BLK, BLK), F32)], 1),
                jnp.concatenate([corner, inverse[p + 1]], 1),
            ],
            0,
        )
        value = dot_split(value, pair_inverse)
        high, low = halves(value)
        for w in range(2):
            lanes = slice(w * BLK, (w + 1) * BLK)
            solved[p + w] = value[:, lanes]
            solved_high[p + w], solved_low[p + w] = high[:, lanes], low[:, lanes]


def pair(ref, p):
    return jnp.concatenate([ref[p], ref[p + 1]], 1)


def place_of(block_map, front, child, slots):
    for m in range(FB):
        slots[child, m] = -1
    for i in range(NB):
        slots[child, block_map[front, child, i]] = i


def kept(pattern, front, row, col):
    return (pattern[front, row, col] == 1) | (pattern[front, col, row] == 1) | (row == col)


def first_turn(core, z):
    return jnp.where((core == 0) & (z >= 4), 1, 0)


def send_blocks(tile, core, z, out):
    base = NB // 2 * core
    for turn in range(2):
        local = (z + first_turn(core, z) + turn) % 4
        block = tile[local]
        at = turn * BLK

        @pl.when(base + local >= z)
        def _():
            out[at : at + BLK, :] = block

        @pl.when(base + local < z)
        def _():
            out[at : at + BLK, :] = block.T

    block = tile[(z + 2) % 4]

    @pl.when(z % 4 < 2)
    def _():
        out[2 * BLK :, :] = block[:HALF, :]

    @pl.when(z % 4 >= 2)
    def _():
        out[2 * BLK :, :] = block.T[HALF:, :]


def static_blocks():
    where = {}
    for core in range(2):
        for z in range(NB):
            turn0 = 1 if core == 0 and z >= 4 else 0
            for turn in range(2):
                row = 4 * core + (z + turn0 + turn) % 4
                where[max(row, z), min(row, z)] = [(core * NB + z, turn * BLK, BLK)]
            if z // 4 == core:
                row = 4 * core + (z + 2) % 4
                key = (max(row, z), min(row, z))
                entry = (core * NB + z, 2 * BLK, HALF)
                known = where.setdefault(key, [])
                if z % 4 < 2:
                    known.insert(0, entry)
                else:
                    known.append(entry)
    return where


def send_child(child, z, out):
    for turn in range(4):
        row = (z + turn) % NB
        at = turn * BLK
        block = child[pl.ds(pl.multiple_of(row * BLK, BLK), BLK), :]

        @pl.when(row >= z)
        def _():
            out[at : at + BLK, :] = block

        @pl.when(row < z)
        def _():
            out[at : at + BLK, :] = block.T

    row = (z + 4) % NB
    block = child[pl.ds(pl.multiple_of(row * BLK, BLK), BLK), :]

    @pl.when(row > z)
    def _():
        out[4 * BLK :, :] = block[:HALF, :]

    @pl.when(row < z)
    def _():
        out[4 * BLK :, :] = block.T[HALF:, :]


def child_copies(gathered, children, sems):
    return [
        pltpu.make_async_copy(
            gathered.at[:, :CHILD_ROWS, :], children.at[:, :CHILD_ROWS, :], sems.at[0]
        )
    ] + [
        pltpu.make_async_copy(
            gathered.at[child * NB + 4 : child * NB + 8, 4 * BLK : CHILD_ROWS, :],
            children.at[child * NB : child * NB + 4, CHILD_ROWS:, :],
            sems.at[1 + child],
        )
        for child in range(2)
    ]


def each_gathered(block_map, front, children, visit):
    def one(n, carry):
        child, m = n // 36, n % 36
        z = jnp.where(m < 32, m // 4, m - 32)
        turn = jnp.where(m < 32, m % 4, 4)
        other = (z + turn) % NB
        row = block_map[front, child, jnp.maximum(z, other)]
        col = block_map[front, child, jnp.minimum(z, other)]
        start = pl.multiple_of(turn * BLK, BLK)
        visit(row, col, lambda: children[child * NB + z, pl.ds(start, BLK), :])
        return carry

    lax.fori_loop(0, 72, one, 0)


def add_packed_separators(block_map, front, children, work, evens):
    def one_child(child, carry):
        count = jnp.int32(0)
        for i in range(NB):
            evens[count] = i
            count = count + 1 - block_map[front, child, i] % 2

        def one_col(b, carry):
            k = evens[b]
            col = block_map[front, child, k] // 2

            def one_row(a, carry):
                i = evens[a]
                row = block_map[front, child, i] // 2
                index = packed_index(i, k)

                @pl.when(row >= col)
                def _():
                    add_at(work, col, row, children[child, index])

                @pl.when(row < col)
                def _():
                    add_at(work, row, col, children[child, index].T)

                return carry

            return lax.fori_loop(b, count, one_row, carry)

        return lax.fori_loop(0, count, one_col, carry)

    lax.fori_loop(0, 2, one_child, 0)


def add_at(ref, lead, block_row, block):
    place = pl.ds(pl.multiple_of(block_row * BLK, BLK), BLK)
    ref[lead, place, :] = ref[lead, place, :] + block


def contributions_into(corner, lower, trail):
    def visit(row, col, block):
        row_odd, col_odd = row % 2 == 1, col % 2 == 1
        row_half, col_half = row // 2, col // 2

        @pl.when(~row_odd & ~col_odd & (row >= col))
        def _():
            add_at(corner, col_half, row_half, block())

        @pl.when(~row_odd & ~col_odd & (row < col))
        def _():
            add_at(corner, row_half, col_half, block().T)

        @pl.when(row_odd & ~col_odd)
        def _():
            add_at(lower, col_half, row_half, block())

        @pl.when(~row_odd & col_odd)
        def _():
            add_at(lower, row_half, col_half, block().T)

        @pl.when(row_odd & col_odd & (row >= col))
        def _():
            add_at(trail, packed_index(row_half, col_half), 0, block())

        @pl.when(row_odd & col_odd & (row < col))
        def _():
            add_at(trail, packed_index(col_half, row_half), 0, block().T)

    return visit


def masked_tile(initial, pattern, front, row, local, col):
    keep = kept(pattern, front, row, col)
    return jnp.where(keep, initial[local * BLK : (local + 1) * BLK, :], 0.0)


def pack_kernel(ids, pattern_one, child, initial, merged, columns, tile, sem):
    front_one, side, z = ids[0], ids[1], ids[2]
    copy = pltpu.make_async_copy(initial.at[:, :BLK], columns, sem)
    copy.start()
    send_child(child, z, merged.at[:CHILD_ROWS, :])
    copy.wait()
    for r in range(4):
        tile[r] = masked_tile(columns, pattern_one, front_one, NB * side + 2 * r, 2 * r, 2 * z)
    send_blocks(tile, side, z, merged.at[CHILD_ROWS:, :])


def mask_kernel(
    ids,
    pattern_one,
    pattern_two,
    initial_one,
    initial_two,
    merged,
    corner_two,
    lower_two,
    row_two,
    tail_two,
    tile,
):
    front_one, side, z, front_two, sub = ids[0], ids[1], ids[2], ids[3], ids[4]
    first, second = initial_one.at[:, :BLK], initial_one.at[:, BLK:]
    for r in range(4):
        row = NB * side + 2 * r + 1
        merged[r * BLK : (r + 1) * BLK, :] = masked_tile(
            first, pattern_one, front_one, row, 2 * r + 1, 2 * z
        )
        tile[r] = masked_tile(second, pattern_one, front_one, row, 2 * r + 1, 2 * z + 1)
    send_blocks(tile, side, z, merged.at[LOWER_ROWS:, :])
    for r in range(4):
        for w in range(2):
            columns = initial_two.at[:, w * BLK : (w + 1) * BLK]
            block = masked_tile(columns, pattern_two, front_two, 4 * sub + r, r, 2 * z + w)
            at = slice(r // 2 * BLK, (r // 2 + 1) * BLK)
            if w == 0:
                (corner_two if r % 2 == 0 else lower_two)[at, :] = block
            elif r % 2 == 0:
                row_two[at, :] = block.T
            else:
                tail_two[r // 2] = block


def chol_kernel(
    ids,
    block_map,
    gathered,
    chol,
    inverse,
    lower_out,
    trail_out,
    work,
    children,
    lower,
    trail,
    sems,
):
    front = ids[0]
    copies = child_copies(gathered, children, sems)
    for (row, col), parts in static_blocks().items():
        start = row * BLK
        for piece, at, rows in parts:
            copies.append(
                pltpu.make_async_copy(
                    gathered.at[piece, CHILD_ROWS + at : CHILD_ROWS + at + rows, :],
                    work.at[col, start : start + rows, :],
                    sems.at[len(copies)],
                )
            )
            start += rows
    for copy in copies:
        copy.start()
    lower[...] = jnp.zeros_like(lower)
    trail[...] = jnp.zeros_like(trail)
    for copy in copies:
        copy.wait()
    each_gathered(block_map, front, children, contributions_into(work, lower, trail))
    outs = [
        pltpu.make_async_copy(lower, lower_out, sems.at[0]),
        pltpu.make_async_copy(trail, trail_out, sems.at[1]),
    ]
    for copy in outs:
        copy.start()
    factor_corner(work, chol, inverse)
    for copy in outs:
        copy.wait()


def rest_kernel(
    ids,
    chol_in,
    inverse_in,
    lower_in,
    trail_in,
    merged,
    factor,
    mine,
    other,
    chol,
    inverse,
    lower,
    lower_add,
    solved,
    solved_high,
    solved_low,
    trail,
    trail_add,
    sems,
):
    side, z = ids[1], ids[2]
    half = NB // 2 * BLK
    used = []

    def fetch(source, target):
        copy = pltpu.make_async_copy(source, target, sems.at[len(used)])
        copy.start()
        used.append(copy)
        return copy

    first = [fetch(inverse_in, inverse)]
    columns = {}
    for p in range(0, NB, 2):
        columns[p] = [fetch(lower_in.at[p : p + 2], lower_add.at[p : p + 2])]
        for core in range(2):
            columns[p].append(
                fetch(
                    merged.at[core * NB + p : core * NB + p + 2, :LOWER_ROWS, :],
                    lower.at[p : p + 2, core * half : (core + 1) * half, :],
                )
            )
        if p == 0:
            first.append(fetch(chol_in, chol))
    last = [fetch(trail_in, trail_add)]
    for (row, col), parts in static_blocks().items():
        start = 0
        for piece, at, rows in parts:
            last.append(
                fetch(
                    merged.at[piece, LOWER_ROWS + at : LOWER_ROWS + at + rows, :],
                    trail.at[packed_index(row, col), start : start + rows, :],
                )
            )
            start += rows
    for copy in first:
        copy.wait()

    def right_side(p):
        for copy in columns[p]:
            copy.wait()
        return pair(lower, p) + pair(lower_add, p)

    solve_rows(right_side, chol, inverse, solved, solved_high, solved_low)
    for copy in last:
        copy.wait()
    for p in range(0, NB, 2):
        high = jnp.concatenate([solved_high[k, p * BLK :, :] for k in range(NB)], 1)
        low = jnp.concatenate([solved_low[k, p * BLK :, :] for k in range(NB)], 1)
        wide_high, wide_low = high[: 2 * BLK], low[: 2 * BLK]
        update = dot_nt(high, wide_high) + dot_nt(high, wide_low) + dot_nt(low, wide_high)
        for w in range(2):
            for i in range(p + w, NB):
                index = packed_index(i, p + w)
                trail[index] = (
                    trail[index]
                    + trail_add[index]
                    - update[(i - p) * BLK : (i - p + 1) * BLK, w * BLK : (w + 1) * BLK]
                )
    outs = [
        pltpu.make_async_copy(trail.at[pl.ds(18 * side, 18)], mine, sems.at[0]),
        pltpu.make_async_copy(trail.at[pl.ds(18 * (1 - side), 18)], other, sems.at[1]),
    ]
    for copy in outs:
        copy.start()
    for r in range(NB):
        source = solved if r % 2 else chol
        start = pl.multiple_of((side * (NB // 2) + r // 2) * BLK, BLK)
        factor[r * BLK : (r + 1) * BLK, :] = source[z, pl.ds(start, BLK), :]
    for copy in outs:
        copy.wait()


def fetch_children(side, mine, refs, children, sems):
    near_mine, near_other, far_mine, far_other = refs
    copies = []
    for n, (ref, child, half) in enumerate(
        (
            (near_mine, mine, side),
            (near_other, mine, 1 - side),
            (far_mine, 1 - mine, side),
            (far_other, 1 - mine, 1 - side),
        )
    ):
        copies.append(pltpu.make_async_copy(ref, children.at[child, pl.ds(18 * half, 18)], sems.at[n]))
        copies[-1].start()
    return copies


def chol_two_kernel(
    ids,
    block_map,
    gathered,
    near_mine,
    near_other,
    far_mine,
    far_other,
    chol,
    inverse,
    work,
    children,
    evens,
    sems,
):
    side, front, sub = ids[1], ids[3], ids[4]
    copies = fetch_children(
        side, sub // 2, (near_mine, near_other, far_mine, far_other), children, sems
    )
    for core in range(2):
        for n, y in ((0, sub // 2), (1, 1 - sub // 2)):
            start = pl.multiple_of(2 * (2 * y + core) * BLK, BLK)
            copies.append(
                pltpu.make_async_copy(
                    gathered.at[core * NB : (core + 1) * NB, 2 * n * BLK : 2 * (n + 1) * BLK, :],
                    work.at[:, pl.ds(start, 2 * BLK), :],
                    sems.at[4 + 2 * core + n],
                )
            )
            copies[-1].start()
    for copy in copies:
        copy.wait()
    add_packed_separators(block_map, front, children, work, evens)
    factor_corner(work, chol, inverse)


def tail_kernel(
    ids,
    map_two,
    chol_in,
    inverse,
    lower_near,
    rows_all,
    tail,
    near_mine,
    near_other,
    far_mine,
    far_other,
    factor,
    schur,
    chol,
    children,
    lower,
    solved,
    solved_high,
    solved_low,
    trail,
    slots,
    sems,
):
    side, z, front, sub = ids[1], ids[2], ids[3], ids[4]
    mine = sub // 2
    copies = fetch_children(
        side, mine, (near_mine, near_other, far_mine, far_other), children, sems
    )
    chol_copy = pltpu.make_async_copy(chol_in, chol, sems.at[4])
    chol_copy.start()
    place_of(map_two, front, 0, slots)
    place_of(map_two, front, 1, slots)
    lower[:, : 2 * BLK, :] = lower_near[...]
    for s in range(4):
        for b in range(2):
            lower[2 * s + b, 2 * BLK :, :] = rows_all[s, b * BLK : (b + 1) * BLK, :]
    trail[...] = tail[...]
    for copy in copies:
        copy.wait()
    wanted = (2 * sub, 2 * sub + 1, z)

    def one_child(child, carry):
        for slot, target in enumerate(wanted):
            i = slots[child, 2 * target + 1]

            def one_block(k, carry):
                col = map_two[front, child, k]
                index = packed_index(jnp.maximum(i, k), jnp.minimum(i, k))

                @pl.when((col % 2 == 0) & (i > k))
                def _():
                    add_at(lower, col // 2, slot, children[child, index])

                @pl.when((col % 2 == 0) & (i < k))
                def _():
                    add_at(lower, col // 2, slot, children[child, index].T)

                return carry

            lax.fori_loop(0, jnp.where(i >= 0, NB, 0), one_block, 0)
        k = slots[child, 2 * z + 1]
        for slot in range(2):
            i = slots[child, 2 * wanted[slot] + 1]
            both = (i >= 0) & (k >= 0)
            index = jnp.where(both, packed_index(jnp.maximum(i, k), jnp.minimum(i, k)), 0)

            @pl.when(both & (i >= k))
            def _():
                trail[slot] = trail[slot] + children[child, index]

            @pl.when(both & (i < k))
            def _():
                trail[slot] = trail[slot] + children[child, index].T

        return carry

    lax.fori_loop(0, 2, one_child, 0)
    chol_copy.wait()
    solve_rows(lambda p: pair(lower, p), chol, inverse, solved, solved_high, solved_low)
    high = jnp.concatenate([solved_high[k] for k in range(NB)], 1)
    low = jnp.concatenate([solved_low[k] for k in range(NB)], 1)
    left_high, left_low = high[: 2 * BLK], low[: 2 * BLK]
    right_high, right_low = high[2 * BLK :], low[2 * BLK :]
    update = (
        dot_nt(left_high, right_high)
        + dot_nt(left_high, right_low)
        + dot_nt(left_low, right_high)
    )
    for r in range(2):
        schur[r * BLK : (r + 1) * BLK, :] = trail[r] - update[r * BLK : (r + 1) * BLK, :]
        start = pl.multiple_of((2 * sub + r) * BLK, BLK)
        factor[2 * r * BLK : (2 * r + 1) * BLK, :] = chol[z, pl.ds(start, BLK), :]
        factor[(2 * r + 1) * BLK : (2 * r + 2) * BLK, :] = solved[z, r * BLK : (r + 1) * BLK, :]


def call(kernel, name, outs, specs, args, scratch=(), flops=0, out_specs=None):
    return pl.pallas_call(
        kernel,
        name=name,
        out_shape=outs,
        in_specs=specs,
        out_specs=out_specs or [VMEM] * len(outs),
        scratch_shapes=list(scratch),
        compiler_params=PARAMS,
        cost_estimate=pl.CostEstimate(flops=flops, bytes_accessed=flops // 400, transcendentals=0)
        if flops
        else None,
    )(*args)


def swap(value, axis):
    return lax.ppermute(value, axis, [(0, 1), (1, 0)])


def per_device(
    child_updates,
    initial_one,
    initial_two,
    pattern_one,
    pattern_two,
    parent_map_one,
    parent_map_two,
):
    x, yh, yl = lax.axis_index("x"), lax.axis_index("yh"), lax.axis_index("yl")
    core, z = lax.axis_index("core"), lax.axis_index("front")
    ids = jnp.stack([x * 4 + yh * 2 + yl, core, z, x * 2 + yh, yl * 2 + core]).astype(jnp.int32)
    panel = (NB, NB * BLK, BLK)
    block = (BLK, BLK)

    (sent,) = call(
        pack_kernel,
        "pack",
        [shape(CHILD_ROWS + CORNER_ROWS, BLK)],
        [SMEM, SMEM, VMEM, ANY],
        (ids, pattern_one, child_updates, initial_one),
        [pltpu.VMEM((NB * BLK, BLK), F32), pltpu.VMEM((4, *block), F32), pltpu.SemaphoreType.DMA],
    )
    gathered = lax.all_gather(sent, ("core", "front"), axis=0, tiled=False)
    ids_mask, _ = lax.optimization_barrier((ids, sent))
    merged, corner_two, lower_two, row_two, tail_two = call(
        mask_kernel,
        "mask",
        [
            shape(LOWER_ROWS + CORNER_ROWS, BLK),
            shape(2 * BLK, BLK),
            shape(2 * BLK, BLK),
            shape(2 * BLK, BLK),
            shape(2, *block),
        ],
        [SMEM, SMEM, SMEM, VMEM, VMEM],
        (ids_mask, pattern_one, pattern_two, initial_one, initial_two),
        [pltpu.VMEM((4, *block), F32)],
    )
    corner_two = jnp.concatenate([corner_two, swap(corner_two, "yl")], 0)
    rows_all = lax.all_gather(row_two, ("yl", "core"), axis=0, tiled=False)
    merged, gathered, corner_two, rows_all = lax.optimization_barrier(
        (merged, gathered, corner_two, rows_all)
    )
    merged_all = lax.all_gather(merged, ("core", "front"), axis=0, tiled=False)
    chol, inverse, lower_add, trail_add = call(
        chol_kernel,
        "chol",
        [shape(*panel), shape(NB, *block), shape(*panel), shape(36, *block)],
        [SMEM, SMEM, ANY],
        (ids, parent_map_one, gathered),
        [
            pltpu.VMEM(panel, F32),
            pltpu.VMEM((2 * NB, 5 * BLK, BLK), F32),
            pltpu.VMEM(panel, F32),
            pltpu.VMEM((36, *block), F32),
            pltpu.SemaphoreType.DMA((64,)),
        ],
        flops=40_000_000_000,
        out_specs=[VMEM, VMEM, ANY, ANY],
    )
    lower_two, _ = lax.optimization_barrier((lower_two, gathered))
    gathered_two = lax.all_gather(corner_two, ("core", "front"), axis=0, tiled=False)
    lower_near = lax.all_gather(lower_two, "front", axis=0, tiled=False)
    factor_one, near_mine, near_other = call(
        rest_kernel,
        "rest",
        [shape(NB * BLK, BLK), shape(18, *block), shape(18, *block)],
        [SMEM] + [ANY] * 5,
        (ids, chol, inverse, lower_add, trail_add, merged_all),
        [pltpu.VMEM(panel, F32), pltpu.VMEM((NB, *block), F32)]
        + [pltpu.VMEM(panel, F32)] * 3
        + [pltpu.VMEM(panel, BF16)] * 2
        + [pltpu.VMEM((36, *block), F32)] * 2
        + [pltpu.SemaphoreType.DMA((64,))],
        flops=15_000_000_000,
        out_specs=[VMEM, ANY, ANY],
    )
    far_mine = swap(near_mine, "yl")
    far_other = swap(far_mine, "core")
    packed = (near_mine, near_other, far_mine, far_other)
    children = pltpu.VMEM((2, 36, *block), F32)
    chol, inverse = call(
        chol_two_kernel,
        "chol_two",
        [shape(*panel), shape(NB, *block)],
        [SMEM, SMEM] + [ANY] * 5,
        (ids, parent_map_two, gathered_two, *packed),
        [
            pltpu.VMEM(panel, F32),
            children,
            pltpu.SMEM((NB + 1,), jnp.int32),
            pltpu.SemaphoreType.DMA((8,)),
        ],
        flops=40_000_000_000,
    )
    rows = (NB, 3 * BLK, BLK)
    factor_two, schur_two = call(
        tail_kernel,
        "tail",
        [shape(4 * BLK, BLK), shape(2 * BLK, BLK)],
        [SMEM, SMEM, ANY] + [VMEM] * 4 + [ANY] * 4,
        (ids, parent_map_two, chol, inverse, lower_near, rows_all, tail_two, *packed),
        [
            pltpu.VMEM(panel, F32),
            children,
            pltpu.VMEM(rows, F32),
            pltpu.VMEM(rows, F32),
            pltpu.VMEM(rows, BF16),
            pltpu.VMEM(rows, BF16),
            pltpu.VMEM((2, *block), F32),
            pltpu.SMEM((2, FB), jnp.int32),
            pltpu.SemaphoreType.DMA((5,)),
        ],
    )
    return factor_one, factor_two, schur_two


def solution(mesh):
    cut = Mesh(mesh.devices.reshape(4, 2, 2, 2, 8), LEAF + ("front",))
    tile = P(LEAF, "front")
    return jax.shard_map(
        per_device,
        mesh=cut,
        in_specs=(tile, tile, tile, P(), P(), P(), P()),
        out_specs=(tile, tile, tile),
        check_vma=False,
    )
```

```python
import jax
import jax.numpy as jnp
from jax import lax
from jax.experimental import pallas as pl
from jax.experimental.pallas import tpu as pltpu
from jax.sharding import Mesh, PartitionSpec as P

BLK = 128
NB = 8
FB = 16
F32 = jnp.float32
BF16 = jnp.bfloat16
VMEM = pl.BlockSpec(memory_space=pltpu.VMEM)
SMEM = pl.BlockSpec(memory_space=pltpu.SMEM)
ANY = pl.BlockSpec(memory_space=pl.ANY)
HALF = BLK // 2
CORNER_ROWS = 2 * BLK + HALF
CHILD_ROWS = 4 * BLK + HALF
LOWER_ROWS = 4 * BLK
PARAMS = pltpu.CompilerParams(vmem_limit_bytes=58 * 1024 * 1024)
LEAF = ("x", "yh", "yl", "core")
MOST = 6
SOON = 22
LATE = 36 - SOON


def shape(*dims):
    return jax.ShapeDtypeStruct(dims, F32)


def packed_index(row, col):
    return col * NB - col * (col - 1) // 2 + row - col


def across(piece):
    return jnp.broadcast_to(piece, (8, BLK))


def lane_columns(rows, t):
    return [across(rows[:, 8 * t + b : 8 * t + b + 1]) for b in range(8)]


def factor_eights(rows, first, last):
    sub = lax.broadcasted_iota(jnp.int32, (8, BLK), 0)
    lane = lax.broadcasted_iota(jnp.int32, (8, BLK), 1)
    diag = jnp.zeros((8, BLK), F32)
    outs = []
    following = lane_columns(rows[first], first)
    for t in range(first, last):
        head = following
        below = {g: lane_columns(rows[g], t) for g in range(t + 1, last)}
        if t + 1 < last:
            following = lane_columns(rows[t + 1], t + 1)
        scale, weight = [], {}
        for b in range(8):
            pivot = across(head[b][b : b + 1])
            scale.append(lax.rsqrt(pivot))
            diag = jnp.where(lane == 8 * t + b, pivot * scale[b], diag)
            low = head[b] * scale[b]
            for a in range(b + 1, 8):
                weight[a, b] = across(low[a : a + 1])
                head[a] = head[a] - low * weight[a, b]
        inside = (lane >= 8 * t) & (lane < 8 * t + 8)
        pivots = []
        for b in range(8):
            unit = jnp.where(lane == 8 * t + b, 1.0, 0.0)
            row = jnp.where(inside, unit, across(rows[t][b : b + 1]))
            for a in range(b):
                row = row - weight[b, a] * pivots[a]
            pivots.append(row * scale[b])
        for g in range(t + 1, last):
            lows = []
            for b in range(8):
                column = below[g][b]
                for a in range(b):
                    column = column - lows[a] * weight[b, a]
                lows.append(column * scale[b])
            if g == t + 1:
                for b in range(8):
                    for a in range(8):
                        following[a] = following[a] - lows[b] * across(lows[b][a : a + 1])
            group = jnp.where(inside, 0.0, rows[g])
            for b in range(8):
                group = group - lows[b] * pivots[b]
            rows[g] = group
        group = pivots[7]
        for b in range(6, -1, -1):
            group = jnp.where(sub == b, pivots[b], group)
        rows[t] = group
        for a in range(1, 8):
            column = weight[a, a - 1]
            for b in range(a - 2, -1, -1):
                column = jnp.where(sub == b, weight[a, b], column)
            group = jnp.where((lane == 8 * t + a) & (sub < a), column, group)
        outs.append(group)
    return outs, diag


def factor_block(block):
    rows = [block[8 * g : 8 * g + 8] for g in range(16)]
    outs, diag = factor_eights(rows, 0, 8)
    lane = lax.broadcasted_iota(jnp.int32, (8, BLK), 1)
    row_id = lax.broadcasted_iota(jnp.int32, (BLK // 2, BLK), 0)
    col_id = lax.broadcasted_iota(jnp.int32, (BLK // 2, BLK), 1)
    left = jnp.concatenate(rows[:8], 0)
    right = jnp.where((col_id > row_id) & (col_id < BLK // 2), 0.0, left)
    left_high, left_low = halves(left)
    right_high, right_low = halves(right)
    update = lax.dot_general(
        jnp.concatenate([left_high, left_high, left_low], 0),
        jnp.concatenate([right_high, right_low, right_high], 0),
        (((0,), (0,)), ((), ())),
        preferred_element_type=F32,
    )
    for g in range(8, 16):
        rows[g] = jnp.where(lane < BLK // 2, 0.0, rows[g]) - update[8 * g : 8 * g + 8]
    more, more_diag = factor_eights(rows, 8, 16)
    full = jnp.concatenate(outs + more, 0)
    row_id = lax.broadcasted_iota(jnp.int32, (BLK, BLK), 0)
    col_id = lax.broadcasted_iota(jnp.int32, (BLK, BLK), 1)
    on_diag = jnp.broadcast_to((diag + more_diag)[0:1], (BLK, BLK))
    upper = jnp.where(col_id > row_id, full, jnp.where(col_id == row_id, on_diag, 0.0))
    return upper.T, jnp.where(col_id <= row_id, full, 0.0)


def halves(value):
    high = value.astype(BF16)
    return high, (value - high.astype(F32)).astype(BF16)


def dot_nt(left, right):
    return lax.dot_general(
        left, right, (((1,), (1,)), ((), ())), preferred_element_type=F32
    )


def dot_split(left, right):
    left_high, left_low = halves(left)
    right_high, right_low = halves(right)
    return dot_nt(
        jnp.concatenate([left_high, left_high, left_low], 1),
        jnp.concatenate([right_high, right_low, right_high], 1),
    )


def factor_corner(work, chol, inverse):
    order = NB * BLK

    def one_panel(step, carry):
        first = pl.multiple_of(step * BLK, BLK)
        lower, lower_inverse = factor_block(work[step, pl.ds(first, BLK), :])
        chol[step, pl.ds(first, BLK), :] = lower
        inverse[step] = lower_inverse
        for j in range(NB - 1):

            @pl.when(step == j)
            def _():
                start = BLK * (j + 1)
                panel = dot_split(work[j, start:, :], inverse[j])
                chol[j, start:, :] = panel
                high, low = halves(panel)
                left = jnp.concatenate([high, high, low], 1)
                right = jnp.concatenate([high, low, high], 1)
                for k in range(j + 1, NB, 2):
                    wide = min(2, NB - k)
                    top = BLK * k - start
                    update = dot_nt(left[top:], right[top : top + wide * BLK])
                    for w in range(wide):
                        work[k + w, BLK * k :, :] = (
                            work[k + w, BLK * k :, :] - update[:, w * BLK : (w + 1) * BLK]
                        )

        return carry

    for j in range(1, NB):
        chol[j, : j * BLK, :] = jnp.zeros((j * BLK, BLK), F32)
    lax.fori_loop(0, NB, one_panel, 0)


def factor_corner_again(work, chol, inverse):
    def rows_of(block):
        return pl.ds(pl.multiple_of(block * BLK, BLK), BLK)

    def one_panel(step, carry):
        lower, lower_inverse = factor_block(work[step, rows_of(step), :])
        chol[step, rows_of(step), :] = lower
        inverse[step] = lower_inverse

        def one_block(i, carry):
            chol[step, rows_of(i), :] = dot_split(work[step, rows_of(i), :], inverse[step])
            return carry

        def one_col(k, carry):
            def one_row(i, carry):
                work[k, rows_of(i), :] = work[k, rows_of(i), :] - dot_split(
                    chol[step, rows_of(i), :], chol[step, rows_of(k), :]
                )
                return carry

            return lax.fori_loop(k, NB, one_row, carry)

        lax.fori_loop(step + 1, NB, one_block, 0)
        return lax.fori_loop(step + 1, NB, one_col, carry)

    chol[...] = jnp.zeros_like(chol)
    lax.fori_loop(0, NB, one_panel, 0)


def solve_rows(right_side, chol, inverse, solved, solved_high, solved_low):
    for p in range(0, NB, 2):
        value = right_side(p)
        if p:
            depth = range(p)
            left_high = jnp.concatenate([solved_high[k] for k in depth], 1)
            left_low = jnp.concatenate([solved_low[k] for k in depth], 1)
            right = jnp.concatenate([chol[k, p * BLK : (p + 2) * BLK, :] for k in depth], 1)
            right_high, right_low = halves(right)
            value = value - (
                dot_nt(left_high, right_high)
                + dot_nt(left_high, right_low)
                + dot_nt(left_low, right_high)
            )
        between = chol[p, (p + 1) * BLK : (p + 2) * BLK, :]
        corner = -dot_split(inverse[p + 1], dot_split(inverse[p].T, between))
        pair_inverse = jnp.concatenate(
            [
                jnp.concatenate([inverse[p], jnp.zeros((BLK, BLK), F32)], 1),
                jnp.concatenate([corner, inverse[p + 1]], 1),
            ],
            0,
        )
        value = dot_split(value, pair_inverse)
        high, low = halves(value)
        for w in range(2):
            lanes = slice(w * BLK, (w + 1) * BLK)
            solved[p + w] = value[:, lanes]
            solved_high[p + w], solved_low[p + w] = high[:, lanes], low[:, lanes]


def pair(ref, p):
    return jnp.concatenate([ref[p], ref[p + 1]], 1)


def place_of(block_map, front, child, slots):
    for m in range(FB):
        slots[child, m] = -1
    for i in range(NB):
        slots[child, block_map[front, child, i]] = i


def kept(pattern, front, row, col):
    return (pattern[front, row, col] == 1) | (pattern[front, col, row] == 1) | (row == col)


def first_turn(core, z):
    return jnp.where((core == 0) & (z >= 4), 1, 0)


def send_blocks(tile, core, z, out):
    base = NB // 2 * core
    for turn in range(2):
        local = (z + first_turn(core, z) + turn) % 4
        block = tile[local]
        at = turn * BLK

        @pl.when(base + local >= z)
        def _():
            out[at : at + BLK, :] = block

        @pl.when(base + local < z)
        def _():
            out[at : at + BLK, :] = block.T

    block = tile[(z + 2) % 4]

    @pl.when(z % 4 < 2)
    def _():
        out[2 * BLK :, :] = block[:HALF, :]

    @pl.when(z % 4 >= 2)
    def _():
        out[2 * BLK :, :] = block.T[HALF:, :]


def static_blocks():
    where = {}
    for core in range(2):
        for z in range(NB):
            turn0 = 1 if core == 0 and z >= 4 else 0
            for turn in range(2):
                row = 4 * core + (z + turn0 + turn) % 4
                where[max(row, z), min(row, z)] = [(core * NB + z, turn * BLK, BLK)]
            if z // 4 == core:
                row = 4 * core + (z + 2) % 4
                key = (max(row, z), min(row, z))
                entry = (core * NB + z, 2 * BLK, HALF)
                known = where.setdefault(key, [])
                if z % 4 < 2:
                    known.insert(0, entry)
                else:
                    known.append(entry)
    return where


def send_child(child, z, out):
    for turn in range(4):
        row = (z + turn) % NB
        at = turn * BLK
        block = child[pl.ds(pl.multiple_of(row * BLK, BLK), BLK), :]

        @pl.when(row >= z)
        def _():
            out[at : at + BLK, :] = block

        @pl.when(row < z)
        def _():
            out[at : at + BLK, :] = block.T

    row = (z + 4) % NB
    block = child[pl.ds(pl.multiple_of(row * BLK, BLK), BLK), :]

    @pl.when(row > z)
    def _():
        out[4 * BLK :, :] = block[:HALF, :]

    @pl.when(row < z)
    def _():
        out[4 * BLK :, :] = block.T[HALF:, :]


def child_copies(gathered, children, sems):
    return [
        pltpu.make_async_copy(
            gathered.at[:, :CHILD_ROWS, :], children.at[:, :CHILD_ROWS, :], sems.at[0]
        )
    ] + [
        pltpu.make_async_copy(
            gathered.at[child * NB + 4 : child * NB + 8, 4 * BLK : CHILD_ROWS, :],
            children.at[child * NB : child * NB + 4, CHILD_ROWS:, :],
            sems.at[1 + child],
        )
        for child in range(2)
    ]


def each_gathered(block_map, front, children, visit):
    def one(n, carry):
        child, m = n // 36, n % 36
        z = jnp.where(m < 32, m // 4, m - 32)
        turn = jnp.where(m < 32, m % 4, 4)
        other = (z + turn) % NB
        row = block_map[front, child, jnp.maximum(z, other)]
        col = block_map[front, child, jnp.minimum(z, other)]
        start = pl.multiple_of(turn * BLK, BLK)
        visit(row, col, lambda: children[child * NB + z, pl.ds(start, BLK), :])
        return carry

    lax.fori_loop(0, 72, one, 0)


def ordered(block_map, front, child, order, place):
    count = jnp.int32(0)
    for parity in range(2):
        for i in range(NB):
            hit = block_map[front, child, i] % 2 == parity

            @pl.when(hit)
            def _(count=count, i=i):
                order[child, count] = i
                place[child, i] = count

            count = count + jnp.where(hit, 1, 0)
        if parity == 0:
            separators = count
    return separators


def number_of(a, b):
    return a * (a + 1) // 2 + b


def block_number(place, child, i, k):
    a, b = place[child, i], place[child, k]
    return number_of(jnp.maximum(a, b), jnp.minimum(a, b))


def add_ordered_separators(block_map, front, children, work, order, counts):
    for child in range(2):

        def one_place(a, carry):
            def other_place(b, carry):
                i, k = order[child, a], order[child, b]
                row = block_map[front, child, jnp.maximum(i, k)] // 2
                col = block_map[front, child, jnp.minimum(i, k)] // 2
                number = number_of(a, b)

                @pl.when(row >= col)
                def _():
                    add_at(work, col, row, children[child, number])

                @pl.when(row < col)
                def _():
                    add_at(work, row, col, children[child, number].T)

                return carry

            return lax.fori_loop(0, a + 1, other_place, carry)

        lax.fori_loop(0, counts[child], one_place, 0)


def add_at(ref, lead, block_row, block):
    place = pl.ds(pl.multiple_of(block_row * BLK, BLK), BLK)
    ref[lead, place, :] = ref[lead, place, :] + block


def contributions_into(corner, lower, trail):
    def visit(row, col, block):
        row_odd, col_odd = row % 2 == 1, col % 2 == 1
        row_half, col_half = row // 2, col // 2

        @pl.when(~row_odd & ~col_odd & (row >= col))
        def _():
            add_at(corner, col_half, row_half, block())

        @pl.when(~row_odd & ~col_odd & (row < col))
        def _():
            add_at(corner, row_half, col_half, block().T)

        @pl.when(row_odd & ~col_odd)
        def _():
            add_at(lower, col_half, row_half, block())

        @pl.when(~row_odd & col_odd)
        def _():
            add_at(lower, row_half, col_half, block().T)

        @pl.when(row_odd & col_odd & (row >= col))
        def _():
            add_at(trail, packed_index(row_half, col_half), 0, block())

        @pl.when(row_odd & col_odd & (row < col))
        def _():
            add_at(trail, packed_index(col_half, row_half), 0, block().T)

    return visit


def masked_tile(initial, pattern, front, row, local, col):
    keep = kept(pattern, front, row, col)
    return jnp.where(keep, initial[local * BLK : (local + 1) * BLK, :], 0.0)


def pack_kernel(ids, pattern_one, child, initial, merged, columns, tile, sem):
    front_one, side, z = ids[0], ids[1], ids[2]
    copy = pltpu.make_async_copy(initial.at[:, :BLK], columns, sem)
    copy.start()
    send_child(child, z, merged.at[:CHILD_ROWS, :])
    copy.wait()
    for r in range(4):
        tile[r] = masked_tile(columns, pattern_one, front_one, NB * side + 2 * r, 2 * r, 2 * z)
    send_blocks(tile, side, z, merged.at[CHILD_ROWS:, :])


def mask_kernel(
    ids,
    pattern_one,
    pattern_two,
    initial_one,
    initial_two,
    merged,
    corner_two,
    lower_two,
    row_two,
    tail_two,
    tile,
):
    front_one, side, z, front_two, sub = ids[0], ids[1], ids[2], ids[3], ids[4]
    first, second = initial_one.at[:, :BLK], initial_one.at[:, BLK:]
    for r in range(4):
        row = NB * side + 2 * r + 1
        merged[r * BLK : (r + 1) * BLK, :] = masked_tile(
            first, pattern_one, front_one, row, 2 * r + 1, 2 * z
        )
        tile[r] = masked_tile(second, pattern_one, front_one, row, 2 * r + 1, 2 * z + 1)
    send_blocks(tile, side, z, merged.at[LOWER_ROWS:, :])
    for r in range(4):
        for w in range(2):
            columns = initial_two.at[:, w * BLK : (w + 1) * BLK]
            block = masked_tile(columns, pattern_two, front_two, 4 * sub + r, r, 2 * z + w)
            at = slice(r // 2 * BLK, (r // 2 + 1) * BLK)
            if w == 0:
                (corner_two if r % 2 == 0 else lower_two)[at, :] = block
            elif r % 2 == 0:
                row_two[at, :] = block.T
            else:
                tail_two[r // 2] = block


def chol_kernel(
    ids,
    block_map,
    gathered,
    chol,
    inverse,
    lower_out,
    trail_out,
    work,
    children,
    lower,
    trail,
    sems,
):
    front = ids[0]
    copies = child_copies(gathered, children, sems)
    for (row, col), parts in static_blocks().items():
        start = row * BLK
        for piece, at, rows in parts:
            copies.append(
                pltpu.make_async_copy(
                    gathered.at[piece, CHILD_ROWS + at : CHILD_ROWS + at + rows, :],
                    work.at[col, start : start + rows, :],
                    sems.at[len(copies)],
                )
            )
            start += rows
    for copy in copies:
        copy.start()
    lower[...] = jnp.zeros_like(lower)
    trail[...] = jnp.zeros_like(trail)
    for copy in copies:
        copy.wait()
    each_gathered(block_map, front, children, contributions_into(work, lower, trail))
    outs = [
        pltpu.make_async_copy(lower, lower_out, sems.at[0]),
        pltpu.make_async_copy(trail, trail_out, sems.at[1]),
    ]
    for copy in outs:
        copy.start()
    factor_corner(work, chol, inverse)
    for copy in outs:
        copy.wait()


def rest_kernel(
    ids,
    block_map,
    chol_in,
    inverse_in,
    lower_in,
    trail_in,
    merged,
    factor,
    mine,
    other,
    late,
    chol,
    inverse,
    lower,
    lower_add,
    solved,
    solved_high,
    solved_low,
    trail,
    trail_add,
    staged,
    order,
    place,
    sems,
):
    side, z, child = ids[1], ids[2], ids[4] // 2
    half = NB // 2 * BLK
    used = []

    def fetch(source, target):
        copy = pltpu.make_async_copy(source, target, sems.at[len(used)])
        copy.start()
        used.append(copy)
        return copy

    first = [fetch(inverse_in, inverse)]
    columns = {}
    for p in range(0, NB, 2):
        columns[p] = [fetch(lower_in.at[p : p + 2], lower_add.at[p : p + 2])]
        for core in range(2):
            columns[p].append(
                fetch(
                    merged.at[core * NB + p : core * NB + p + 2, :LOWER_ROWS, :],
                    lower.at[p : p + 2, core * half : (core + 1) * half, :],
                )
            )
        if p == 0:
            first.append(fetch(chol_in, chol))
    last = [fetch(trail_in, trail_add)]
    for (row, col), parts in static_blocks().items():
        start = 0
        for piece, at, rows in parts:
            last.append(
                fetch(
                    merged.at[piece, LOWER_ROWS + at : LOWER_ROWS + at + rows, :],
                    trail.at[packed_index(row, col), start : start + rows, :],
                )
            )
            start += rows
    ordered(block_map, ids[3], child, order, place)
    for copy in first:
        copy.wait()

    def right_side(p):
        for copy in columns[p]:
            copy.wait()
        return pair(lower, p) + pair(lower_add, p)

    solve_rows(right_side, chol, inverse, solved, solved_high, solved_low)
    for copy in last:
        copy.wait()
    for p in range(0, NB, 2):
        high = jnp.concatenate([solved_high[k, p * BLK :, :] for k in range(NB)], 1)
        low = jnp.concatenate([solved_low[k, p * BLK :, :] for k in range(NB)], 1)
        wide_high, wide_low = high[: 2 * BLK], low[: 2 * BLK]
        update = dot_nt(high, wide_high) + dot_nt(high, wide_low) + dot_nt(low, wide_high)
        for w in range(2):
            for i in range(p + w, NB):
                index = packed_index(i, p + w)
                number = block_number(place, child, i, p + w)
                half_id = jnp.where(number < SOON // 2, 0, 1)
                soon = (half_id + side) % 2 * (SOON // 2) + number - half_id * (SOON // 2)
                staged[jnp.where(number < SOON, soon, number)] = (
                    trail[index]
                    + trail_add[index]
                    - update[(i - p) * BLK : (i - p + 1) * BLK, w * BLK : (w + 1) * BLK]
                )
    outs = [
        pltpu.make_async_copy(staged.at[: SOON // 2], mine, sems.at[0]),
        pltpu.make_async_copy(staged.at[SOON // 2 : SOON], other, sems.at[1]),
        pltpu.make_async_copy(staged.at[SOON:], late, sems.at[2]),
    ]
    for copy in outs:
        copy.start()
    for r in range(NB):
        source = solved if r % 2 else chol
        start = pl.multiple_of((side * (NB // 2) + r // 2) * BLK, BLK)
        factor[r * BLK : (r + 1) * BLK, :] = source[z, pl.ds(start, BLK), :]
    for copy in outs:
        copy.wait()


def fetch_children(side, mine, refs, children, sems):
    near_mine, near_other, far_mine, far_other = refs
    half = SOON // 2
    copies = []
    for n, (ref, child, half_id) in enumerate(
        (
            (near_mine, mine, side),
            (near_other, mine, 1 - side),
            (far_mine, 1 - mine, side),
            (far_other, 1 - mine, 1 - side),
        )
    ):
        target = children.at[child, pl.ds(half * half_id, half)]
        copies.append(pltpu.make_async_copy(ref, target, sems.at[n]))
        copies[-1].start()
    return copies


def corner_copies(side_of, gathered, work, sems):
    copies = []
    for core in range(2):
        for n, y in ((0, side_of), (1, 1 - side_of)):
            start = pl.multiple_of(2 * (2 * y + core) * BLK, BLK)
            copies.append(
                pltpu.make_async_copy(
                    gathered.at[core * NB : (core + 1) * NB, 2 * n * BLK : 2 * (n + 1) * BLK, :],
                    work.at[:, pl.ds(start, 2 * BLK), :],
                    sems.at[2 * core + n],
                )
            )
            copies[-1].start()
    return copies


def chol_two_kernel(
    ids,
    block_map,
    gathered,
    near_mine,
    near_other,
    far_mine,
    far_other,
    chol,
    inverse,
    work,
    children,
    order,
    place,
    sems,
    corner_sems,
):
    side, front, sub = ids[1], ids[3], ids[4]
    copies = fetch_children(
        side, sub // 2, (near_mine, near_other, far_mine, far_other), children, sems
    )
    copies += corner_copies(sub // 2, gathered, work, corner_sems)
    counts = [
        jnp.minimum(ordered(block_map, front, child, order, place), MOST) for child in range(2)
    ]
    for copy in copies:
        copy.wait()
    add_ordered_separators(block_map, front, children, work, order, counts)
    factor_corner(work, chol, inverse)


def tail_kernel(
    ids,
    map_two,
    gathered,
    chol_in,
    inverse_in,
    lower_near,
    rows_all,
    tail,
    near_mine,
    near_other,
    far_mine,
    far_other,
    near_late,
    far_late,
    factor,
    schur,
    chol,
    inverse,
    work,
    children,
    lower,
    solved,
    solved_high,
    solved_low,
    trail,
    slots,
    order,
    place,
    sems,
    corner_sems,
):
    side, z, front, sub = ids[1], ids[2], ids[3], ids[4]
    mine = sub // 2
    copies = fetch_children(
        side, mine, (near_mine, near_other, far_mine, far_other), children, sems
    )
    for n, (ref, child) in enumerate(((near_late, mine), (far_late, 1 - mine))):
        copies.append(
            pltpu.make_async_copy(ref, children.at[child, pl.ds(SOON, LATE)], sems.at[4 + n])
        )
        copies[-1].start()
    factors = [
        pltpu.make_async_copy(chol_in, chol, sems.at[6]),
        pltpu.make_async_copy(inverse_in, inverse, sems.at[7]),
    ]
    for copy in factors:
        copy.start()
    counts = [ordered(map_two, front, child, order, place) for child in range(2)]
    place_of(map_two, front, 0, slots)
    place_of(map_two, front, 1, slots)
    lower[:, : 2 * BLK, :] = lower_near[...]
    for s in range(4):
        for b in range(2):
            lower[2 * s + b, 2 * BLK :, :] = rows_all[s, b * BLK : (b + 1) * BLK, :]
    trail[...] = tail[...]
    for copy in copies:
        copy.wait()
    wanted = (2 * sub, 2 * sub + 1, z)

    def one_child(child, carry):
        for slot, target in enumerate(wanted):
            i = slots[child, 2 * target + 1]

            def one_block(k, carry):
                col = map_two[front, child, k]
                index = block_number(place, child, i, k)

                @pl.when((col % 2 == 0) & (i > k))
                def _():
                    add_at(lower, col // 2, slot, children[child, index])

                @pl.when((col % 2 == 0) & (i < k))
                def _():
                    add_at(lower, col // 2, slot, children[child, index].T)

                return carry

            lax.fori_loop(0, jnp.where(i >= 0, NB, 0), one_block, 0)
        k = slots[child, 2 * z + 1]
        for slot in range(2):
            i = slots[child, 2 * wanted[slot] + 1]
            both = (i >= 0) & (k >= 0)
            index = block_number(place, child, jnp.maximum(i, 0), jnp.maximum(k, 0))

            @pl.when(both & (i >= k))
            def _():
                trail[slot] = trail[slot] + children[child, index]

            @pl.when(both & (i < k))
            def _():
                trail[slot] = trail[slot] + children[child, index].T

        return carry

    lax.fori_loop(0, 2, one_child, 0)
    for copy in factors:
        copy.wait()

    @pl.when(jnp.maximum(counts[0], counts[1]) > MOST)
    def _():
        for copy in corner_copies(mine, gathered, work, corner_sems):
            copy.wait()
        add_ordered_separators(map_two, front, children, work, order, counts)
        factor_corner_again(work, chol, inverse)

    solve_rows(lambda p: pair(lower, p), chol, inverse, solved, solved_high, solved_low)
    high = jnp.concatenate([solved_high[k] for k in range(NB)], 1)
    low = jnp.concatenate([solved_low[k] for k in range(NB)], 1)
    left_high, left_low = high[: 2 * BLK], low[: 2 * BLK]
    right_high, right_low = high[2 * BLK :], low[2 * BLK :]
    update = (
        dot_nt(left_high, right_high)
        + dot_nt(left_high, right_low)
        + dot_nt(left_low, right_high)
    )
    for r in range(2):
        schur[r * BLK : (r + 1) * BLK, :] = trail[r] - update[r * BLK : (r + 1) * BLK, :]
        start = pl.multiple_of((2 * sub + r) * BLK, BLK)
        factor[2 * r * BLK : (2 * r + 1) * BLK, :] = chol[z, pl.ds(start, BLK), :]
        factor[(2 * r + 1) * BLK : (2 * r + 2) * BLK, :] = solved[z, r * BLK : (r + 1) * BLK, :]


def call(kernel, name, outs, specs, args, scratch=(), flops=0, out_specs=None):
    return pl.pallas_call(
        kernel,
        name=name,
        out_shape=outs,
        in_specs=specs,
        out_specs=out_specs or [VMEM] * len(outs),
        scratch_shapes=list(scratch),
        compiler_params=PARAMS,
        cost_estimate=pl.CostEstimate(flops=flops, bytes_accessed=flops // 400, transcendentals=0)
        if flops
        else None,
    )(*args)


def swap(value, axis):
    return lax.ppermute(value, axis, [(0, 1), (1, 0)])


def per_device(
    child_updates,
    initial_one,
    initial_two,
    pattern_one,
    pattern_two,
    parent_map_one,
    parent_map_two,
):
    x, yh, yl = lax.axis_index("x"), lax.axis_index("yh"), lax.axis_index("yl")
    core, z = lax.axis_index("core"), lax.axis_index("front")
    ids = jnp.stack([x * 4 + yh * 2 + yl, core, z, x * 2 + yh, yl * 2 + core]).astype(jnp.int32)
    panel = (NB, NB * BLK, BLK)
    block = (BLK, BLK)

    (sent,) = call(
        pack_kernel,
        "pack",
        [shape(CHILD_ROWS + CORNER_ROWS, BLK)],
        [SMEM, SMEM, VMEM, ANY],
        (ids, pattern_one, child_updates, initial_one),
        [pltpu.VMEM((NB * BLK, BLK), F32), pltpu.VMEM((4, *block), F32), pltpu.SemaphoreType.DMA],
    )
    gathered = lax.all_gather(sent, ("core", "front"), axis=0, tiled=False)
    ids_mask, _ = lax.optimization_barrier((ids, sent))
    merged, corner_two, lower_two, row_two, tail_two = call(
        mask_kernel,
        "mask",
        [
            shape(LOWER_ROWS + CORNER_ROWS, BLK),
            shape(2 * BLK, BLK),
            shape(2 * BLK, BLK),
            shape(2 * BLK, BLK),
            shape(2, *block),
        ],
        [SMEM, SMEM, SMEM, VMEM, VMEM],
        (ids_mask, pattern_one, pattern_two, initial_one, initial_two),
        [pltpu.VMEM((4, *block), F32)],
    )
    corner_two = jnp.concatenate([corner_two, swap(corner_two, "yl")], 0)
    rows_all = lax.all_gather(row_two, ("yl", "core"), axis=0, tiled=False)
    merged, gathered, corner_two, rows_all = lax.optimization_barrier(
        (merged, gathered, corner_two, rows_all)
    )
    merged_all = lax.all_gather(merged, ("core", "front"), axis=0, tiled=False)
    chol, inverse, lower_add, trail_add = call(
        chol_kernel,
        "chol",
        [shape(*panel), shape(NB, *block), shape(*panel), shape(36, *block)],
        [SMEM, SMEM, ANY],
        (ids, parent_map_one, gathered),
        [
            pltpu.VMEM(panel, F32),
            pltpu.VMEM((2 * NB, 5 * BLK, BLK), F32),
            pltpu.VMEM(panel, F32),
            pltpu.VMEM((36, *block), F32),
            pltpu.SemaphoreType.DMA((64,)),
        ],
        flops=40_000_000_000,
        out_specs=[VMEM, VMEM, ANY, ANY],
    )
    lower_two, _ = lax.optimization_barrier((lower_two, gathered))
    gathered_two = lax.all_gather(corner_two, ("core", "front"), axis=0, tiled=False)
    lower_near = lax.all_gather(lower_two, "front", axis=0, tiled=False)
    places = pltpu.SMEM((2, NB), jnp.int32)
    factor_one, near_mine, near_other, near_late = call(
        rest_kernel,
        "rest",
        [
            shape(NB * BLK, BLK),
            shape(SOON // 2, *block),
            shape(SOON // 2, *block),
            shape(LATE, *block),
        ],
        [SMEM, SMEM] + [ANY] * 5,
        (ids, parent_map_two, chol, inverse, lower_add, trail_add, merged_all),
        [pltpu.VMEM(panel, F32), pltpu.VMEM((NB, *block), F32)]
        + [pltpu.VMEM(panel, F32)] * 3
        + [pltpu.VMEM(panel, BF16)] * 2
        + [pltpu.VMEM((36, *block), F32)] * 3
        + [places, places, pltpu.SemaphoreType.DMA((64,))],
        flops=15_000_000_000,
        out_specs=[VMEM, ANY, ANY, ANY],
    )
    far_mine = swap(near_mine, "yl")
    far_other = swap(far_mine, "core")
    packed = (near_mine, near_other, far_mine, far_other)
    given_late, _ = lax.optimization_barrier((near_late, far_mine))
    far_late = swap(given_late, "yl")
    children = pltpu.VMEM((2, 36, *block), F32)
    chol, inverse = call(
        chol_two_kernel,
        "chol_two",
        [shape(*panel), shape(NB, *block)],
        [SMEM, SMEM] + [ANY] * 5,
        (ids, parent_map_two, gathered_two, *packed),
        [
            pltpu.VMEM(panel, F32),
            children,
            places,
            places,
            pltpu.SemaphoreType.DMA((4,)),
            pltpu.SemaphoreType.DMA((4,)),
        ],
        flops=40_000_000_000,
    )
    rows = (NB, 3 * BLK, BLK)
    factor_two, schur_two = call(
        tail_kernel,
        "tail",
        [shape(4 * BLK, BLK), shape(2 * BLK, BLK)],
        [SMEM, SMEM, ANY, ANY, ANY] + [VMEM] * 3 + [ANY] * 6,
        (
            ids,
            parent_map_two,
            gathered_two,
            chol,
            inverse,
            lower_near,
            rows_all,
            tail_two,
            *packed,
            near_late,
            far_late,
        ),
        [
            pltpu.VMEM(panel, F32),
            pltpu.VMEM((NB, *block), F32),
            pltpu.VMEM(panel, F32),
            children,
            pltpu.VMEM(rows, F32),
            pltpu.VMEM(rows, F32),
            pltpu.VMEM(rows, BF16),
            pltpu.VMEM(rows, BF16),
            pltpu.VMEM((2, *block), F32),
            pltpu.SMEM((2, FB), jnp.int32),
            places,
            places,
            pltpu.SemaphoreType.DMA((8,)),
            pltpu.SemaphoreType.DMA((4,)),
        ],
    )
    return factor_one, factor_two, schur_two


def solution(mesh):
    cut = Mesh(mesh.devices.reshape(4, 2, 2, 2, 8), LEAF + ("front",))
    tile = P(LEAF, "front")
    return jax.shard_map(
        per_device,
        mesh=cut,
        in_specs=(tile, tile, tile, P(), P(), P(), P()),
        out_specs=(tile, tile, tile),
        check_vma=False,
    )
```

```python
import jax
import jax.numpy as jnp
from jax import lax
from jax.experimental import pallas as pl
from jax.experimental.pallas import tpu as pltpu
from jax.sharding import Mesh, PartitionSpec as P

BLK = 128
NB = 8
FB = 16
F32 = jnp.float32
BF16 = jnp.bfloat16
VMEM = pl.BlockSpec(memory_space=pltpu.VMEM)
SMEM = pl.BlockSpec(memory_space=pltpu.SMEM)
ANY = pl.BlockSpec(memory_space=pl.ANY)
HALF = BLK // 2
CORNER_ROWS = 2 * BLK + HALF
CHILD_ROWS = 4 * BLK + HALF
LOWER_ROWS = 4 * BLK
PARAMS = pltpu.CompilerParams(vmem_limit_bytes=58 * 1024 * 1024)
LEAF = ("x", "yh", "yl", "core")
MOST = 6
SOON = 22
LATE = 36 - SOON


def shape(*dims):
    return jax.ShapeDtypeStruct(dims, F32)


def packed_index(row, col):
    return col * NB - col * (col - 1) // 2 + row - col


def across(piece):
    return jnp.broadcast_to(piece, (8, BLK))


def lane_columns(rows, t):
    return [across(rows[:, 8 * t + b : 8 * t + b + 1]) for b in range(8)]


def factor_eights(rows, first, last):
    sub = lax.broadcasted_iota(jnp.int32, (8, BLK), 0)
    lane = lax.broadcasted_iota(jnp.int32, (8, BLK), 1)
    diag = jnp.zeros((8, BLK), F32)
    outs = []
    following = lane_columns(rows[first], first)
    for t in range(first, last):
        head = following
        below = {g: lane_columns(rows[g], t) for g in range(t + 1, last)}
        if t + 1 < last:
            following = lane_columns(rows[t + 1], t + 1)
        scale, weight = [], {}
        ahead = across(head[0][0:1])
        for b in range(8):
            pivot = ahead
            scale.append(lax.rsqrt(pivot))
            diag = jnp.where(lane == 8 * t + b, pivot * scale[b], diag)
            low = head[b] * scale[b]
            for a in range(b + 1, 8):
                weight[a, b] = across(head[b][a : a + 1]) * scale[b]
                if a == b + 1:
                    ahead = across(head[a][a : a + 1]) - weight[a, b] * weight[a, b]
                head[a] = head[a] - low * weight[a, b]
        inside = (lane >= 8 * t) & (lane < 8 * t + 8)
        pivots = []
        for b in range(8):
            unit = jnp.where(lane == 8 * t + b, 1.0, 0.0)
            row = jnp.where(inside, unit, across(rows[t][b : b + 1]))
            for a in range(b):
                row = row - weight[b, a] * pivots[a]
            pivots.append(row * scale[b])
        for g in range(t + 1, last):
            lows = []
            for b in range(8):
                column = below[g][b]
                for a in range(b):
                    column = column - lows[a] * weight[b, a]
                lows.append(column * scale[b])
            if g == t + 1:
                for b in range(8):
                    for a in range(8):
                        following[a] = following[a] - lows[b] * across(lows[b][a : a + 1])
            group = jnp.where(inside, 0.0, rows[g])
            for b in range(8):
                group = group - lows[b] * pivots[b]
            rows[g] = group
        group = pivots[7]
        for b in range(6, -1, -1):
            group = jnp.where(sub == b, pivots[b], group)
        rows[t] = group
        for a in range(1, 8):
            column = weight[a, a - 1]
            for b in range(a - 2, -1, -1):
                column = jnp.where(sub == b, weight[a, b], column)
            group = jnp.where((lane == 8 * t + a) & (sub < a), column, group)
        outs.append(group)
    return outs, diag


def factor_block(block):
    rows = [block[8 * g : 8 * g + 8] for g in range(16)]
    outs, diag = factor_eights(rows, 0, 8)
    lane = lax.broadcasted_iota(jnp.int32, (8, BLK), 1)
    row_id = lax.broadcasted_iota(jnp.int32, (BLK // 2, BLK), 0)
    col_id = lax.broadcasted_iota(jnp.int32, (BLK // 2, BLK), 1)
    left = jnp.concatenate(rows[:8], 0)
    right = jnp.where((col_id > row_id) & (col_id < BLK // 2), 0.0, left)
    left_high, left_low = halves(left)
    right_high, right_low = halves(right)
    update = lax.dot_general(
        jnp.concatenate([left_high, left_high, left_low], 0),
        jnp.concatenate([right_high, right_low, right_high], 0),
        (((0,), (0,)), ((), ())),
        preferred_element_type=F32,
    )
    for g in range(8, 16):
        rows[g] = jnp.where(lane < BLK // 2, 0.0, rows[g]) - update[8 * g : 8 * g + 8]
    more, more_diag = factor_eights(rows, 8, 16)
    full = jnp.concatenate(outs + more, 0)
    row_id = lax.broadcasted_iota(jnp.int32, (BLK, BLK), 0)
    col_id = lax.broadcasted_iota(jnp.int32, (BLK, BLK), 1)
    on_diag = jnp.broadcast_to((diag + more_diag)[0:1], (BLK, BLK))
    upper = jnp.where(col_id > row_id, full, jnp.where(col_id == row_id, on_diag, 0.0))
    return upper.T, jnp.where(col_id <= row_id, full, 0.0)


def halves(value):
    high = value.astype(BF16)
    return high, (value - high.astype(F32)).astype(BF16)


def dot_nt(left, right):
    return lax.dot_general(
        left, right, (((1,), (1,)), ((), ())), preferred_element_type=F32
    )


def dot_split(left, right):
    left_high, left_low = halves(left)
    right_high, right_low = halves(right)
    return dot_nt(
        jnp.concatenate([left_high, left_high, left_low], 1),
        jnp.concatenate([right_high, right_low, right_high], 1),
    )


def factor_corner(work, chol, inverse):
    order = NB * BLK

    def one_panel(step, carry):
        first = pl.multiple_of(step * BLK, BLK)
        lower, lower_inverse = factor_block(work[step, pl.ds(first, BLK), :])
        chol[step, pl.ds(first, BLK), :] = lower
        inverse[step] = lower_inverse
        for j in range(NB - 1):

            @pl.when(step == j)
            def _():
                start = BLK * (j + 1)
                panel = dot_split(work[j, start:, :], inverse[j])
                chol[j, start:, :] = panel
                high, low = halves(panel)
                left = jnp.concatenate([high, high, low], 1)
                right = jnp.concatenate([high, low, high], 1)
                for k in range(j + 1, NB, 2):
                    wide = min(2, NB - k)
                    top = BLK * k - start
                    update = dot_nt(left[top:], right[top : top + wide * BLK])
                    for w in range(wide):
                        work[k + w, BLK * k :, :] = (
                            work[k + w, BLK * k :, :] - update[:, w * BLK : (w + 1) * BLK]
                        )

        return carry

    for j in range(1, NB):
        chol[j, : j * BLK, :] = jnp.zeros((j * BLK, BLK), F32)
    lax.fori_loop(0, NB, one_panel, 0)


def factor_corner_again(work, chol, inverse):
    def rows_of(block):
        return pl.ds(pl.multiple_of(block * BLK, BLK), BLK)

    def one_panel(step, carry):
        lower, lower_inverse = factor_block(work[step, rows_of(step), :])
        chol[step, rows_of(step), :] = lower
        inverse[step] = lower_inverse

        def one_block(i, carry):
            chol[step, rows_of(i), :] = dot_split(work[step, rows_of(i), :], inverse[step])
            return carry

        def one_col(k, carry):
            def one_row(i, carry):
                work[k, rows_of(i), :] = work[k, rows_of(i), :] - dot_split(
                    chol[step, rows_of(i), :], chol[step, rows_of(k), :]
                )
                return carry

            return lax.fori_loop(k, NB, one_row, carry)

        lax.fori_loop(step + 1, NB, one_block, 0)
        return lax.fori_loop(step + 1, NB, one_col, carry)

    chol[...] = jnp.zeros_like(chol)
    lax.fori_loop(0, NB, one_panel, 0)


def solve_rows(right_side, chol, inverse, solved, solved_high, solved_low):
    for p in range(0, NB, 2):
        value = right_side(p)
        if p:
            depth = range(p)
            left_high = jnp.concatenate([solved_high[k] for k in depth], 1)
            left_low = jnp.concatenate([solved_low[k] for k in depth], 1)
            right = jnp.concatenate([chol[k, p * BLK : (p + 2) * BLK, :] for k in depth], 1)
            right_high, right_low = halves(right)
            value = value - (
                dot_nt(left_high, right_high)
                + dot_nt(left_high, right_low)
                + dot_nt(left_low, right_high)
            )
        between = chol[p, (p + 1) * BLK : (p + 2) * BLK, :]
        corner = -dot_split(inverse[p + 1], dot_split(inverse[p].T, between))
        pair_inverse = jnp.concatenate(
            [
                jnp.concatenate([inverse[p], jnp.zeros((BLK, BLK), F32)], 1),
                jnp.concatenate([corner, inverse[p + 1]], 1),
            ],
            0,
        )
        value = dot_split(value, pair_inverse)
        high, low = halves(value)
        for w in range(2):
            lanes = slice(w * BLK, (w + 1) * BLK)
            solved[p + w] = value[:, lanes]
            solved_high[p + w], solved_low[p + w] = high[:, lanes], low[:, lanes]


def pair(ref, p):
    return jnp.concatenate([ref[p], ref[p + 1]], 1)


def place_of(block_map, front, child, slots):
    for m in range(FB):
        slots[child, m] = -1
    for i in range(NB):
        slots[child, block_map[front, child, i]] = i


def kept(pattern, front, row, col):
    return (pattern[front, row, col] == 1) | (pattern[front, col, row] == 1) | (row == col)


def first_turn(core, z):
    return jnp.where((core == 0) & (z >= 4), 1, 0)


def send_blocks(tile, core, z, out):
    base = NB // 2 * core
    for turn in range(2):
        local = (z + first_turn(core, z) + turn) % 4
        block = tile[local]
        at = turn * BLK

        @pl.when(base + local >= z)
        def _():
            out[at : at + BLK, :] = block

        @pl.when(base + local < z)
        def _():
            out[at : at + BLK, :] = block.T

    block = tile[(z + 2) % 4]

    @pl.when(z % 4 < 2)
    def _():
        out[2 * BLK :, :] = block[:HALF, :]

    @pl.when(z % 4 >= 2)
    def _():
        out[2 * BLK :, :] = block.T[HALF:, :]


def static_blocks():
    where = {}
    for core in range(2):
        for z in range(NB):
            turn0 = 1 if core == 0 and z >= 4 else 0
            for turn in range(2):
                row = 4 * core + (z + turn0 + turn) % 4
                where[max(row, z), min(row, z)] = [(core * NB + z, turn * BLK, BLK)]
            if z // 4 == core:
                row = 4 * core + (z + 2) % 4
                key = (max(row, z), min(row, z))
                entry = (core * NB + z, 2 * BLK, HALF)
                known = where.setdefault(key, [])
                if z % 4 < 2:
                    known.insert(0, entry)
                else:
                    known.append(entry)
    return where


def send_child(child, z, out):
    for turn in range(4):
        row = (z + turn) % NB
        at = turn * BLK
        block = child[pl.ds(pl.multiple_of(row * BLK, BLK), BLK), :]

        @pl.when(row >= z)
        def _():
            out[at : at + BLK, :] = block

        @pl.when(row < z)
        def _():
            out[at : at + BLK, :] = block.T

    row = (z + 4) % NB
    block = child[pl.ds(pl.multiple_of(row * BLK, BLK), BLK), :]

    @pl.when(row > z)
    def _():
        out[4 * BLK :, :] = block[:HALF, :]

    @pl.when(row < z)
    def _():
        out[4 * BLK :, :] = block.T[HALF:, :]


def child_copies(gathered, children, sems):
    return [
        pltpu.make_async_copy(
            gathered.at[:, :CHILD_ROWS, :], children.at[:, :CHILD_ROWS, :], sems.at[0]
        )
    ] + [
        pltpu.make_async_copy(
            gathered.at[child * NB + 4 : child * NB + 8, 4 * BLK : CHILD_ROWS, :],
            children.at[child * NB : child * NB + 4, CHILD_ROWS:, :],
            sems.at[1 + child],
        )
        for child in range(2)
    ]


def each_gathered(block_map, front, children, visit):
    def one(n, carry):
        child, m = n // 36, n % 36
        z = jnp.where(m < 32, m // 4, m - 32)
        turn = jnp.where(m < 32, m % 4, 4)
        other = (z + turn) % NB
        row = block_map[front, child, jnp.maximum(z, other)]
        col = block_map[front, child, jnp.minimum(z, other)]
        start = pl.multiple_of(turn * BLK, BLK)
        visit(row, col, lambda: children[child * NB + z, pl.ds(start, BLK), :])
        return carry

    lax.fori_loop(0, 72, one, 0)


def ordered(block_map, front, child, order, place):
    count = jnp.int32(0)
    for parity in range(2):
        for i in range(NB):
            hit = block_map[front, child, i] % 2 == parity

            @pl.when(hit)
            def _(count=count, i=i):
                order[child, count] = i
                place[child, i] = count

            count = count + jnp.where(hit, 1, 0)
        if parity == 0:
            separators = count
    return separators


def number_of(a, b):
    return a * (a + 1) // 2 + b


def block_number(place, child, i, k):
    a, b = place[child, i], place[child, k]
    return number_of(jnp.maximum(a, b), jnp.minimum(a, b))


def add_ordered_separators(block_map, front, children, work, order, counts):
    for child in range(2):

        def one_place(a, carry):
            def other_place(b, carry):
                i, k = order[child, a], order[child, b]
                row = block_map[front, child, jnp.maximum(i, k)] // 2
                col = block_map[front, child, jnp.minimum(i, k)] // 2
                number = number_of(a, b)

                @pl.when(row >= col)
                def _():
                    add_at(work, col, row, children[child, number])

                @pl.when(row < col)
                def _():
                    add_at(work, row, col, children[child, number].T)

                return carry

            return lax.fori_loop(0, a + 1, other_place, carry)

        lax.fori_loop(0, counts[child], one_place, 0)


def add_at(ref, lead, block_row, block):
    place = pl.ds(pl.multiple_of(block_row * BLK, BLK), BLK)
    ref[lead, place, :] = ref[lead, place, :] + block


def contributions_into(corner, lower, trail):
    def visit(row, col, block):
        row_odd, col_odd = row % 2 == 1, col % 2 == 1
        row_half, col_half = row // 2, col // 2

        @pl.when(~row_odd & ~col_odd & (row >= col))
        def _():
            add_at(corner, col_half, row_half, block())

        @pl.when(~row_odd & ~col_odd & (row < col))
        def _():
            add_at(corner, row_half, col_half, block().T)

        @pl.when(row_odd & ~col_odd)
        def _():
            add_at(lower, col_half, row_half, block())

        @pl.when(~row_odd & col_odd)
        def _():
            add_at(lower, row_half, col_half, block().T)

        @pl.when(row_odd & col_odd & (row >= col))
        def _():
            add_at(trail, packed_index(row_half, col_half), 0, block())

        @pl.when(row_odd & col_odd & (row < col))
        def _():
            add_at(trail, packed_index(col_half, row_half), 0, block().T)

    return visit


def masked_tile(initial, pattern, front, row, local, col):
    keep = kept(pattern, front, row, col)
    return jnp.where(keep, initial[local * BLK : (local + 1) * BLK, :], 0.0)


def pack_kernel(ids, pattern_one, child_in, initial, sent, child, corner, trail, sems):
    front_one, side, z = ids[0], ids[1], ids[2]
    copies = [pltpu.make_async_copy(child_in, child, sems.at[NB])]
    for r in range(NB):
        w = r % 2
        source = initial.at[r * BLK : (r + 1) * BLK, w * BLK : (w + 1) * BLK]
        target = (trail if w else corner).at[r // 2]
        copies.append(pltpu.make_async_copy(source, target, sems.at[r]))
    for copy in copies:
        copy.start()
    copies[0].wait()
    send_child(child, z, sent.at[:CHILD_ROWS, :])
    for copy in copies[1:]:
        copy.wait()
    for r in range(NB):
        tile = trail if r % 2 else corner
        keep = kept(pattern_one, front_one, NB * side + r, 2 * z + r % 2)
        tile[r // 2] = jnp.where(keep, tile[r // 2], 0.0)
    send_blocks(corner, side, z, sent.at[CHILD_ROWS : CHILD_ROWS + CORNER_ROWS, :])
    send_blocks(trail, side, z, sent.at[CHILD_ROWS + CORNER_ROWS :, :])


def mask_kernel(
    ids,
    pattern_one,
    pattern_two,
    initial_one,
    initial_two,
    merged,
    corner_two,
    lower_two,
    row_two,
    tail_two,
):
    front_one, side, z, front_two, sub = ids[0], ids[1], ids[2], ids[3], ids[4]
    first = initial_one.at[:, :BLK]
    for r in range(4):
        row = NB * side + 2 * r + 1
        merged[r * BLK : (r + 1) * BLK, :] = masked_tile(
            first, pattern_one, front_one, row, 2 * r + 1, 2 * z
        )
    for r in range(4):
        for w in range(2):
            columns = initial_two.at[:, w * BLK : (w + 1) * BLK]
            block = masked_tile(columns, pattern_two, front_two, 4 * sub + r, r, 2 * z + w)
            at = slice(r // 2 * BLK, (r // 2 + 1) * BLK)
            if w == 0:
                (corner_two if r % 2 == 0 else lower_two)[at, :] = block
            elif r % 2 == 0:
                row_two[at, :] = block.T
            else:
                tail_two[r // 2] = block


def chol_kernel(
    ids,
    block_map,
    gathered,
    chol,
    inverse,
    lower_out,
    trail_out,
    work,
    children,
    lower,
    trail,
    sems,
):
    front = ids[0]
    copies = child_copies(gathered, children, sems)
    for (row, col), parts in static_blocks().items():
        start = 0
        for piece, at, rows in parts:
            for base, target in (
                (CHILD_ROWS, work.at[col, row * BLK + start : row * BLK + start + rows, :]),
                (
                    CHILD_ROWS + CORNER_ROWS,
                    trail.at[packed_index(row, col), start : start + rows, :],
                ),
            ):
                source = gathered.at[piece, base + at : base + at + rows, :]
                copies.append(pltpu.make_async_copy(source, target, sems.at[len(copies)]))
            start += rows
    for copy in copies:
        copy.start()
    lower[...] = jnp.zeros_like(lower)
    for copy in copies:
        copy.wait()
    each_gathered(block_map, front, children, contributions_into(work, lower, trail))
    outs = [
        pltpu.make_async_copy(lower, lower_out, sems.at[0]),
        pltpu.make_async_copy(trail, trail_out, sems.at[1]),
    ]
    for copy in outs:
        copy.start()
    factor_corner(work, chol, inverse)
    for copy in outs:
        copy.wait()


def rest_kernel(
    ids,
    block_map,
    chol_in,
    inverse_in,
    lower_in,
    trail_in,
    merged,
    factor,
    mine,
    other,
    late,
    chol,
    inverse,
    lower,
    lower_add,
    solved,
    solved_high,
    solved_low,
    trail,
    staged,
    order,
    place,
    sems,
):
    side, z, child = ids[1], ids[2], ids[4] // 2
    half = NB // 2 * BLK
    used = []

    def fetch(source, target):
        copy = pltpu.make_async_copy(source, target, sems.at[len(used)])
        copy.start()
        used.append(copy)
        return copy

    first = [fetch(inverse_in, inverse)]
    columns = {}
    for p in range(0, NB, 2):
        columns[p] = [fetch(lower_in.at[p : p + 2], lower_add.at[p : p + 2])]
        for core in range(2):
            columns[p].append(
                fetch(
                    merged.at[core * NB + p : core * NB + p + 2],
                    lower.at[p : p + 2, core * half : (core + 1) * half, :],
                )
            )
        if p == 0:
            first.append(fetch(chol_in, chol))
    last = fetch(trail_in, trail)
    ordered(block_map, ids[3], child, order, place)
    for copy in first:
        copy.wait()

    def right_side(p):
        for copy in columns[p]:
            copy.wait()
        return pair(lower, p) + pair(lower_add, p)

    solve_rows(right_side, chol, inverse, solved, solved_high, solved_low)
    last.wait()
    for p in range(0, NB, 2):
        high = jnp.concatenate([solved_high[k, p * BLK :, :] for k in range(NB)], 1)
        low = jnp.concatenate([solved_low[k, p * BLK :, :] for k in range(NB)], 1)
        wide_high, wide_low = high[: 2 * BLK], low[: 2 * BLK]
        update = dot_nt(high, wide_high) + dot_nt(high, wide_low) + dot_nt(low, wide_high)
        for w in range(2):
            for i in range(p + w, NB):
                index = packed_index(i, p + w)
                number = block_number(place, child, i, p + w)
                half_id = jnp.where(number < SOON // 2, 0, 1)
                soon = (half_id + side) % 2 * (SOON // 2) + number - half_id * (SOON // 2)
                staged[jnp.where(number < SOON, soon, number)] = (
                    trail[index]
                    - update[(i - p) * BLK : (i - p + 1) * BLK, w * BLK : (w + 1) * BLK]
                )
    outs = [
        pltpu.make_async_copy(staged.at[: SOON // 2], mine, sems.at[0]),
        pltpu.make_async_copy(staged.at[SOON // 2 : SOON], other, sems.at[1]),
        pltpu.make_async_copy(staged.at[SOON:], late, sems.at[2]),
    ]
    for copy in outs:
        copy.start()
    for r in range(NB):
        source = solved if r % 2 else chol
        start = pl.multiple_of((side * (NB // 2) + r // 2) * BLK, BLK)
        factor[r * BLK : (r + 1) * BLK, :] = source[z, pl.ds(start, BLK), :]
    for copy in outs:
        copy.wait()


def fetch_children(side, mine, refs, children, sems):
    near_mine, near_other, far_mine, far_other = refs
    half = SOON // 2
    copies = []
    for n, (ref, child, half_id) in enumerate(
        (
            (near_mine, mine, side),
            (near_other, mine, 1 - side),
            (far_mine, 1 - mine, side),
            (far_other, 1 - mine, 1 - side),
        )
    ):
        target = children.at[child, pl.ds(half * half_id, half)]
        copies.append(pltpu.make_async_copy(ref, target, sems.at[n]))
        copies[-1].start()
    return copies


def corner_copies(side_of, gathered, work, sems):
    copies = []
    for core in range(2):
        for n, y in ((0, side_of), (1, 1 - side_of)):
            start = pl.multiple_of(2 * (2 * y + core) * BLK, BLK)
            copies.append(
                pltpu.make_async_copy(
                    gathered.at[core * NB : (core + 1) * NB, 2 * n * BLK : 2 * (n + 1) * BLK, :],
                    work.at[:, pl.ds(start, 2 * BLK), :],
                    sems.at[2 * core + n],
                )
            )
            copies[-1].start()
    return copies


def chol_two_kernel(
    ids,
    block_map,
    gathered,
    near_mine,
    near_other,
    far_mine,
    far_other,
    chol,
    inverse,
    work,
    children,
    order,
    place,
    sems,
    corner_sems,
):
    side, front, sub = ids[1], ids[3], ids[4]
    copies = fetch_children(
        side, sub // 2, (near_mine, near_other, far_mine, far_other), children, sems
    )
    copies += corner_copies(sub // 2, gathered, work, corner_sems)
    counts = [
        jnp.minimum(ordered(block_map, front, child, order, place), MOST) for child in range(2)
    ]
    for copy in copies:
        copy.wait()
    add_ordered_separators(block_map, front, children, work, order, counts)
    factor_corner(work, chol, inverse)


def tail_kernel(
    ids,
    map_two,
    gathered,
    chol_in,
    inverse_in,
    rows_all,
    tail,
    near_mine,
    near_other,
    far_mine,
    far_other,
    near_late,
    far_late,
    factor,
    schur,
    chol,
    inverse,
    work,
    children,
    lower,
    solved,
    solved_high,
    solved_low,
    trail,
    slots,
    order,
    place,
    sems,
    corner_sems,
):
    side, z, front, sub = ids[1], ids[2], ids[3], ids[4]
    mine = sub // 2
    copies = fetch_children(
        side, mine, (near_mine, near_other, far_mine, far_other), children, sems
    )
    for n, (ref, child) in enumerate(((near_late, mine), (far_late, 1 - mine))):
        copies.append(
            pltpu.make_async_copy(ref, children.at[child, pl.ds(SOON, LATE)], sems.at[4 + n])
        )
        copies[-1].start()
    copies.append(
        pltpu.make_async_copy(
            gathered.at[pl.ds(side * NB, NB), 4 * BLK :, :],
            lower.at[:, : 2 * BLK, :],
            sems.at[8],
        )
    )
    copies[-1].start()
    factors = [
        pltpu.make_async_copy(chol_in, chol, sems.at[6]),
        pltpu.make_async_copy(inverse_in, inverse, sems.at[7]),
    ]
    for copy in factors:
        copy.start()
    counts = [ordered(map_two, front, child, order, place) for child in range(2)]
    place_of(map_two, front, 0, slots)
    place_of(map_two, front, 1, slots)
    for s in range(4):
        for b in range(2):
            lower[2 * s + b, 2 * BLK :, :] = rows_all[s, b * BLK : (b + 1) * BLK, :]
    trail[...] = tail[...]
    for copy in copies:
        copy.wait()
    wanted = (2 * sub, 2 * sub + 1, z)

    def one_child(child, carry):
        for slot, target in enumerate(wanted):
            i = slots[child, 2 * target + 1]

            def one_block(k, carry):
                col = map_two[front, child, k]
                index = block_number(place, child, i, k)

                @pl.when((col % 2 == 0) & (i > k))
                def _():
                    add_at(lower, col // 2, slot, children[child, index])

                @pl.when((col % 2 == 0) & (i < k))
                def _():
                    add_at(lower, col // 2, slot, children[child, index].T)

                return carry

            lax.fori_loop(0, jnp.where(i >= 0, NB, 0), one_block, 0)
        k = slots[child, 2 * z + 1]
        for slot in range(2):
            i = slots[child, 2 * wanted[slot] + 1]
            both = (i >= 0) & (k >= 0)
            index = block_number(place, child, jnp.maximum(i, 0), jnp.maximum(k, 0))

            @pl.when(both & (i >= k))
            def _():
                trail[slot] = trail[slot] + children[child, index]

            @pl.when(both & (i < k))
            def _():
                trail[slot] = trail[slot] + children[child, index].T

        return carry

    lax.fori_loop(0, 2, one_child, 0)
    for copy in factors:
        copy.wait()

    @pl.when(jnp.maximum(counts[0], counts[1]) > MOST)
    def _():
        for copy in corner_copies(mine, gathered, work, corner_sems):
            copy.wait()
        add_ordered_separators(map_two, front, children, work, order, counts)
        factor_corner_again(work, chol, inverse)

    solve_rows(lambda p: pair(lower, p), chol, inverse, solved, solved_high, solved_low)
    high = jnp.concatenate([solved_high[k] for k in range(NB)], 1)
    low = jnp.concatenate([solved_low[k] for k in range(NB)], 1)
    left_high, left_low = high[: 2 * BLK], low[: 2 * BLK]
    right_high, right_low = high[2 * BLK :], low[2 * BLK :]
    update = (
        dot_nt(left_high, right_high)
        + dot_nt(left_high, right_low)
        + dot_nt(left_low, right_high)
    )
    for r in range(2):
        schur[r * BLK : (r + 1) * BLK, :] = trail[r] - update[r * BLK : (r + 1) * BLK, :]
        start = pl.multiple_of((2 * sub + r) * BLK, BLK)
        factor[2 * r * BLK : (2 * r + 1) * BLK, :] = chol[z, pl.ds(start, BLK), :]
        factor[(2 * r + 1) * BLK : (2 * r + 2) * BLK, :] = solved[z, r * BLK : (r + 1) * BLK, :]


def call(kernel, name, outs, specs, args, scratch=(), flops=0, out_specs=None):
    return pl.pallas_call(
        kernel,
        name=name,
        out_shape=outs,
        in_specs=specs,
        out_specs=out_specs or [VMEM] * len(outs),
        scratch_shapes=list(scratch),
        compiler_params=PARAMS,
        cost_estimate=pl.CostEstimate(flops=flops, bytes_accessed=flops // 400, transcendentals=0)
        if flops
        else None,
    )(*args)


def swap(value, axis):
    return lax.ppermute(value, axis, [(0, 1), (1, 0)])


def per_device(
    child_updates,
    initial_one,
    initial_two,
    pattern_one,
    pattern_two,
    parent_map_one,
    parent_map_two,
):
    x, yh, yl = lax.axis_index("x"), lax.axis_index("yh"), lax.axis_index("yl")
    core, z = lax.axis_index("core"), lax.axis_index("front")
    ids = jnp.stack([x * 4 + yh * 2 + yl, core, z, x * 2 + yh, yl * 2 + core]).astype(jnp.int32)
    panel = (NB, NB * BLK, BLK)
    block = (BLK, BLK)

    (sent,) = call(
        pack_kernel,
        "pack",
        [shape(CHILD_ROWS + 2 * CORNER_ROWS, BLK)],
        [SMEM, SMEM, ANY, ANY],
        (ids, pattern_one, child_updates, initial_one),
        [
            pltpu.VMEM((NB * BLK, BLK), F32),
            pltpu.VMEM((4, *block), F32),
            pltpu.VMEM((4, *block), F32),
            pltpu.SemaphoreType.DMA((NB + 1,)),
        ],
    )
    gathered = lax.all_gather(sent, ("core", "front"), axis=0, tiled=False)
    ids_mask, _ = lax.optimization_barrier((ids, sent))
    merged, corner_two, lower_two, row_two, tail_two = call(
        mask_kernel,
        "mask",
        [
            shape(LOWER_ROWS, BLK),
            shape(2 * BLK, BLK),
            shape(2 * BLK, BLK),
            shape(2 * BLK, BLK),
            shape(2, *block),
        ],
        [SMEM, SMEM, SMEM, VMEM, VMEM],
        (ids_mask, pattern_one, pattern_two, initial_one, initial_two),
    )
    corner_two = jnp.concatenate([corner_two, swap(corner_two, "yl"), lower_two], 0)
    rows_all = lax.all_gather(row_two, ("yl", "core"), axis=0, tiled=False)
    merged, gathered, corner_two, rows_all = lax.optimization_barrier(
        (merged, gathered, corner_two, rows_all)
    )
    merged_all = lax.all_gather(merged, ("core", "front"), axis=0, tiled=False)
    chol, inverse, lower_add, trail_add = call(
        chol_kernel,
        "chol",
        [shape(*panel), shape(NB, *block), shape(*panel), shape(36, *block)],
        [SMEM, SMEM, ANY],
        (ids, parent_map_one, gathered),
        [
            pltpu.VMEM(panel, F32),
            pltpu.VMEM((2 * NB, 5 * BLK, BLK), F32),
            pltpu.VMEM(panel, F32),
            pltpu.VMEM((36, *block), F32),
            pltpu.SemaphoreType.DMA((96,)),
        ],
        flops=40_000_000_000,
        out_specs=[VMEM, VMEM, ANY, ANY],
    )
    gathered_two = lax.all_gather(corner_two, ("core", "front"), axis=0, tiled=False)
    places = pltpu.SMEM((2, NB), jnp.int32)
    factor_one, near_mine, near_other, near_late = call(
        rest_kernel,
        "rest",
        [
            shape(NB * BLK, BLK),
            shape(SOON // 2, *block),
            shape(SOON // 2, *block),
            shape(LATE, *block),
        ],
        [SMEM, SMEM] + [ANY] * 5,
        (ids, parent_map_two, chol, inverse, lower_add, trail_add, merged_all),
        [pltpu.VMEM(panel, F32), pltpu.VMEM((NB, *block), F32)]
        + [pltpu.VMEM(panel, F32)] * 3
        + [pltpu.VMEM(panel, BF16)] * 2
        + [pltpu.VMEM((36, *block), F32)] * 2
        + [places, places, pltpu.SemaphoreType.DMA((64,))],
        flops=15_000_000_000,
        out_specs=[VMEM, ANY, ANY, ANY],
    )
    far_mine = swap(near_mine, "yl")
    far_other = swap(far_mine, "core")
    packed = (near_mine, near_other, far_mine, far_other)
    given_late, _ = lax.optimization_barrier((near_late, far_mine))
    far_late = swap(given_late, "yl")
    children = pltpu.VMEM((2, 36, *block), F32)
    chol, inverse = call(
        chol_two_kernel,
        "chol_two",
        [shape(*panel), shape(NB, *block)],
        [SMEM, SMEM] + [ANY] * 5,
        (ids, parent_map_two, gathered_two, *packed),
        [
            pltpu.VMEM(panel, F32),
            children,
            places,
            places,
            pltpu.SemaphoreType.DMA((4,)),
            pltpu.SemaphoreType.DMA((4,)),
        ],
        flops=40_000_000_000,
    )
    rows = (NB, 3 * BLK, BLK)
    factor_two, schur_two = call(
        tail_kernel,
        "tail",
        [shape(4 * BLK, BLK), shape(2 * BLK, BLK)],
        [SMEM, SMEM, ANY, ANY, ANY] + [VMEM] * 2 + [ANY] * 6,
        (
            ids,
            parent_map_two,
            gathered_two,
            chol,
            inverse,
            rows_all,
            tail_two,
            *packed,
            near_late,
            far_late,
        ),
        [
            pltpu.VMEM(panel, F32),
            pltpu.VMEM((NB, *block), F32),
            pltpu.VMEM(panel, F32),
            children,
            pltpu.VMEM(rows, F32),
            pltpu.VMEM(rows, F32),
            pltpu.VMEM(rows, BF16),
            pltpu.VMEM(rows, BF16),
            pltpu.VMEM((2, *block), F32),
            pltpu.SMEM((2, FB), jnp.int32),
            places,
            places,
            pltpu.SemaphoreType.DMA((9,)),
            pltpu.SemaphoreType.DMA((4,)),
        ],
    )
    return factor_one, factor_two, schur_two


def solution(mesh):
    cut = Mesh(mesh.devices.reshape(4, 2, 2, 2, 8), LEAF + ("front",))
    tile = P(LEAF, "front")
    return jax.shard_map(
        per_device,
        mesh=cut,
        in_specs=(tile, tile, tile, P(), P(), P(), P()),
        out_specs=(tile, tile, tile),
        check_vma=False,
    )
```

```python
import jax
import jax.numpy as jnp
from jax import lax
from jax.experimental import pallas as pl
from jax.experimental.pallas import tpu as pltpu
from jax.sharding import Mesh, PartitionSpec as P

BLK = 128
NB = 8
FB = 16
F32 = jnp.float32
BF16 = jnp.bfloat16
VMEM = pl.BlockSpec(memory_space=pltpu.VMEM)
SMEM = pl.BlockSpec(memory_space=pltpu.SMEM)
ANY = pl.BlockSpec(memory_space=pl.ANY)
HALF = BLK // 2
CORNER_ROWS = 2 * BLK + HALF
CHILD_ROWS = 4 * BLK + HALF
LOWER_ROWS = 4 * BLK
PARAMS = pltpu.CompilerParams(vmem_limit_bytes=58 * 1024 * 1024)
LEAF = ("x", "yh", "yl", "core")
MOST = 6
SOON = 22
LATE = 36 - SOON


def shape(*dims):
    return jax.ShapeDtypeStruct(dims, F32)


def packed_index(row, col):
    return col * NB - col * (col - 1) // 2 + row - col


def across(piece):
    return jnp.broadcast_to(piece, (8, BLK))


def lane_columns(rows, t):
    return [across(rows[:, 8 * t + b : 8 * t + b + 1]) for b in range(8)]


def factor_eights(rows, first, last):
    sub = lax.broadcasted_iota(jnp.int32, (8, BLK), 0)
    lane = lax.broadcasted_iota(jnp.int32, (8, BLK), 1)
    diag = jnp.zeros((8, BLK), F32)
    outs = []
    following = lane_columns(rows[first], first)
    for t in range(first, last):
        head = following
        below = {g: lane_columns(rows[g], t) for g in range(t + 1, last)}
        if t + 1 < last:
            following = lane_columns(rows[t + 1], t + 1)
        scale, weight = [], {}
        ahead = across(head[0][0:1])
        for b in range(8):
            pivot = ahead
            scale.append(lax.rsqrt(pivot))
            diag = jnp.where(lane == 8 * t + b, pivot * scale[b], diag)
            low = head[b] * scale[b]
            for a in range(b + 1, 8):
                weight[a, b] = across(head[b][a : a + 1]) * scale[b]
                if a == b + 1:
                    ahead = across(head[a][a : a + 1]) - weight[a, b] * weight[a, b]
                head[a] = head[a] - low * weight[a, b]
        inside = (lane >= 8 * t) & (lane < 8 * t + 8)
        pivots = []
        for b in range(8):
            unit = jnp.where(lane == 8 * t + b, 1.0, 0.0)
            row = jnp.where(inside, unit, across(rows[t][b : b + 1]))
            for a in range(b):
                row = row - weight[b, a] * pivots[a]
            pivots.append(row * scale[b])
        for g in range(t + 1, last):
            lows = []
            for b in range(8):
                column = below[g][b]
                for a in range(b):
                    column = column - lows[a] * weight[b, a]
                lows.append(column * scale[b])
            if g == t + 1:
                for b in range(8):
                    for a in range(8):
                        following[a] = following[a] - lows[b] * across(lows[b][a : a + 1])
            group = jnp.where(inside, 0.0, rows[g])
            for b in range(8):
                group = group - lows[b] * pivots[b]
            rows[g] = group
        group = pivots[7]
        for b in range(6, -1, -1):
            group = jnp.where(sub == b, pivots[b], group)
        rows[t] = group
        for a in range(1, 8):
            column = weight[a, a - 1]
            for b in range(a - 2, -1, -1):
                column = jnp.where(sub == b, weight[a, b], column)
            group = jnp.where((lane == 8 * t + a) & (sub < a), column, group)
        outs.append(group)
    return outs, diag


def factor_block(block):
    rows = [block[8 * g : 8 * g + 8] for g in range(16)]
    outs, diag = factor_eights(rows, 0, 8)
    lane = lax.broadcasted_iota(jnp.int32, (8, BLK), 1)
    row_id = lax.broadcasted_iota(jnp.int32, (BLK // 2, BLK), 0)
    col_id = lax.broadcasted_iota(jnp.int32, (BLK // 2, BLK), 1)
    left = jnp.concatenate(rows[:8], 0)
    right = jnp.where((col_id > row_id) & (col_id < BLK // 2), 0.0, left)
    left_high, left_low = halves(left)
    right_high, right_low = halves(right)
    update = lax.dot_general(
        jnp.concatenate([left_high, left_high, left_low], 0),
        jnp.concatenate([right_high, right_low, right_high], 0),
        (((0,), (0,)), ((), ())),
        preferred_element_type=F32,
    )
    for g in range(8, 16):
        rows[g] = jnp.where(lane < BLK // 2, 0.0, rows[g]) - update[8 * g : 8 * g + 8]
    more, more_diag = factor_eights(rows, 8, 16)
    full = jnp.concatenate(outs + more, 0)
    row_id = lax.broadcasted_iota(jnp.int32, (BLK, BLK), 0)
    col_id = lax.broadcasted_iota(jnp.int32, (BLK, BLK), 1)
    on_diag = jnp.broadcast_to((diag + more_diag)[0:1], (BLK, BLK))
    upper = jnp.where(col_id > row_id, full, jnp.where(col_id == row_id, on_diag, 0.0))
    return upper.T, jnp.where(col_id <= row_id, full, 0.0)


def halves(value):
    high = value.astype(BF16)
    return high, (value - high.astype(F32)).astype(BF16)


def dot_nt(left, right):
    return lax.dot_general(
        left, right, (((1,), (1,)), ((), ())), preferred_element_type=F32
    )


def dot_split(left, right):
    left_high, left_low = halves(left)
    right_high, right_low = halves(right)
    return dot_nt(
        jnp.concatenate([left_high, left_high, left_low], 1),
        jnp.concatenate([right_high, right_low, right_high], 1),
    )


def factor_corner(work, chol, inverse):
    order = NB * BLK

    def one_panel(step, carry):
        first = pl.multiple_of(step * BLK, BLK)
        lower, lower_inverse = factor_block(work[step, pl.ds(first, BLK), :])
        chol[step, pl.ds(first, BLK), :] = lower
        inverse[step] = lower_inverse
        for j in range(NB - 1):

            @pl.when(step == j)
            def _():
                start = BLK * (j + 1)
                panel = dot_split(work[j, start:, :], inverse[j])
                chol[j, start:, :] = panel
                high, low = halves(panel)
                left = jnp.concatenate([high, high, low], 1)
                right = jnp.concatenate([high, low, high], 1)
                for k in range(j + 1, NB, 2):
                    wide = min(2, NB - k)
                    top = BLK * k - start
                    update = dot_nt(left[top:], right[top : top + wide * BLK])
                    for w in range(wide):
                        work[k + w, BLK * k :, :] = (
                            work[k + w, BLK * k :, :] - update[:, w * BLK : (w + 1) * BLK]
                        )

        return carry

    for j in range(1, NB):
        chol[j, : j * BLK, :] = jnp.zeros((j * BLK, BLK), F32)
    lax.fori_loop(0, NB, one_panel, 0)


def factor_corner_again(work, chol, inverse):
    def rows_of(block):
        return pl.ds(pl.multiple_of(block * BLK, BLK), BLK)

    def one_panel(step, carry):
        lower, lower_inverse = factor_block(work[step, rows_of(step), :])
        chol[step, rows_of(step), :] = lower
        inverse[step] = lower_inverse

        def one_block(i, carry):
            chol[step, rows_of(i), :] = dot_split(work[step, rows_of(i), :], inverse[step])
            return carry

        def one_col(k, carry):
            def one_row(i, carry):
                work[k, rows_of(i), :] = work[k, rows_of(i), :] - dot_split(
                    chol[step, rows_of(i), :], chol[step, rows_of(k), :]
                )
                return carry

            return lax.fori_loop(k, NB, one_row, carry)

        lax.fori_loop(step + 1, NB, one_block, 0)
        return lax.fori_loop(step + 1, NB, one_col, carry)

    chol[...] = jnp.zeros_like(chol)
    lax.fori_loop(0, NB, one_panel, 0)


def solve_rows(right_side, chol, inverse, solved, solved_high, solved_low):
    for p in range(0, NB, 2):
        value = right_side(p)
        if p:
            depth = range(p)
            left_high = jnp.concatenate([solved_high[k] for k in depth], 1)
            left_low = jnp.concatenate([solved_low[k] for k in depth], 1)
            right = jnp.concatenate([chol[k, p * BLK : (p + 2) * BLK, :] for k in depth], 1)
            right_high, right_low = halves(right)
            value = value - (
                dot_nt(left_high, right_high)
                + dot_nt(left_high, right_low)
                + dot_nt(left_low, right_high)
            )
        between = chol[p, (p + 1) * BLK : (p + 2) * BLK, :]
        corner = -dot_split(inverse[p + 1], dot_split(inverse[p].T, between))
        pair_inverse = jnp.concatenate(
            [
                jnp.concatenate([inverse[p], jnp.zeros((BLK, BLK), F32)], 1),
                jnp.concatenate([corner, inverse[p + 1]], 1),
            ],
            0,
        )
        value = dot_split(value, pair_inverse)
        high, low = halves(value)
        for w in range(2):
            lanes = slice(w * BLK, (w + 1) * BLK)
            solved[p + w] = value[:, lanes]
            solved_high[p + w], solved_low[p + w] = high[:, lanes], low[:, lanes]


def pair(ref, p):
    return jnp.concatenate([ref[p], ref[p + 1]], 1)


def place_of(block_map, front, child, slots):
    for m in range(FB):
        slots[child, m] = -1
    for i in range(NB):
        slots[child, block_map[front, child, i]] = i


def kept(pattern, front, row, col):
    return (pattern[front, row, col] == 1) | (pattern[front, col, row] == 1) | (row == col)


def first_turn(core, z):
    return jnp.where((core == 0) & (z >= 4), 1, 0)


def send_blocks(tile, core, z, out):
    base = NB // 2 * core
    for turn in range(2):
        local = (z + first_turn(core, z) + turn) % 4
        block = tile[local]
        at = turn * BLK

        @pl.when(base + local >= z)
        def _():
            out[at : at + BLK, :] = block

        @pl.when(base + local < z)
        def _():
            out[at : at + BLK, :] = block.T

    block = tile[(z + 2) % 4]

    @pl.when(z % 4 < 2)
    def _():
        out[2 * BLK :, :] = block[:HALF, :]

    @pl.when(z % 4 >= 2)
    def _():
        out[2 * BLK :, :] = block.T[HALF:, :]


def static_blocks():
    where = {}
    for core in range(2):
        for z in range(NB):
            turn0 = 1 if core == 0 and z >= 4 else 0
            for turn in range(2):
                row = 4 * core + (z + turn0 + turn) % 4
                where[max(row, z), min(row, z)] = [(core * NB + z, turn * BLK, BLK)]
            if z // 4 == core:
                row = 4 * core + (z + 2) % 4
                key = (max(row, z), min(row, z))
                entry = (core * NB + z, 2 * BLK, HALF)
                known = where.setdefault(key, [])
                if z % 4 < 2:
                    known.insert(0, entry)
                else:
                    known.append(entry)
    return where


def send_child(child, z, out):
    for turn in range(4):
        row = (z + turn) % NB
        at = turn * BLK
        block = child[pl.ds(pl.multiple_of(row * BLK, BLK), BLK), :]

        @pl.when(row >= z)
        def _():
            out[at : at + BLK, :] = block

        @pl.when(row < z)
        def _():
            out[at : at + BLK, :] = block.T

    row = (z + 4) % NB
    block = child[pl.ds(pl.multiple_of(row * BLK, BLK), BLK), :]

    @pl.when(row > z)
    def _():
        out[4 * BLK :, :] = block[:HALF, :]

    @pl.when(row < z)
    def _():
        out[4 * BLK :, :] = block.T[HALF:, :]


def child_copies(gathered, children, sems):
    return [
        pltpu.make_async_copy(
            gathered.at[:, :CHILD_ROWS, :], children.at[:, :CHILD_ROWS, :], sems.at[0]
        )
    ] + [
        pltpu.make_async_copy(
            gathered.at[child * NB + 4 : child * NB + 8, 4 * BLK : CHILD_ROWS, :],
            children.at[child * NB : child * NB + 4, CHILD_ROWS:, :],
            sems.at[1 + child],
        )
        for child in range(2)
    ]


def each_gathered(block_map, front, children, visit):
    def one(n, carry):
        child, m = n // 36, n % 36
        z = jnp.where(m < 32, m // 4, m - 32)
        turn = jnp.where(m < 32, m % 4, 4)
        other = (z + turn) % NB
        row = block_map[front, child, jnp.maximum(z, other)]
        col = block_map[front, child, jnp.minimum(z, other)]
        start = pl.multiple_of(turn * BLK, BLK)
        visit(row, col, lambda: children[child * NB + z, pl.ds(start, BLK), :])
        return carry

    lax.fori_loop(0, 72, one, 0)


def ordered(block_map, front, child, order, place):
    count = jnp.int32(0)
    for parity in range(2):
        for i in range(NB):
            hit = block_map[front, child, i] % 2 == parity

            @pl.when(hit)
            def _(count=count, i=i):
                order[child, count] = i
                place[child, i] = count

            count = count + jnp.where(hit, 1, 0)
        if parity == 0:
            separators = count
    return separators


def number_of(a, b):
    return a * (a + 1) // 2 + b


def block_number(place, child, i, k):
    a, b = place[child, i], place[child, k]
    return number_of(jnp.maximum(a, b), jnp.minimum(a, b))


def add_ordered_separators(block_map, front, children, work, order, counts):
    for child in range(2):

        def one_place(a, carry):
            def other_place(b, carry):
                i, k = order[child, a], order[child, b]
                row = block_map[front, child, jnp.maximum(i, k)] // 2
                col = block_map[front, child, jnp.minimum(i, k)] // 2
                number = number_of(a, b)

                @pl.when(row >= col)
                def _():
                    add_at(work, col, row, children[child, number])

                @pl.when(row < col)
                def _():
                    add_at(work, row, col, children[child, number].T)

                return carry

            return lax.fori_loop(0, a + 1, other_place, carry)

        lax.fori_loop(0, counts[child], one_place, 0)


def add_at(ref, lead, block_row, block):
    place = pl.ds(pl.multiple_of(block_row * BLK, BLK), BLK)
    ref[lead, place, :] = ref[lead, place, :] + block


def contributions_into(corner, lower, trail):
    def visit(row, col, block):
        row_odd, col_odd = row % 2 == 1, col % 2 == 1
        row_half, col_half = row // 2, col // 2

        @pl.when(~row_odd & ~col_odd & (row >= col))
        def _():
            add_at(corner, col_half, row_half, block())

        @pl.when(~row_odd & ~col_odd & (row < col))
        def _():
            add_at(corner, row_half, col_half, block().T)

        @pl.when(row_odd & ~col_odd)
        def _():
            add_at(lower, col_half, row_half, block())

        @pl.when(~row_odd & col_odd)
        def _():
            add_at(lower, row_half, col_half, block().T)

        @pl.when(row_odd & col_odd & (row >= col))
        def _():
            add_at(trail, packed_index(row_half, col_half), 0, block())

        @pl.when(row_odd & col_odd & (row < col))
        def _():
            add_at(trail, packed_index(col_half, row_half), 0, block().T)

    return visit


def masked_tile(initial, pattern, front, row, local, col):
    keep = kept(pattern, front, row, col)
    return jnp.where(keep, initial[local * BLK : (local + 1) * BLK, :], 0.0)


def pack_kernel(ids, pattern_one, child_in, initial, sent, child, corner, sems):
    front_one, side, z = ids[0], ids[1], ids[2]
    copies = [pltpu.make_async_copy(child_in, child, sems.at[4])]
    for r in range(4):
        source = initial.at[2 * r * BLK : (2 * r + 1) * BLK, :BLK]
        copies.append(pltpu.make_async_copy(source, corner.at[r], sems.at[r]))
    for copy in copies:
        copy.start()
    copies[0].wait()
    send_child(child, z, sent.at[:CHILD_ROWS, :])
    for copy in copies[1:]:
        copy.wait()
    for r in range(4):
        keep = kept(pattern_one, front_one, NB * side + 2 * r, 2 * z)
        corner[r] = jnp.where(keep, corner[r], 0.0)
    send_blocks(corner, side, z, sent.at[CHILD_ROWS:, :])


def mask_kernel(
    ids,
    pattern_one,
    pattern_two,
    initial_one,
    initial_two,
    merged,
    corner_two,
    lower_two,
    row_two,
    tail_two,
    tile,
):
    front_one, side, z, front_two, sub = ids[0], ids[1], ids[2], ids[3], ids[4]
    first, second = initial_one.at[:, :BLK], initial_one.at[:, BLK:]
    for r in range(4):
        row = NB * side + 2 * r + 1
        merged[r * BLK : (r + 1) * BLK, :] = masked_tile(
            first, pattern_one, front_one, row, 2 * r + 1, 2 * z
        )
        tile[r] = masked_tile(second, pattern_one, front_one, row, 2 * r + 1, 2 * z + 1)
    send_blocks(tile, side, z, merged.at[LOWER_ROWS:, :])
    for r in range(4):
        for w in range(2):
            columns = initial_two.at[:, w * BLK : (w + 1) * BLK]
            block = masked_tile(columns, pattern_two, front_two, 4 * sub + r, r, 2 * z + w)
            at = slice(r // 2 * BLK, (r // 2 + 1) * BLK)
            if w == 0:
                (corner_two if r % 2 == 0 else lower_two)[at, :] = block
            elif r % 2 == 0:
                row_two[at, :] = block.T
            else:
                tail_two[r // 2] = block


def chol_kernel(
    ids,
    block_map,
    gathered,
    chol,
    inverse,
    lower_out,
    trail_out,
    work,
    children,
    lower,
    trail,
    sems,
):
    front = ids[0]
    copies = child_copies(gathered, children, sems)
    for (row, col), parts in static_blocks().items():
        start = row * BLK
        for piece, at, rows in parts:
            copies.append(
                pltpu.make_async_copy(
                    gathered.at[piece, CHILD_ROWS + at : CHILD_ROWS + at + rows, :],
                    work.at[col, start : start + rows, :],
                    sems.at[len(copies)],
                )
            )
            start += rows
    for copy in copies:
        copy.start()
    lower[...] = jnp.zeros_like(lower)
    trail[...] = jnp.zeros_like(trail)
    for copy in copies:
        copy.wait()
    each_gathered(block_map, front, children, contributions_into(work, lower, trail))
    outs = [
        pltpu.make_async_copy(lower, lower_out, sems.at[0]),
        pltpu.make_async_copy(trail, trail_out, sems.at[1]),
    ]
    for copy in outs:
        copy.start()
    factor_corner(work, chol, inverse)
    for copy in outs:
        copy.wait()


def rest_kernel(
    ids,
    block_map,
    chol_in,
    inverse_in,
    lower_in,
    trail_in,
    merged,
    factor,
    mine,
    other,
    late,
    chol,
    inverse,
    lower,
    lower_add,
    solved,
    solved_high,
    solved_low,
    trail,
    trail_add,
    staged,
    order,
    place,
    sems,
):
    side, z, child = ids[1], ids[2], ids[4] // 2
    half = NB // 2 * BLK
    used = []

    def fetch(source, target):
        copy = pltpu.make_async_copy(source, target, sems.at[len(used)])
        copy.start()
        used.append(copy)
        return copy

    first = [fetch(inverse_in, inverse)]
    columns = {}
    for p in range(0, NB, 2):
        columns[p] = [fetch(lower_in.at[p : p + 2], lower_add.at[p : p + 2])]
        for core in range(2):
            columns[p].append(
                fetch(
                    merged.at[core * NB + p : core * NB + p + 2, :LOWER_ROWS, :],
                    lower.at[p : p + 2, core * half : (core + 1) * half, :],
                )
            )
        if p == 0:
            first.append(fetch(chol_in, chol))
    last = [fetch(trail_in, trail_add)]
    for (row, col), parts in static_blocks().items():
        start = 0
        for piece, at, rows in parts:
            last.append(
                fetch(
                    merged.at[piece, LOWER_ROWS + at : LOWER_ROWS + at + rows, :],
                    trail.at[packed_index(row, col), start : start + rows, :],
                )
            )
            start += rows
    ordered(block_map, ids[3], child, order, place)
    for copy in first:
        copy.wait()

    def right_side(p):
        for copy in columns[p]:
            copy.wait()
        return pair(lower, p) + pair(lower_add, p)

    solve_rows(right_side, chol, inverse, solved, solved_high, solved_low)
    for copy in last:
        copy.wait()
    for p in range(0, NB, 2):
        high = jnp.concatenate([solved_high[k, p * BLK :, :] for k in range(NB)], 1)
        low = jnp.concatenate([solved_low[k, p * BLK :, :] for k in range(NB)], 1)
        wide_high, wide_low = high[: 2 * BLK], low[: 2 * BLK]
        update = dot_nt(high, wide_high) + dot_nt(high, wide_low) + dot_nt(low, wide_high)
        for w in range(2):
            for i in range(p + w, NB):
                index = packed_index(i, p + w)
                number = block_number(place, child, i, p + w)
                half_id = jnp.where(number < SOON // 2, 0, 1)
                soon = (half_id + side) % 2 * (SOON // 2) + number - half_id * (SOON // 2)
                staged[jnp.where(number < SOON, soon, number)] = (
                    trail[index]
                    + trail_add[index]
                    - update[(i - p) * BLK : (i - p + 1) * BLK, w * BLK : (w + 1) * BLK]
                )
    outs = [
        pltpu.make_async_copy(staged.at[: SOON // 2], mine, sems.at[0]),
        pltpu.make_async_copy(staged.at[SOON // 2 : SOON], other, sems.at[1]),
        pltpu.make_async_copy(staged.at[SOON:], late, sems.at[2]),
    ]
    for copy in outs:
        copy.start()
    for r in range(NB):
        source = solved if r % 2 else chol
        start = pl.multiple_of((side * (NB // 2) + r // 2) * BLK, BLK)
        factor[r * BLK : (r + 1) * BLK, :] = source[z, pl.ds(start, BLK), :]
    for copy in outs:
        copy.wait()


def fetch_children(side, mine, refs, children, sems):
    near_mine, near_other, far_mine, far_other = refs
    half = SOON // 2
    copies = []
    for n, (ref, child, half_id) in enumerate(
        (
            (near_mine, mine, side),
            (near_other, mine, 1 - side),
            (far_mine, 1 - mine, side),
            (far_other, 1 - mine, 1 - side),
        )
    ):
        target = children.at[child, pl.ds(half * half_id, half)]
        copies.append(pltpu.make_async_copy(ref, target, sems.at[n]))
        copies[-1].start()
    return copies


def corner_copies(side_of, gathered, work, sems):
    copies = []
    for core in range(2):
        for n, y in ((0, side_of), (1, 1 - side_of)):
            start = pl.multiple_of(2 * (2 * y + core) * BLK, BLK)
            copies.append(
                pltpu.make_async_copy(
                    gathered.at[core * NB : (core + 1) * NB, 2 * n * BLK : 2 * (n + 1) * BLK, :],
                    work.at[:, pl.ds(start, 2 * BLK), :],
                    sems.at[2 * core + n],
                )
            )
            copies[-1].start()
    return copies


def chol_two_kernel(
    ids,
    block_map,
    gathered,
    near_mine,
    near_other,
    far_mine,
    far_other,
    chol,
    inverse,
    work,
    children,
    order,
    place,
    sems,
    corner_sems,
):
    side, front, sub = ids[1], ids[3], ids[4]
    copies = fetch_children(
        side, sub // 2, (near_mine, near_other, far_mine, far_other), children, sems
    )
    copies += corner_copies(sub // 2, gathered, work, corner_sems)
    counts = [
        jnp.minimum(ordered(block_map, front, child, order, place), MOST) for child in range(2)
    ]
    for copy in copies:
        copy.wait()
    add_ordered_separators(block_map, front, children, work, order, counts)
    factor_corner(work, chol, inverse)


def tail_kernel(
    ids,
    map_two,
    gathered,
    chol_in,
    inverse_in,
    rows_all,
    tail,
    near_mine,
    near_other,
    far_mine,
    far_other,
    near_late,
    far_late,
    factor,
    schur,
    chol,
    inverse,
    work,
    children,
    lower,
    solved,
    solved_high,
    solved_low,
    trail,
    slots,
    order,
    place,
    sems,
    corner_sems,
):
    side, z, front, sub = ids[1], ids[2], ids[3], ids[4]
    mine = sub // 2
    copies = fetch_children(
        side, mine, (near_mine, near_other, far_mine, far_other), children, sems
    )
    for n, (ref, child) in enumerate(((near_late, mine), (far_late, 1 - mine))):
        copies.append(
            pltpu.make_async_copy(ref, children.at[child, pl.ds(SOON, LATE)], sems.at[4 + n])
        )
        copies[-1].start()
    copies.append(
        pltpu.make_async_copy(
            gathered.at[pl.ds(side * NB, NB), 4 * BLK :, :],
            lower.at[:, : 2 * BLK, :],
            sems.at[8],
        )
    )
    copies[-1].start()
    factors = [
        pltpu.make_async_copy(chol_in, chol, sems.at[6]),
        pltpu.make_async_copy(inverse_in, inverse, sems.at[7]),
    ]
    for copy in factors:
        copy.start()
    counts = [ordered(map_two, front, child, order, place) for child in range(2)]
    place_of(map_two, front, 0, slots)
    place_of(map_two, front, 1, slots)
    for s in range(4):
        for b in range(2):
            lower[2 * s + b, 2 * BLK :, :] = rows_all[s, b * BLK : (b + 1) * BLK, :]
    trail[...] = tail[...]
    for copy in copies:
        copy.wait()
    wanted = (2 * sub, 2 * sub + 1, z)

    def one_child(child, carry):
        for slot, target in enumerate(wanted):
            i = slots[child, 2 * target + 1]

            def one_block(k, carry):
                col = map_two[front, child, k]
                index = block_number(place, child, i, k)

                @pl.when((col % 2 == 0) & (i > k))
                def _():
                    add_at(lower, col // 2, slot, children[child, index])

                @pl.when((col % 2 == 0) & (i < k))
                def _():
                    add_at(lower, col // 2, slot, children[child, index].T)

                return carry

            lax.fori_loop(0, jnp.where(i >= 0, NB, 0), one_block, 0)
        k = slots[child, 2 * z + 1]
        for slot in range(2):
            i = slots[child, 2 * wanted[slot] + 1]
            both = (i >= 0) & (k >= 0)
            index = block_number(place, child, jnp.maximum(i, 0), jnp.maximum(k, 0))

            @pl.when(both & (i >= k))
            def _():
                trail[slot] = trail[slot] + children[child, index]

            @pl.when(both & (i < k))
            def _():
                trail[slot] = trail[slot] + children[child, index].T

        return carry

    lax.fori_loop(0, 2, one_child, 0)
    for copy in factors:
        copy.wait()

    @pl.when(jnp.maximum(counts[0], counts[1]) > MOST)
    def _():
        for copy in corner_copies(mine, gathered, work, corner_sems):
            copy.wait()
        add_ordered_separators(map_two, front, children, work, order, counts)
        factor_corner_again(work, chol, inverse)

    solve_rows(lambda p: pair(lower, p), chol, inverse, solved, solved_high, solved_low)
    high = jnp.concatenate([solved_high[k] for k in range(NB)], 1)
    low = jnp.concatenate([solved_low[k] for k in range(NB)], 1)
    left_high, left_low = high[: 2 * BLK], low[: 2 * BLK]
    right_high, right_low = high[2 * BLK :], low[2 * BLK :]
    update = (
        dot_nt(left_high, right_high)
        + dot_nt(left_high, right_low)
        + dot_nt(left_low, right_high)
    )
    for r in range(2):
        schur[r * BLK : (r + 1) * BLK, :] = trail[r] - update[r * BLK : (r + 1) * BLK, :]
        start = pl.multiple_of((2 * sub + r) * BLK, BLK)
        factor[2 * r * BLK : (2 * r + 1) * BLK, :] = chol[z, pl.ds(start, BLK), :]
        factor[(2 * r + 1) * BLK : (2 * r + 2) * BLK, :] = solved[z, r * BLK : (r + 1) * BLK, :]


def call(kernel, name, outs, specs, args, scratch=(), flops=0, out_specs=None):
    return pl.pallas_call(
        kernel,
        name=name,
        out_shape=outs,
        in_specs=specs,
        out_specs=out_specs or [VMEM] * len(outs),
        scratch_shapes=list(scratch),
        compiler_params=PARAMS,
        cost_estimate=pl.CostEstimate(flops=flops, bytes_accessed=flops // 400, transcendentals=0)
        if flops
        else None,
    )(*args)


def swap(value, axis):
    return lax.ppermute(value, axis, [(0, 1), (1, 0)])


def per_device(
    child_updates,
    initial_one,
    initial_two,
    pattern_one,
    pattern_two,
    parent_map_one,
    parent_map_two,
):
    x, yh, yl = lax.axis_index("x"), lax.axis_index("yh"), lax.axis_index("yl")
    core, z = lax.axis_index("core"), lax.axis_index("front")
    ids = jnp.stack([x * 4 + yh * 2 + yl, core, z, x * 2 + yh, yl * 2 + core]).astype(jnp.int32)
    panel = (NB, NB * BLK, BLK)
    block = (BLK, BLK)

    (sent,) = call(
        pack_kernel,
        "pack",
        [shape(CHILD_ROWS + CORNER_ROWS, BLK)],
        [SMEM, SMEM, ANY, ANY],
        (ids, pattern_one, child_updates, initial_one),
        [
            pltpu.VMEM((NB * BLK, BLK), F32),
            pltpu.VMEM((4, *block), F32),
            pltpu.SemaphoreType.DMA((5,)),
        ],
    )
    gathered = lax.all_gather(sent, ("core", "front"), axis=0, tiled=False)
    ids_mask, _ = lax.optimization_barrier((ids, sent))
    merged, corner_two, lower_two, row_two, tail_two = call(
        mask_kernel,
        "mask",
        [
            shape(LOWER_ROWS + CORNER_ROWS, BLK),
            shape(2 * BLK, BLK),
            shape(2 * BLK, BLK),
            shape(2 * BLK, BLK),
            shape(2, *block),
        ],
        [SMEM, SMEM, SMEM, VMEM, VMEM],
        (ids_mask, pattern_one, pattern_two, initial_one, initial_two),
        [pltpu.VMEM((4, *block), F32)],
    )
    corner_two = jnp.concatenate([corner_two, swap(corner_two, "yl"), lower_two], 0)
    rows_all = lax.all_gather(row_two, ("yl", "core"), axis=0, tiled=False)
    merged, gathered, corner_two, rows_all = lax.optimization_barrier(
        (merged, gathered, corner_two, rows_all)
    )
    merged_all = lax.all_gather(merged, ("core", "front"), axis=0, tiled=False)
    chol, inverse, lower_add, trail_add = call(
        chol_kernel,
        "chol",
        [shape(*panel), shape(NB, *block), shape(*panel), shape(36, *block)],
        [SMEM, SMEM, ANY],
        (ids, parent_map_one, gathered),
        [
            pltpu.VMEM(panel, F32),
            pltpu.VMEM((2 * NB, 5 * BLK, BLK), F32),
            pltpu.VMEM(panel, F32),
            pltpu.VMEM((36, *block), F32),
            pltpu.SemaphoreType.DMA((64,)),
        ],
        flops=40_000_000_000,
        out_specs=[VMEM, VMEM, ANY, ANY],
    )
    gathered_two = lax.all_gather(corner_two, ("core", "front"), axis=0, tiled=False)
    places = pltpu.SMEM((2, NB), jnp.int32)
    factor_one, near_mine, near_other, near_late = call(
        rest_kernel,
        "rest",
        [
            shape(NB * BLK, BLK),
            shape(SOON // 2, *block),
            shape(SOON // 2, *block),
            shape(LATE, *block),
        ],
        [SMEM, SMEM] + [ANY] * 5,
        (ids, parent_map_two, chol, inverse, lower_add, trail_add, merged_all),
        [pltpu.VMEM(panel, F32), pltpu.VMEM((NB, *block), F32)]
        + [pltpu.VMEM(panel, F32)] * 3
        + [pltpu.VMEM(panel, BF16)] * 2
        + [pltpu.VMEM((36, *block), F32)] * 3
        + [places, places, pltpu.SemaphoreType.DMA((64,))],
        flops=15_000_000_000,
        out_specs=[VMEM, ANY, ANY, ANY],
    )
    far_mine = swap(near_mine, "yl")
    far_other = swap(far_mine, "core")
    packed = (near_mine, near_other, far_mine, far_other)
    given_late, _ = lax.optimization_barrier((near_late, far_mine))
    far_late = swap(given_late, "yl")
    children = pltpu.VMEM((2, 36, *block), F32)
    chol, inverse = call(
        chol_two_kernel,
        "chol_two",
        [shape(*panel), shape(NB, *block)],
        [SMEM, SMEM] + [ANY] * 5,
        (ids, parent_map_two, gathered_two, *packed),
        [
            pltpu.VMEM(panel, F32),
            children,
            places,
            places,
            pltpu.SemaphoreType.DMA((4,)),
            pltpu.SemaphoreType.DMA((4,)),
        ],
        flops=40_000_000_000,
    )
    rows = (NB, 3 * BLK, BLK)
    factor_two, schur_two = call(
        tail_kernel,
        "tail",
        [shape(4 * BLK, BLK), shape(2 * BLK, BLK)],
        [SMEM, SMEM, ANY, ANY, ANY] + [VMEM] * 2 + [ANY] * 6,
        (
            ids,
            parent_map_two,
            gathered_two,
            chol,
            inverse,
            rows_all,
            tail_two,
            *packed,
            near_late,
            far_late,
        ),
        [
            pltpu.VMEM(panel, F32),
            pltpu.VMEM((NB, *block), F32),
            pltpu.VMEM(panel, F32),
            children,
            pltpu.VMEM(rows, F32),
            pltpu.VMEM(rows, F32),
            pltpu.VMEM(rows, BF16),
            pltpu.VMEM(rows, BF16),
            pltpu.VMEM((2, *block), F32),
            pltpu.SMEM((2, FB), jnp.int32),
            places,
            places,
            pltpu.SemaphoreType.DMA((9,)),
            pltpu.SemaphoreType.DMA((4,)),
        ],
    )
    return factor_one, factor_two, schur_two


def solution(mesh):
    cut = Mesh(mesh.devices.reshape(4, 2, 2, 2, 8), LEAF + ("front",))
    tile = P(LEAF, "front")
    return jax.shard_map(
        per_device,
        mesh=cut,
        in_specs=(tile, tile, tile, P(), P(), P(), P()),
        out_specs=(tile, tile, tile),
        check_vma=False,
    )
```

```python
import jax
import jax.numpy as jnp
from jax import lax
from jax.experimental import pallas as pl
from jax.experimental.pallas import tpu as pltpu
from jax.sharding import Mesh, PartitionSpec as P

BLK = 128
NB = 8
FB = 16
F32 = jnp.float32
BF16 = jnp.bfloat16
VMEM = pl.BlockSpec(memory_space=pltpu.VMEM)
SMEM = pl.BlockSpec(memory_space=pltpu.SMEM)
ANY = pl.BlockSpec(memory_space=pl.ANY)
HALF = BLK // 2
CORNER_ROWS = 2 * BLK + HALF
CHILD_ROWS = 4 * BLK + HALF
LOWER_ROWS = 4 * BLK
PARAMS = pltpu.CompilerParams(vmem_limit_bytes=58 * 1024 * 1024)
LEAF = ("x", "yh", "yl", "core")
MOST = 6
SOON = 22
LATE = 36 - SOON
PAIR_ROWS = BLK + HALF


def shape(*dims):
    return jax.ShapeDtypeStruct(dims, F32)


def packed_index(row, col):
    return col * NB - col * (col - 1) // 2 + row - col


def across(piece):
    return jnp.broadcast_to(piece, (8, BLK))


def lane_columns(rows, t):
    return [across(rows[:, 8 * t + b : 8 * t + b + 1]) for b in range(8)]


def factor_eights(rows, first, last):
    sub = lax.broadcasted_iota(jnp.int32, (8, BLK), 0)
    lane = lax.broadcasted_iota(jnp.int32, (8, BLK), 1)
    diag = jnp.zeros((8, BLK), F32)
    outs = []
    following = lane_columns(rows[first], first)
    for t in range(first, last):
        head = following
        below = {g: lane_columns(rows[g], t) for g in range(t + 1, last)}
        if t + 1 < last:
            following = lane_columns(rows[t + 1], t + 1)
        scale, weight = [], {}
        ahead = across(head[0][0:1])
        for b in range(8):
            pivot = ahead
            scale.append(lax.rsqrt(pivot))
            diag = jnp.where(lane == 8 * t + b, pivot * scale[b], diag)
            low = head[b] * scale[b]
            for a in range(b + 1, 8):
                weight[a, b] = across(head[b][a : a + 1]) * scale[b]
                if a == b + 1:
                    ahead = across(head[a][a : a + 1]) - weight[a, b] * weight[a, b]
                head[a] = head[a] - low * weight[a, b]
        inside = (lane >= 8 * t) & (lane < 8 * t + 8)
        pivots = []
        for b in range(8):
            unit = jnp.where(lane == 8 * t + b, 1.0, 0.0)
            row = jnp.where(inside, unit, across(rows[t][b : b + 1]))
            for a in range(b):
                row = row - weight[b, a] * pivots[a]
            pivots.append(row * scale[b])
        for g in range(t + 1, last):
            lows = []
            for b in range(8):
                column = below[g][b]
                for a in range(b):
                    column = column - lows[a] * weight[b, a]
                lows.append(column * scale[b])
            if g == t + 1:
                for b in range(8):
                    for a in range(8):
                        following[a] = following[a] - lows[b] * across(lows[b][a : a + 1])
            group = jnp.where(inside, 0.0, rows[g])
            for b in range(8):
                group = group - lows[b] * pivots[b]
            rows[g] = group
        group = pivots[7]
        for b in range(6, -1, -1):
            group = jnp.where(sub == b, pivots[b], group)
        rows[t] = group
        for a in range(1, 8):
            column = weight[a, a - 1]
            for b in range(a - 2, -1, -1):
                column = jnp.where(sub == b, weight[a, b], column)
            group = jnp.where((lane == 8 * t + a) & (sub < a), column, group)
        outs.append(group)
    return outs, diag


def factor_block(block):
    rows = [block[8 * g : 8 * g + 8] for g in range(16)]
    outs, diag = factor_eights(rows, 0, 8)
    lane = lax.broadcasted_iota(jnp.int32, (8, BLK), 1)
    row_id = lax.broadcasted_iota(jnp.int32, (BLK // 2, BLK), 0)
    col_id = lax.broadcasted_iota(jnp.int32, (BLK // 2, BLK), 1)
    left = jnp.concatenate(rows[:8], 0)
    right = jnp.where((col_id > row_id) & (col_id < BLK // 2), 0.0, left)
    left_high, left_low = halves(left)
    right_high, right_low = halves(right)
    update = lax.dot_general(
        jnp.concatenate([left_high, left_high, left_low], 0),
        jnp.concatenate([right_high, right_low, right_high], 0),
        (((0,), (0,)), ((), ())),
        preferred_element_type=F32,
    )
    for g in range(8, 16):
        rows[g] = jnp.where(lane < BLK // 2, 0.0, rows[g]) - update[8 * g : 8 * g + 8]
    more, more_diag = factor_eights(rows, 8, 16)
    full = jnp.concatenate(outs + more, 0)
    row_id = lax.broadcasted_iota(jnp.int32, (BLK, BLK), 0)
    col_id = lax.broadcasted_iota(jnp.int32, (BLK, BLK), 1)
    on_diag = jnp.broadcast_to((diag + more_diag)[0:1], (BLK, BLK))
    upper = jnp.where(col_id > row_id, full, jnp.where(col_id == row_id, on_diag, 0.0))
    return upper.T, jnp.where(col_id <= row_id, full, 0.0)


def halves(value):
    high = value.astype(BF16)
    return high, (value - high.astype(F32)).astype(BF16)


def dot_nt(left, right):
    return lax.dot_general(
        left, right, (((1,), (1,)), ((), ())), preferred_element_type=F32
    )


def dot_split(left, right):
    left_high, left_low = halves(left)
    right_high, right_low = halves(right)
    return dot_nt(
        jnp.concatenate([left_high, left_high, left_low], 1),
        jnp.concatenate([right_high, right_low, right_high], 1),
    )


def factor_corner(work, chol, inverse):
    order = NB * BLK

    def one_panel(step, carry):
        first = pl.multiple_of(step * BLK, BLK)
        lower, lower_inverse = factor_block(work[step, pl.ds(first, BLK), :])
        chol[step, pl.ds(first, BLK), :] = lower
        inverse[step] = lower_inverse
        for j in range(NB - 1):

            @pl.when(step == j)
            def _():
                start = BLK * (j + 1)
                panel = dot_split(work[j, start:, :], inverse[j])
                chol[j, start:, :] = panel
                high, low = halves(panel)
                left = jnp.concatenate([high, high, low], 1)
                right = jnp.concatenate([high, low, high], 1)
                for k in range(j + 1, NB, 2):
                    wide = min(2, NB - k)
                    top = BLK * k - start
                    update = dot_nt(left[top:], right[top : top + wide * BLK])
                    for w in range(wide):
                        work[k + w, BLK * k :, :] = (
                            work[k + w, BLK * k :, :] - update[:, w * BLK : (w + 1) * BLK]
                        )

        return carry

    for j in range(1, NB):
        chol[j, : j * BLK, :] = jnp.zeros((j * BLK, BLK), F32)
    lax.fori_loop(0, NB, one_panel, 0)


def factor_corner_again(work, chol, inverse):
    def rows_of(block):
        return pl.ds(pl.multiple_of(block * BLK, BLK), BLK)

    def one_panel(step, carry):
        lower, lower_inverse = factor_block(work[step, rows_of(step), :])
        chol[step, rows_of(step), :] = lower
        inverse[step] = lower_inverse

        def one_block(i, carry):
            chol[step, rows_of(i), :] = dot_split(work[step, rows_of(i), :], inverse[step])
            return carry

        def one_col(k, carry):
            def one_row(i, carry):
                work[k, rows_of(i), :] = work[k, rows_of(i), :] - dot_split(
                    chol[step, rows_of(i), :], chol[step, rows_of(k), :]
                )
                return carry

            return lax.fori_loop(k, NB, one_row, carry)

        lax.fori_loop(step + 1, NB, one_block, 0)
        return lax.fori_loop(step + 1, NB, one_col, carry)

    chol[...] = jnp.zeros_like(chol)
    lax.fori_loop(0, NB, one_panel, 0)


def solve_rows(right_side, chol, inverse, solved, solved_high, solved_low):
    for p in range(0, NB, 2):
        value = right_side(p)
        if p:
            depth = range(p)
            left_high = jnp.concatenate([solved_high[k] for k in depth], 1)
            left_low = jnp.concatenate([solved_low[k] for k in depth], 1)
            right = jnp.concatenate([chol[k, p * BLK : (p + 2) * BLK, :] for k in depth], 1)
            right_high, right_low = halves(right)
            value = value - (
                dot_nt(left_high, right_high)
                + dot_nt(left_high, right_low)
                + dot_nt(left_low, right_high)
            )
        between = chol[p, (p + 1) * BLK : (p + 2) * BLK, :]
        corner = -dot_split(inverse[p + 1], dot_split(inverse[p].T, between))
        pair_inverse = jnp.concatenate(
            [
                jnp.concatenate([inverse[p], jnp.zeros((BLK, BLK), F32)], 1),
                jnp.concatenate([corner, inverse[p + 1]], 1),
            ],
            0,
        )
        value = dot_split(value, pair_inverse)
        high, low = halves(value)
        for w in range(2):
            lanes = slice(w * BLK, (w + 1) * BLK)
            solved[p + w] = value[:, lanes]
            solved_high[p + w], solved_low[p + w] = high[:, lanes], low[:, lanes]


def pair(ref, p):
    return jnp.concatenate([ref[p], ref[p + 1]], 1)


def place_of(block_map, front, child, slots):
    for m in range(FB):
        slots[child, m] = -1
    for i in range(NB):
        slots[child, block_map[front, child, i]] = i


def kept(pattern, front, row, col):
    return (pattern[front, row, col] == 1) | (pattern[front, col, row] == 1) | (row == col)


def first_turn(core, z):
    return jnp.where((core == 0) & (z >= 4), 1, 0)


def send_blocks(tile, core, z, out):
    base = NB // 2 * core
    for turn in range(2):
        local = (z + first_turn(core, z) + turn) % 4
        block = tile[local]
        at = turn * BLK

        @pl.when(base + local >= z)
        def _():
            out[at : at + BLK, :] = block

        @pl.when(base + local < z)
        def _():
            out[at : at + BLK, :] = block.T

    block = tile[(z + 2) % 4]

    @pl.when(z % 4 < 2)
    def _():
        out[2 * BLK :, :] = block[:HALF, :]

    @pl.when(z % 4 >= 2)
    def _():
        out[2 * BLK :, :] = block.T[HALF:, :]


def static_blocks():
    where = {}
    for core in range(2):
        for z in range(NB):
            turn0 = 1 if core == 0 and z >= 4 else 0
            for turn in range(2):
                row = 4 * core + (z + turn0 + turn) % 4
                where[max(row, z), min(row, z)] = [(core * NB + z, turn * BLK, BLK)]
            if z // 4 == core:
                row = 4 * core + (z + 2) % 4
                key = (max(row, z), min(row, z))
                entry = (core * NB + z, 2 * BLK, HALF)
                known = where.setdefault(key, [])
                if z % 4 < 2:
                    known.insert(0, entry)
                else:
                    known.append(entry)
    return where


def send_child(child, z, out):
    for turn in range(4):
        row = (z + turn) % NB
        at = turn * BLK
        block = child[pl.ds(pl.multiple_of(row * BLK, BLK), BLK), :]

        @pl.when(row >= z)
        def _():
            out[at : at + BLK, :] = block

        @pl.when(row < z)
        def _():
            out[at : at + BLK, :] = block.T

    row = (z + 4) % NB
    block = child[pl.ds(pl.multiple_of(row * BLK, BLK), BLK), :]

    @pl.when(row > z)
    def _():
        out[4 * BLK :, :] = block[:HALF, :]

    @pl.when(row < z)
    def _():
        out[4 * BLK :, :] = block.T[HALF:, :]


def child_copies(gathered, children, sems):
    return [
        pltpu.make_async_copy(
            gathered.at[:, :CHILD_ROWS, :], children.at[:, :CHILD_ROWS, :], sems.at[0]
        )
    ] + [
        pltpu.make_async_copy(
            gathered.at[child * NB + 4 : child * NB + 8, 4 * BLK : CHILD_ROWS, :],
            children.at[child * NB : child * NB + 4, CHILD_ROWS:, :],
            sems.at[1 + child],
        )
        for child in range(2)
    ]


def each_gathered(block_map, front, children, visit):
    def one(n, carry):
        child, m = n // 36, n % 36
        z = jnp.where(m < 32, m // 4, m - 32)
        turn = jnp.where(m < 32, m % 4, 4)
        other = (z + turn) % NB
        row = block_map[front, child, jnp.maximum(z, other)]
        col = block_map[front, child, jnp.minimum(z, other)]
        start = pl.multiple_of(turn * BLK, BLK)
        visit(row, col, lambda: children[child * NB + z, pl.ds(start, BLK), :])
        return carry

    lax.fori_loop(0, 72, one, 0)


def ordered(block_map, front, child, order, place):
    count = jnp.int32(0)
    for parity in range(2):
        for i in range(NB):
            hit = block_map[front, child, i] % 2 == parity

            @pl.when(hit)
            def _(count=count, i=i):
                order[child, count] = i
                place[child, i] = count

            count = count + jnp.where(hit, 1, 0)
        if parity == 0:
            separators = count
    return separators


def number_of(a, b):
    return a * (a + 1) // 2 + b


def block_number(place, child, i, k):
    a, b = place[child, i], place[child, k]
    return number_of(jnp.maximum(a, b), jnp.minimum(a, b))


def add_ordered_separators(block_map, front, children, work, order, counts):
    for child in range(2):

        def one_place(a, carry):
            def other_place(b, carry):
                i, k = order[child, a], order[child, b]
                row = block_map[front, child, jnp.maximum(i, k)] // 2
                col = block_map[front, child, jnp.minimum(i, k)] // 2
                number = number_of(a, b)

                @pl.when(row >= col)
                def _():
                    add_at(work, col, row, children[child, number])

                @pl.when(row < col)
                def _():
                    add_at(work, row, col, children[child, number].T)

                return carry

            return lax.fori_loop(0, a + 1, other_place, carry)

        lax.fori_loop(0, counts[child], one_place, 0)


def add_at(ref, lead, block_row, block):
    place = pl.ds(pl.multiple_of(block_row * BLK, BLK), BLK)
    ref[lead, place, :] = ref[lead, place, :] + block


def contributions_into(corner, lower, trail):
    def visit(row, col, block):
        row_odd, col_odd = row % 2 == 1, col % 2 == 1
        row_half, col_half = row // 2, col // 2

        @pl.when(~row_odd & ~col_odd & (row >= col))
        def _():
            add_at(corner, col_half, row_half, block())

        @pl.when(~row_odd & ~col_odd & (row < col))
        def _():
            add_at(corner, row_half, col_half, block().T)

        @pl.when(row_odd & ~col_odd)
        def _():
            add_at(lower, col_half, row_half, block())

        @pl.when(~row_odd & col_odd)
        def _():
            add_at(lower, row_half, col_half, block().T)

        @pl.when(row_odd & col_odd & (row >= col))
        def _():
            add_at(trail, packed_index(row_half, col_half), 0, block())

        @pl.when(row_odd & col_odd & (row < col))
        def _():
            add_at(trail, packed_index(col_half, row_half), 0, block().T)

    return visit


def sent_row(sub, z):
    return jnp.where(sub >= z // 2, z % 2, 1 - z % 2)


def send_pair(tile, sub, z, out):
    block = tile[sent_row(sub, z)]

    @pl.when(2 * sub + sent_row(sub, z) >= z)
    def _():
        out[:BLK, :] = block

    @pl.when(2 * sub + sent_row(sub, z) < z)
    def _():
        out[:BLK, :] = block.T

    @pl.when(z % 2 == 0)
    def _():
        out[BLK:, :] = tile[1][:HALF, :]

    @pl.when(z % 2 == 1)
    def _():
        out[BLK:, :] = tile[0].T[HALF:, :]


def masked_tile(initial, pattern, front, row, local, col):
    keep = kept(pattern, front, row, col)
    return jnp.where(keep, initial[local * BLK : (local + 1) * BLK, :], 0.0)


def pack_kernel(ids, pattern_one, child_in, initial, sent, child, corner, sems):
    front_one, side, z = ids[0], ids[1], ids[2]
    copies = [pltpu.make_async_copy(child_in, child, sems.at[4])]
    for r in range(4):
        source = initial.at[2 * r * BLK : (2 * r + 1) * BLK, :BLK]
        copies.append(pltpu.make_async_copy(source, corner.at[r], sems.at[r]))
    for copy in copies:
        copy.start()
    copies[0].wait()
    send_child(child, z, sent.at[:CHILD_ROWS, :])
    for copy in copies[1:]:
        copy.wait()
    for r in range(4):
        keep = kept(pattern_one, front_one, NB * side + 2 * r, 2 * z)
        corner[r] = jnp.where(keep, corner[r], 0.0)
    send_blocks(corner, side, z, sent.at[CHILD_ROWS:, :])


def mask_kernel(
    ids,
    pattern_one,
    pattern_two,
    initial_one,
    initial_two,
    merged,
    corner_two,
    lower_two,
    row_two,
    tail_two,
    tile,
    corner_tile,
):
    front_one, side, z, front_two, sub = ids[0], ids[1], ids[2], ids[3], ids[4]
    first, second = initial_one.at[:, :BLK], initial_one.at[:, BLK:]
    for r in range(4):
        row = NB * side + 2 * r + 1
        merged[r * BLK : (r + 1) * BLK, :] = masked_tile(
            first, pattern_one, front_one, row, 2 * r + 1, 2 * z
        )
        tile[r] = masked_tile(second, pattern_one, front_one, row, 2 * r + 1, 2 * z + 1)
    send_blocks(tile, side, z, merged.at[LOWER_ROWS:, :])
    for r in range(4):
        for w in range(2):
            columns = initial_two.at[:, w * BLK : (w + 1) * BLK]
            block = masked_tile(columns, pattern_two, front_two, 4 * sub + r, r, 2 * z + w)
            at = slice(r // 2 * BLK, (r // 2 + 1) * BLK)
            if w == 0 and r % 2 == 0:
                corner_tile[r // 2] = block
            elif w == 0:
                lower_two[at, :] = block
            elif r % 2 == 0:
                row_two[at, :] = block.T
            else:
                tail_two[r // 2] = block
    send_pair(corner_tile, sub, z, corner_two)


def chol_kernel(
    ids,
    block_map,
    gathered,
    chol,
    inverse,
    lower_out,
    trail_out,
    work,
    children,
    lower,
    trail,
    sems,
):
    front = ids[0]
    copies = child_copies(gathered, children, sems)
    for (row, col), parts in static_blocks().items():
        start = row * BLK
        for piece, at, rows in parts:
            copies.append(
                pltpu.make_async_copy(
                    gathered.at[piece, CHILD_ROWS + at : CHILD_ROWS + at + rows, :],
                    work.at[col, start : start + rows, :],
                    sems.at[len(copies)],
                )
            )
            start += rows
    for copy in copies:
        copy.start()
    lower[...] = jnp.zeros_like(lower)
    trail[...] = jnp.zeros_like(trail)
    for copy in copies:
        copy.wait()
    each_gathered(block_map, front, children, contributions_into(work, lower, trail))
    outs = [
        pltpu.make_async_copy(lower, lower_out, sems.at[0]),
        pltpu.make_async_copy(trail, trail_out, sems.at[1]),
    ]
    for copy in outs:
        copy.start()
    factor_corner(work, chol, inverse)
    for copy in outs:
        copy.wait()


def rest_kernel(
    ids,
    block_map,
    chol_in,
    inverse_in,
    lower_in,
    trail_in,
    merged,
    factor,
    mine,
    other,
    late,
    chol,
    inverse,
    lower,
    lower_add,
    solved,
    solved_high,
    solved_low,
    trail,
    trail_add,
    staged,
    order,
    place,
    sems,
):
    side, z, child = ids[1], ids[2], ids[4] // 2
    half = NB // 2 * BLK
    used = []

    def fetch(source, target):
        copy = pltpu.make_async_copy(source, target, sems.at[len(used)])
        copy.start()
        used.append(copy)
        return copy

    first = [fetch(inverse_in, inverse)]
    columns = {}
    for p in range(0, NB, 2):
        columns[p] = [fetch(lower_in.at[p : p + 2], lower_add.at[p : p + 2])]
        for core in range(2):
            columns[p].append(
                fetch(
                    merged.at[core * NB + p : core * NB + p + 2, :LOWER_ROWS, :],
                    lower.at[p : p + 2, core * half : (core + 1) * half, :],
                )
            )
        if p == 0:
            first.append(fetch(chol_in, chol))
    last = [fetch(trail_in, trail_add)]
    for (row, col), parts in static_blocks().items():
        start = 0
        for piece, at, rows in parts:
            last.append(
                fetch(
                    merged.at[piece, LOWER_ROWS + at : LOWER_ROWS + at + rows, :],
                    trail.at[packed_index(row, col), start : start + rows, :],
                )
            )
            start += rows
    ordered(block_map, ids[3], child, order, place)
    for copy in first:
        copy.wait()

    def right_side(p):
        for copy in columns[p]:
            copy.wait()
        return pair(lower, p) + pair(lower_add, p)

    solve_rows(right_side, chol, inverse, solved, solved_high, solved_low)
    for copy in last:
        copy.wait()
    for p in range(0, NB, 2):
        high = jnp.concatenate([solved_high[k, p * BLK :, :] for k in range(NB)], 1)
        low = jnp.concatenate([solved_low[k, p * BLK :, :] for k in range(NB)], 1)
        wide_high, wide_low = high[: 2 * BLK], low[: 2 * BLK]
        update = dot_nt(high, wide_high) + dot_nt(high, wide_low) + dot_nt(low, wide_high)
        for w in range(2):
            for i in range(p + w, NB):
                index = packed_index(i, p + w)
                number = block_number(place, child, i, p + w)
                half_id = jnp.where(number < SOON // 2, 0, 1)
                soon = (half_id + side) % 2 * (SOON // 2) + number - half_id * (SOON // 2)
                staged[jnp.where(number < SOON, soon, number)] = (
                    trail[index]
                    + trail_add[index]
                    - update[(i - p) * BLK : (i - p + 1) * BLK, w * BLK : (w + 1) * BLK]
                )
    outs = [
        pltpu.make_async_copy(staged.at[: SOON // 2], mine, sems.at[0]),
        pltpu.make_async_copy(staged.at[SOON // 2 : SOON], other, sems.at[1]),
        pltpu.make_async_copy(staged.at[SOON:], late, sems.at[2]),
    ]
    for copy in outs:
        copy.start()
    for r in range(NB):
        source = solved if r % 2 else chol
        start = pl.multiple_of((side * (NB // 2) + r // 2) * BLK, BLK)
        factor[r * BLK : (r + 1) * BLK, :] = source[z, pl.ds(start, BLK), :]
    for copy in outs:
        copy.wait()


def fetch_children(side, mine, refs, children, sems):
    near_mine, near_other, far_mine, far_other = refs
    half = SOON // 2
    copies = []
    for n, (ref, child, half_id) in enumerate(
        (
            (near_mine, mine, side),
            (near_other, mine, 1 - side),
            (far_mine, 1 - mine, side),
            (far_other, 1 - mine, 1 - side),
        )
    ):
        target = children.at[child, pl.ds(half * half_id, half)]
        copies.append(pltpu.make_async_copy(ref, target, sems.at[n]))
        copies[-1].start()
    return copies


def corner_copies(side_of, gathered, work, sems):
    copies = []

    def fetch(piece, first, rows, block_row, block_col, start):
        place = pl.multiple_of(block_row * BLK + start, HALF)
        copies.append(
            pltpu.make_async_copy(
                gathered.at[piece, first : first + rows, :],
                work.at[block_col, pl.ds(place, rows), :],
                sems.at[len(copies)],
            )
        )
        copies[-1].start()

    for core in range(2):
        for n, y in ((0, side_of), (1, 1 - side_of)):
            sub = 2 * y + core
            for z in range(NB):
                row = 2 * sub + sent_row(sub, z)
                top, left = jnp.maximum(row, z), jnp.minimum(row, z)
                fetch(core * NB + z, n * PAIR_ROWS, BLK, top, left, 0)
            for d in range(2):
                piece = core * NB + 2 * sub + d
                fetch(piece, n * PAIR_ROWS + BLK, HALF, 2 * sub + 1, 2 * sub, d * HALF)
    return copies


def chol_two_kernel(
    ids,
    block_map,
    gathered,
    near_mine,
    near_other,
    far_mine,
    far_other,
    chol,
    inverse,
    work,
    children,
    order,
    place,
    sems,
    corner_sems,
):
    side, front, sub = ids[1], ids[3], ids[4]
    copies = fetch_children(
        side, sub // 2, (near_mine, near_other, far_mine, far_other), children, sems
    )
    copies += corner_copies(sub // 2, gathered, work, corner_sems)
    counts = [
        jnp.minimum(ordered(block_map, front, child, order, place), MOST) for child in range(2)
    ]
    for copy in copies:
        copy.wait()
    add_ordered_separators(block_map, front, children, work, order, counts)
    factor_corner(work, chol, inverse)


def tail_kernel(
    ids,
    map_two,
    gathered,
    chol_in,
    inverse_in,
    rows_all,
    tail,
    near_mine,
    near_other,
    far_mine,
    far_other,
    near_late,
    far_late,
    factor,
    schur,
    chol,
    inverse,
    work,
    children,
    lower,
    solved,
    solved_high,
    solved_low,
    trail,
    slots,
    order,
    place,
    sems,
    corner_sems,
):
    side, z, front, sub = ids[1], ids[2], ids[3], ids[4]
    mine = sub // 2
    copies = fetch_children(
        side, mine, (near_mine, near_other, far_mine, far_other), children, sems
    )
    for n, (ref, child) in enumerate(((near_late, mine), (far_late, 1 - mine))):
        copies.append(
            pltpu.make_async_copy(ref, children.at[child, pl.ds(SOON, LATE)], sems.at[4 + n])
        )
        copies[-1].start()
    copies.append(
        pltpu.make_async_copy(
            gathered.at[pl.ds(side * NB, NB), 2 * PAIR_ROWS :, :],
            lower.at[:, : 2 * BLK, :],
            sems.at[8],
        )
    )
    copies[-1].start()
    factors = [
        pltpu.make_async_copy(chol_in, chol, sems.at[6]),
        pltpu.make_async_copy(inverse_in, inverse, sems.at[7]),
    ]
    for copy in factors:
        copy.start()
    counts = [ordered(map_two, front, child, order, place) for child in range(2)]
    place_of(map_two, front, 0, slots)
    place_of(map_two, front, 1, slots)
    for s in range(4):
        for b in range(2):
            lower[2 * s + b, 2 * BLK :, :] = rows_all[s, b * BLK : (b + 1) * BLK, :]
    trail[...] = tail[...]
    for copy in copies:
        copy.wait()
    wanted = (2 * sub, 2 * sub + 1, z)

    def one_child(child, carry):
        for slot, target in enumerate(wanted):
            i = slots[child, 2 * target + 1]

            def one_block(k, carry):
                col = map_two[front, child, k]
                index = block_number(place, child, i, k)

                @pl.when((col % 2 == 0) & (i > k))
                def _():
                    add_at(lower, col // 2, slot, children[child, index])

                @pl.when((col % 2 == 0) & (i < k))
                def _():
                    add_at(lower, col // 2, slot, children[child, index].T)

                return carry

            lax.fori_loop(0, jnp.where(i >= 0, NB, 0), one_block, 0)
        k = slots[child, 2 * z + 1]
        for slot in range(2):
            i = slots[child, 2 * wanted[slot] + 1]
            both = (i >= 0) & (k >= 0)
            index = block_number(place, child, jnp.maximum(i, 0), jnp.maximum(k, 0))

            @pl.when(both & (i >= k))
            def _():
                trail[slot] = trail[slot] + children[child, index]

            @pl.when(both & (i < k))
            def _():
                trail[slot] = trail[slot] + children[child, index].T

        return carry

    lax.fori_loop(0, 2, one_child, 0)
    for copy in factors:
        copy.wait()

    @pl.when(jnp.maximum(counts[0], counts[1]) > MOST)
    def _():
        for copy in corner_copies(mine, gathered, work, corner_sems):
            copy.wait()
        add_ordered_separators(map_two, front, children, work, order, counts)
        factor_corner_again(work, chol, inverse)

    solve_rows(lambda p: pair(lower, p), chol, inverse, solved, solved_high, solved_low)
    high = jnp.concatenate([solved_high[k] for k in range(NB)], 1)
    low = jnp.concatenate([solved_low[k] for k in range(NB)], 1)
    left_high, left_low = high[: 2 * BLK], low[: 2 * BLK]
    right_high, right_low = high[2 * BLK :], low[2 * BLK :]
    update = (
        dot_nt(left_high, right_high)
        + dot_nt(left_high, right_low)
        + dot_nt(left_low, right_high)
    )
    for r in range(2):
        schur[r * BLK : (r + 1) * BLK, :] = trail[r] - update[r * BLK : (r + 1) * BLK, :]
        start = pl.multiple_of((2 * sub + r) * BLK, BLK)
        factor[2 * r * BLK : (2 * r + 1) * BLK, :] = chol[z, pl.ds(start, BLK), :]
        factor[(2 * r + 1) * BLK : (2 * r + 2) * BLK, :] = solved[z, r * BLK : (r + 1) * BLK, :]


def call(kernel, name, outs, specs, args, scratch=(), flops=0, out_specs=None):
    return pl.pallas_call(
        kernel,
        name=name,
        out_shape=outs,
        in_specs=specs,
        out_specs=out_specs or [VMEM] * len(outs),
        scratch_shapes=list(scratch),
        compiler_params=PARAMS,
        cost_estimate=pl.CostEstimate(flops=flops, bytes_accessed=flops // 400, transcendentals=0)
        if flops
        else None,
    )(*args)


def swap(value, axis):
    return lax.ppermute(value, axis, [(0, 1), (1, 0)])


def per_device(
    child_updates,
    initial_one,
    initial_two,
    pattern_one,
    pattern_two,
    parent_map_one,
    parent_map_two,
):
    x, yh, yl = lax.axis_index("x"), lax.axis_index("yh"), lax.axis_index("yl")
    core, z = lax.axis_index("core"), lax.axis_index("front")
    ids = jnp.stack([x * 4 + yh * 2 + yl, core, z, x * 2 + yh, yl * 2 + core]).astype(jnp.int32)
    panel = (NB, NB * BLK, BLK)
    block = (BLK, BLK)

    (sent,) = call(
        pack_kernel,
        "pack",
        [shape(CHILD_ROWS + CORNER_ROWS, BLK)],
        [SMEM, SMEM, ANY, ANY],
        (ids, pattern_one, child_updates, initial_one),
        [
            pltpu.VMEM((NB * BLK, BLK), F32),
            pltpu.VMEM((4, *block), F32),
            pltpu.SemaphoreType.DMA((5,)),
        ],
    )
    gathered = lax.all_gather(sent, ("core", "front"), axis=0, tiled=False)
    ids_mask, _ = lax.optimization_barrier((ids, sent))
    merged, corner_two, lower_two, row_two, tail_two = call(
        mask_kernel,
        "mask",
        [
            shape(LOWER_ROWS + CORNER_ROWS, BLK),
            shape(PAIR_ROWS, BLK),
            shape(2 * BLK, BLK),
            shape(2 * BLK, BLK),
            shape(2, *block),
        ],
        [SMEM, SMEM, SMEM, VMEM, VMEM],
        (ids_mask, pattern_one, pattern_two, initial_one, initial_two),
        [pltpu.VMEM((4, *block), F32), pltpu.VMEM((2, *block), F32)],
    )
    corner_two = jnp.concatenate([corner_two, swap(corner_two, "yl"), lower_two], 0)
    rows_all = lax.all_gather(row_two, ("yl", "core"), axis=0, tiled=False)
    merged, gathered, corner_two, rows_all = lax.optimization_barrier(
        (merged, gathered, corner_two, rows_all)
    )
    merged_all = lax.all_gather(merged, ("core", "front"), axis=0, tiled=False)
    chol, inverse, lower_add, trail_add = call(
        chol_kernel,
        "chol",
        [shape(*panel), shape(NB, *block), shape(*panel), shape(36, *block)],
        [SMEM, SMEM, ANY],
        (ids, parent_map_one, gathered),
        [
            pltpu.VMEM(panel, F32),
            pltpu.VMEM((2 * NB, 5 * BLK, BLK), F32),
            pltpu.VMEM(panel, F32),
            pltpu.VMEM((36, *block), F32),
            pltpu.SemaphoreType.DMA((64,)),
        ],
        flops=40_000_000_000,
        out_specs=[VMEM, VMEM, ANY, ANY],
    )
    gathered_two = lax.all_gather(corner_two, ("core", "front"), axis=0, tiled=False)
    places = pltpu.SMEM((2, NB), jnp.int32)
    factor_one, near_mine, near_other, near_late = call(
        rest_kernel,
        "rest",
        [
            shape(NB * BLK, BLK),
            shape(SOON // 2, *block),
            shape(SOON // 2, *block),
            shape(LATE, *block),
        ],
        [SMEM, SMEM] + [ANY] * 5,
        (ids, parent_map_two, chol, inverse, lower_add, trail_add, merged_all),
        [pltpu.VMEM(panel, F32), pltpu.VMEM((NB, *block), F32)]
        + [pltpu.VMEM(panel, F32)] * 3
        + [pltpu.VMEM(panel, BF16)] * 2
        + [pltpu.VMEM((36, *block), F32)] * 3
        + [places, places, pltpu.SemaphoreType.DMA((64,))],
        flops=15_000_000_000,
        out_specs=[VMEM, ANY, ANY, ANY],
    )
    far_mine = swap(near_mine, "yl")
    far_other = swap(far_mine, "core")
    packed = (near_mine, near_other, far_mine, far_other)
    given_late, _ = lax.optimization_barrier((near_late, far_mine))
    far_late = swap(given_late, "yl")
    children = pltpu.VMEM((2, 36, *block), F32)
    chol, inverse = call(
        chol_two_kernel,
        "chol_two",
        [shape(*panel), shape(NB, *block)],
        [SMEM, SMEM] + [ANY] * 5,
        (ids, parent_map_two, gathered_two, *packed),
        [
            pltpu.VMEM(panel, F32),
            children,
            places,
            places,
            pltpu.SemaphoreType.DMA((4,)),
            pltpu.SemaphoreType.DMA((40,)),
        ],
        flops=40_000_000_000,
    )
    rows = (NB, 3 * BLK, BLK)
    factor_two, schur_two = call(
        tail_kernel,
        "tail",
        [shape(4 * BLK, BLK), shape(2 * BLK, BLK)],
        [SMEM, SMEM, ANY, ANY, ANY] + [VMEM] * 2 + [ANY] * 6,
        (
            ids,
            parent_map_two,
            gathered_two,
            chol,
            inverse,
            rows_all,
            tail_two,
            *packed,
            near_late,
            far_late,
        ),
        [
            pltpu.VMEM(panel, F32),
            pltpu.VMEM((NB, *block), F32),
            pltpu.VMEM(panel, F32),
            children,
            pltpu.VMEM(rows, F32),
            pltpu.VMEM(rows, F32),
            pltpu.VMEM(rows, BF16),
            pltpu.VMEM(rows, BF16),
            pltpu.VMEM((2, *block), F32),
            pltpu.SMEM((2, FB), jnp.int32),
            places,
            places,
            pltpu.SemaphoreType.DMA((9,)),
            pltpu.SemaphoreType.DMA((40,)),
        ],
    )
    return factor_one, factor_two, schur_two


def solution(mesh):
    cut = Mesh(mesh.devices.reshape(4, 2, 2, 2, 8), LEAF + ("front",))
    tile = P(LEAF, "front")
    return jax.shard_map(
        per_device,
        mesh=cut,
        in_specs=(tile, tile, tile, P(), P(), P(), P()),
        out_specs=(tile, tile, tile),
        check_vma=False,
    )
```

```python
import jax
import jax.numpy as jnp
from jax import lax
from jax.experimental import pallas as pl
from jax.experimental.pallas import tpu as pltpu
from jax.sharding import Mesh, PartitionSpec as P

BLK = 128
NB = 8
FB = 16
F32 = jnp.float32
BF16 = jnp.bfloat16
VMEM = pl.BlockSpec(memory_space=pltpu.VMEM)
SMEM = pl.BlockSpec(memory_space=pltpu.SMEM)
ANY = pl.BlockSpec(memory_space=pl.ANY)
HALF = BLK // 2
CORNER_ROWS = 2 * BLK + HALF
CHILD_ROWS = 4 * BLK + HALF
LOWER_ROWS = 4 * BLK
PARAMS = pltpu.CompilerParams(vmem_limit_bytes=58 * 1024 * 1024)
LEAF = ("x", "yh", "yl", "core")
MOST = 6
SOON = 22
LATE = 36 - SOON
PAIR_ROWS = BLK + HALF


def shape(*dims):
    return jax.ShapeDtypeStruct(dims, F32)


def packed_index(row, col):
    return col * NB - col * (col - 1) // 2 + row - col


def across(piece):
    return jnp.broadcast_to(piece, (8, BLK))


def lane_columns(rows, t):
    return [across(rows[:, 8 * t + b : 8 * t + b + 1]) for b in range(8)]


def factor_eights(rows, first, last):
    sub = lax.broadcasted_iota(jnp.int32, (8, BLK), 0)
    lane = lax.broadcasted_iota(jnp.int32, (8, BLK), 1)
    diag = jnp.zeros((8, BLK), F32)
    outs = []
    following = lane_columns(rows[first], first)
    for t in range(first, last):
        head = following
        below = {g: lane_columns(rows[g], t) for g in range(t + 1, last)}
        if t + 1 < last:
            following = lane_columns(rows[t + 1], t + 1)
        scale, weight = [], {}
        ahead = across(head[0][0:1])
        for b in range(8):
            pivot = ahead
            scale.append(lax.rsqrt(pivot))
            diag = jnp.where(lane == 8 * t + b, pivot * scale[b], diag)
            low = head[b] * scale[b]
            for a in range(b + 1, 8):
                weight[a, b] = across(head[b][a : a + 1]) * scale[b]
                if a == b + 1:
                    ahead = across(head[a][a : a + 1]) - weight[a, b] * weight[a, b]
                head[a] = head[a] - low * weight[a, b]
        inside = (lane >= 8 * t) & (lane < 8 * t + 8)
        pivots = []
        for b in range(8):
            unit = jnp.where(lane == 8 * t + b, 1.0, 0.0)
            row = jnp.where(inside, unit, across(rows[t][b : b + 1]))
            for a in range(b):
                row = row - weight[b, a] * pivots[a]
            pivots.append(row * scale[b])
        for g in range(t + 1, last):
            lows = []
            for b in range(8):
                column = below[g][b]
                for a in range(b):
                    column = column - lows[a] * weight[b, a]
                lows.append(column * scale[b])
            if g == t + 1:
                for b in range(8):
                    for a in range(8):
                        following[a] = following[a] - lows[b] * across(lows[b][a : a + 1])
            group = jnp.where(inside, 0.0, rows[g])
            for b in range(8):
                group = group - lows[b] * pivots[b]
            rows[g] = group
        group = pivots[7]
        for b in range(6, -1, -1):
            group = jnp.where(sub == b, pivots[b], group)
        rows[t] = group
        for a in range(1, 8):
            column = weight[a, a - 1]
            for b in range(a - 2, -1, -1):
                column = jnp.where(sub == b, weight[a, b], column)
            group = jnp.where((lane == 8 * t + a) & (sub < a), column, group)
        outs.append(group)
    return outs, diag


def factor_block(block):
    rows = [block[8 * g : 8 * g + 8] for g in range(16)]
    outs, diag = factor_eights(rows, 0, 8)
    lane = lax.broadcasted_iota(jnp.int32, (8, BLK), 1)
    row_id = lax.broadcasted_iota(jnp.int32, (BLK // 2, BLK), 0)
    col_id = lax.broadcasted_iota(jnp.int32, (BLK // 2, BLK), 1)
    left = jnp.concatenate(rows[:8], 0)
    right = jnp.where((col_id > row_id) & (col_id < BLK // 2), 0.0, left)
    left_high, left_low = halves(left)
    right_high, right_low = halves(right)
    update = lax.dot_general(
        jnp.concatenate([left_high, left_high, left_low], 0),
        jnp.concatenate([right_high, right_low, right_high], 0),
        (((0,), (0,)), ((), ())),
        preferred_element_type=F32,
    )
    for g in range(8, 16):
        rows[g] = jnp.where(lane < BLK // 2, 0.0, rows[g]) - update[8 * g : 8 * g + 8]
    more, more_diag = factor_eights(rows, 8, 16)
    full = jnp.concatenate(outs + more, 0)
    row_id = lax.broadcasted_iota(jnp.int32, (BLK, BLK), 0)
    col_id = lax.broadcasted_iota(jnp.int32, (BLK, BLK), 1)
    on_diag = jnp.broadcast_to((diag + more_diag)[0:1], (BLK, BLK))
    upper = jnp.where(col_id > row_id, full, jnp.where(col_id == row_id, on_diag, 0.0))
    return upper.T, jnp.where(col_id <= row_id, full, 0.0)


def halves(value):
    high = value.astype(BF16)
    return high, (value - high.astype(F32)).astype(BF16)


def dot_nt(left, right):
    return lax.dot_general(
        left, right, (((1,), (1,)), ((), ())), preferred_element_type=F32
    )


def dot_split(left, right):
    left_high, left_low = halves(left)
    right_high, right_low = halves(right)
    return dot_nt(
        jnp.concatenate([left_high, left_high, left_low], 1),
        jnp.concatenate([right_high, right_low, right_high], 1),
    )


def factor_corner(work, chol, inverse):
    order = NB * BLK

    def one_panel(step, carry):
        first = pl.multiple_of(step * BLK, BLK)
        lower, lower_inverse = factor_block(work[step, pl.ds(first, BLK), :])
        chol[step, pl.ds(first, BLK), :] = lower
        inverse[step] = lower_inverse
        for j in range(NB - 1):

            @pl.when(step == j)
            def _():
                start = BLK * (j + 1)
                panel = dot_split(work[j, start:, :], inverse[j])
                chol[j, start:, :] = panel
                high, low = halves(panel)
                left = jnp.concatenate([high, high, low], 1)
                right = jnp.concatenate([high, low, high], 1)
                for k in range(j + 1, NB, 2):
                    wide = min(2, NB - k)
                    top = BLK * k - start
                    update = dot_nt(left[top:], right[top : top + wide * BLK])
                    for w in range(wide):
                        work[k + w, BLK * k :, :] = (
                            work[k + w, BLK * k :, :] - update[:, w * BLK : (w + 1) * BLK]
                        )

        return carry

    for j in range(1, NB):
        chol[j, : j * BLK, :] = jnp.zeros((j * BLK, BLK), F32)
    lax.fori_loop(0, NB, one_panel, 0)


def factor_corner_again(work, chol, inverse):
    def rows_of(block):
        return pl.ds(pl.multiple_of(block * BLK, BLK), BLK)

    def one_panel(step, carry):
        lower, lower_inverse = factor_block(work[step, rows_of(step), :])
        chol[step, rows_of(step), :] = lower
        inverse[step] = lower_inverse

        def one_block(i, carry):
            chol[step, rows_of(i), :] = dot_split(work[step, rows_of(i), :], inverse[step])
            return carry

        def one_col(k, carry):
            def one_row(i, carry):
                work[k, rows_of(i), :] = work[k, rows_of(i), :] - dot_split(
                    chol[step, rows_of(i), :], chol[step, rows_of(k), :]
                )
                return carry

            return lax.fori_loop(k, NB, one_row, carry)

        lax.fori_loop(step + 1, NB, one_block, 0)
        return lax.fori_loop(step + 1, NB, one_col, carry)

    chol[...] = jnp.zeros_like(chol)
    lax.fori_loop(0, NB, one_panel, 0)


def inverse_of_pair(chol, inverse, p):
    between = chol[p, (p + 1) * BLK : (p + 2) * BLK, :]
    corner = -dot_split(inverse[p + 1], dot_split(inverse[p].T, between))
    return jnp.concatenate(
        [
            jnp.concatenate([inverse[p], jnp.zeros((BLK, BLK), F32)], 1),
            jnp.concatenate([corner, inverse[p + 1]], 1),
        ],
        0,
    )


def solve_rows(right_side, chol, inverse, solved, solved_high, solved_low, pairs=None):
    for p in range(0, NB, 2):
        value = right_side(p)
        if p:
            depth = range(p)
            left_high = jnp.concatenate([solved_high[k] for k in depth], 1)
            left_low = jnp.concatenate([solved_low[k] for k in depth], 1)
            right = jnp.concatenate([chol[k, p * BLK : (p + 2) * BLK, :] for k in depth], 1)
            right_high, right_low = halves(right)
            value = value - (
                dot_nt(left_high, right_high)
                + dot_nt(left_high, right_low)
                + dot_nt(left_low, right_high)
            )
        pair_inverse = pairs[p // 2] if pairs is not None else inverse_of_pair(chol, inverse, p)
        value = dot_split(value, pair_inverse)
        high, low = halves(value)
        for w in range(2):
            lanes = slice(w * BLK, (w + 1) * BLK)
            solved[p + w] = value[:, lanes]
            solved_high[p + w], solved_low[p + w] = high[:, lanes], low[:, lanes]


def pair(ref, p):
    return jnp.concatenate([ref[p], ref[p + 1]], 1)


def place_of(block_map, front, child, slots):
    for m in range(FB):
        slots[child, m] = -1
    for i in range(NB):
        slots[child, block_map[front, child, i]] = i


def kept(pattern, front, row, col):
    return (pattern[front, row, col] == 1) | (pattern[front, col, row] == 1) | (row == col)


def first_turn(core, z):
    return jnp.where((core == 0) & (z >= 4), 1, 0)


def send_blocks(tile, core, z, out):
    base = NB // 2 * core
    for turn in range(2):
        local = (z + first_turn(core, z) + turn) % 4
        block = tile[local]
        at = turn * BLK

        @pl.when(base + local >= z)
        def _():
            out[at : at + BLK, :] = block

        @pl.when(base + local < z)
        def _():
            out[at : at + BLK, :] = block.T

    block = tile[(z + 2) % 4]

    @pl.when(z % 4 < 2)
    def _():
        out[2 * BLK :, :] = block[:HALF, :]

    @pl.when(z % 4 >= 2)
    def _():
        out[2 * BLK :, :] = block.T[HALF:, :]


def static_blocks():
    where = {}
    for core in range(2):
        for z in range(NB):
            turn0 = 1 if core == 0 and z >= 4 else 0
            for turn in range(2):
                row = 4 * core + (z + turn0 + turn) % 4
                where[max(row, z), min(row, z)] = [(core * NB + z, turn * BLK, BLK)]
            if z // 4 == core:
                row = 4 * core + (z + 2) % 4
                key = (max(row, z), min(row, z))
                entry = (core * NB + z, 2 * BLK, HALF)
                known = where.setdefault(key, [])
                if z % 4 < 2:
                    known.insert(0, entry)
                else:
                    known.append(entry)
    return where


def send_child(child, z, out):
    for turn in range(4):
        row = (z + turn) % NB
        at = turn * BLK
        block = child[pl.ds(pl.multiple_of(row * BLK, BLK), BLK), :]

        @pl.when(row >= z)
        def _():
            out[at : at + BLK, :] = block

        @pl.when(row < z)
        def _():
            out[at : at + BLK, :] = block.T

    row = (z + 4) % NB
    block = child[pl.ds(pl.multiple_of(row * BLK, BLK), BLK), :]

    @pl.when(row > z)
    def _():
        out[4 * BLK :, :] = block[:HALF, :]

    @pl.when(row < z)
    def _():
        out[4 * BLK :, :] = block.T[HALF:, :]


def child_copies(gathered, children, sems):
    return [
        pltpu.make_async_copy(
            gathered.at[:, :CHILD_ROWS, :], children.at[:, :CHILD_ROWS, :], sems.at[0]
        )
    ] + [
        pltpu.make_async_copy(
            gathered.at[child * NB + 4 : child * NB + 8, 4 * BLK : CHILD_ROWS, :],
            children.at[child * NB : child * NB + 4, CHILD_ROWS:, :],
            sems.at[1 + child],
        )
        for child in range(2)
    ]


def each_gathered(block_map, front, children, visit):
    def one(n, carry):
        child, m = n // 36, n % 36
        z = jnp.where(m < 32, m // 4, m - 32)
        turn = jnp.where(m < 32, m % 4, 4)
        other = (z + turn) % NB
        row = block_map[front, child, jnp.maximum(z, other)]
        col = block_map[front, child, jnp.minimum(z, other)]
        start = pl.multiple_of(turn * BLK, BLK)
        visit(row, col, lambda: children[child * NB + z, pl.ds(start, BLK), :])
        return carry

    lax.fori_loop(0, 72, one, 0)


def ordered(block_map, front, child, order, place):
    count = jnp.int32(0)
    for parity in range(2):
        for i in range(NB):
            hit = block_map[front, child, i] % 2 == parity

            @pl.when(hit)
            def _(count=count, i=i):
                order[child, count] = i
                place[child, i] = count

            count = count + jnp.where(hit, 1, 0)
        if parity == 0:
            separators = count
    return separators


def number_of(a, b):
    return a * (a + 1) // 2 + b


def block_number(place, child, i, k):
    a, b = place[child, i], place[child, k]
    return number_of(jnp.maximum(a, b), jnp.minimum(a, b))


def add_ordered_separators(block_map, front, children, work, order, counts):
    for child in range(2):

        def one_place(a, carry):
            def other_place(b, carry):
                i, k = order[child, a], order[child, b]
                row = block_map[front, child, jnp.maximum(i, k)] // 2
                col = block_map[front, child, jnp.minimum(i, k)] // 2
                number = number_of(a, b)

                @pl.when(row >= col)
                def _():
                    add_at(work, col, row, children[child, number])

                @pl.when(row < col)
                def _():
                    add_at(work, row, col, children[child, number].T)

                return carry

            return lax.fori_loop(0, a + 1, other_place, carry)

        lax.fori_loop(0, counts[child], one_place, 0)


def add_at(ref, lead, block_row, block):
    place = pl.ds(pl.multiple_of(block_row * BLK, BLK), BLK)
    ref[lead, place, :] = ref[lead, place, :] + block


def contributions_into(corner, lower, trail):
    def visit(row, col, block):
        row_odd, col_odd = row % 2 == 1, col % 2 == 1
        row_half, col_half = row // 2, col // 2

        @pl.when(~row_odd & ~col_odd & (row >= col))
        def _():
            add_at(corner, col_half, row_half, block())

        @pl.when(~row_odd & ~col_odd & (row < col))
        def _():
            add_at(corner, row_half, col_half, block().T)

        @pl.when(row_odd & ~col_odd)
        def _():
            add_at(lower, col_half, row_half, block())

        @pl.when(~row_odd & col_odd)
        def _():
            add_at(lower, row_half, col_half, block().T)

        @pl.when(row_odd & col_odd & (row >= col))
        def _():
            add_at(trail, packed_index(row_half, col_half), 0, block())

        @pl.when(row_odd & col_odd & (row < col))
        def _():
            add_at(trail, packed_index(col_half, row_half), 0, block().T)

    return visit


def sent_row(sub, z):
    return jnp.where(sub >= z // 2, z % 2, 1 - z % 2)


def send_pair(tile, sub, z, out):
    block = tile[sent_row(sub, z)]

    @pl.when(2 * sub + sent_row(sub, z) >= z)
    def _():
        out[:BLK, :] = block

    @pl.when(2 * sub + sent_row(sub, z) < z)
    def _():
        out[:BLK, :] = block.T

    @pl.when(z % 2 == 0)
    def _():
        out[BLK:, :] = tile[1][:HALF, :]

    @pl.when(z % 2 == 1)
    def _():
        out[BLK:, :] = tile[0].T[HALF:, :]


def masked_tile(initial, pattern, front, row, local, col):
    keep = kept(pattern, front, row, col)
    return jnp.where(keep, initial[local * BLK : (local + 1) * BLK, :], 0.0)


def pack_kernel(ids, pattern_one, child_in, initial, sent, child, corner, sems):
    front_one, side, z = ids[0], ids[1], ids[2]
    copies = [pltpu.make_async_copy(child_in, child, sems.at[4])]
    for r in range(4):
        source = initial.at[2 * r * BLK : (2 * r + 1) * BLK, :BLK]
        copies.append(pltpu.make_async_copy(source, corner.at[r], sems.at[r]))
    for copy in copies:
        copy.start()
    copies[0].wait()
    send_child(child, z, sent.at[:CHILD_ROWS, :])
    for copy in copies[1:]:
        copy.wait()
    for r in range(4):
        keep = kept(pattern_one, front_one, NB * side + 2 * r, 2 * z)
        corner[r] = jnp.where(keep, corner[r], 0.0)
    send_blocks(corner, side, z, sent.at[CHILD_ROWS:, :])


def mask_kernel(
    ids,
    pattern_one,
    pattern_two,
    initial_one,
    initial_two,
    merged,
    corner_two,
    lower_two,
    row_two,
    tail_two,
    tile,
    corner_tile,
):
    front_one, side, z, front_two, sub = ids[0], ids[1], ids[2], ids[3], ids[4]
    first, second = initial_one.at[:, :BLK], initial_one.at[:, BLK:]
    for r in range(4):
        row = NB * side + 2 * r + 1
        merged[r * BLK : (r + 1) * BLK, :] = masked_tile(
            first, pattern_one, front_one, row, 2 * r + 1, 2 * z
        )
        tile[r] = masked_tile(second, pattern_one, front_one, row, 2 * r + 1, 2 * z + 1)
    send_blocks(tile, side, z, merged.at[LOWER_ROWS:, :])
    for r in range(4):
        for w in range(2):
            columns = initial_two.at[:, w * BLK : (w + 1) * BLK]
            block = masked_tile(columns, pattern_two, front_two, 4 * sub + r, r, 2 * z + w)
            at = slice(r // 2 * BLK, (r // 2 + 1) * BLK)
            if w == 0 and r % 2 == 0:
                corner_tile[r // 2] = block
            elif w == 0:
                lower_two[at, :] = block
            elif r % 2 == 0:
                row_two[at, :] = block.T
            else:
                tail_two[r // 2] = block
    send_pair(corner_tile, sub, z, corner_two)


def chol_kernel(
    ids,
    block_map,
    gathered,
    chol,
    pairs,
    lower_out,
    trail_out,
    work,
    children,
    lower,
    trail,
    inverse,
    sems,
):
    front = ids[0]
    copies = child_copies(gathered, children, sems)
    for (row, col), parts in static_blocks().items():
        start = row * BLK
        for piece, at, rows in parts:
            copies.append(
                pltpu.make_async_copy(
                    gathered.at[piece, CHILD_ROWS + at : CHILD_ROWS + at + rows, :],
                    work.at[col, start : start + rows, :],
                    sems.at[len(copies)],
                )
            )
            start += rows
    for copy in copies:
        copy.start()
    lower[...] = jnp.zeros_like(lower)
    trail[...] = jnp.zeros_like(trail)
    for copy in copies:
        copy.wait()
    each_gathered(block_map, front, children, contributions_into(work, lower, trail))
    outs = [
        pltpu.make_async_copy(lower, lower_out, sems.at[0]),
        pltpu.make_async_copy(trail, trail_out, sems.at[1]),
    ]
    for copy in outs:
        copy.start()
    factor_corner(work, chol, inverse)
    for p in range(0, NB, 2):
        pairs[p // 2] = inverse_of_pair(chol, inverse, p)
    for copy in outs:
        copy.wait()


def rest_kernel(
    ids,
    block_map,
    chol_in,
    pairs_in,
    lower_in,
    trail_in,
    merged,
    factor,
    mine,
    other,
    late,
    chol,
    pairs,
    lower,
    lower_add,
    solved,
    solved_high,
    solved_low,
    trail,
    trail_add,
    staged,
    order,
    place,
    sems,
):
    side, z, child = ids[1], ids[2], ids[4] // 2
    half = NB // 2 * BLK
    used = []

    def fetch(source, target):
        copy = pltpu.make_async_copy(source, target, sems.at[len(used)])
        copy.start()
        used.append(copy)
        return copy

    first = [fetch(pairs_in, pairs)]
    columns = {}
    for p in range(0, NB, 2):
        columns[p] = [fetch(lower_in.at[p : p + 2], lower_add.at[p : p + 2])]
        for core in range(2):
            columns[p].append(
                fetch(
                    merged.at[core * NB + p : core * NB + p + 2, :LOWER_ROWS, :],
                    lower.at[p : p + 2, core * half : (core + 1) * half, :],
                )
            )
        if p == 0:
            first.append(fetch(chol_in, chol))
    last = [fetch(trail_in, trail_add)]
    for (row, col), parts in static_blocks().items():
        start = 0
        for piece, at, rows in parts:
            last.append(
                fetch(
                    merged.at[piece, LOWER_ROWS + at : LOWER_ROWS + at + rows, :],
                    trail.at[packed_index(row, col), start : start + rows, :],
                )
            )
            start += rows
    ordered(block_map, ids[3], child, order, place)
    for copy in first:
        copy.wait()

    def right_side(p):
        for copy in columns[p]:
            copy.wait()
        return pair(lower, p) + pair(lower_add, p)

    solve_rows(right_side, chol, None, solved, solved_high, solved_low, pairs)
    for copy in last:
        copy.wait()
    for p in range(0, NB, 2):
        high = jnp.concatenate([solved_high[k, p * BLK :, :] for k in range(NB)], 1)
        low = jnp.concatenate([solved_low[k, p * BLK :, :] for k in range(NB)], 1)
        wide_high, wide_low = high[: 2 * BLK], low[: 2 * BLK]
        update = dot_nt(high, wide_high) + dot_nt(high, wide_low) + dot_nt(low, wide_high)
        for w in range(2):
            for i in range(p + w, NB):
                index = packed_index(i, p + w)
                number = block_number(place, child, i, p + w)
                half_id = jnp.where(number < SOON // 2, 0, 1)
                soon = (half_id + side) % 2 * (SOON // 2) + number - half_id * (SOON // 2)
                staged[jnp.where(number < SOON, soon, number)] = (
                    trail[index]
                    + trail_add[index]
                    - update[(i - p) * BLK : (i - p + 1) * BLK, w * BLK : (w + 1) * BLK]
                )
    outs = [
        pltpu.make_async_copy(staged.at[: SOON // 2], mine, sems.at[0]),
        pltpu.make_async_copy(staged.at[SOON // 2 : SOON], other, sems.at[1]),
        pltpu.make_async_copy(staged.at[SOON:], late, sems.at[2]),
    ]
    for copy in outs:
        copy.start()
    for r in range(NB):
        source = solved if r % 2 else chol
        start = pl.multiple_of((side * (NB // 2) + r // 2) * BLK, BLK)
        factor[r * BLK : (r + 1) * BLK, :] = source[z, pl.ds(start, BLK), :]
    for copy in outs:
        copy.wait()


def fetch_children(side, mine, refs, children, sems):
    near_mine, near_other, far_mine, far_other = refs
    half = SOON // 2
    copies = []
    for n, (ref, child, half_id) in enumerate(
        (
            (near_mine, mine, side),
            (near_other, mine, 1 - side),
            (far_mine, 1 - mine, side),
            (far_other, 1 - mine, 1 - side),
        )
    ):
        target = children.at[child, pl.ds(half * half_id, half)]
        copies.append(pltpu.make_async_copy(ref, target, sems.at[n]))
        copies[-1].start()
    return copies


def corner_copies(side_of, gathered, work, sems):
    copies = []

    def fetch(piece, first, rows, block_row, block_col, start):
        place = pl.multiple_of(block_row * BLK + start, HALF)
        copies.append(
            pltpu.make_async_copy(
                gathered.at[piece, first : first + rows, :],
                work.at[block_col, pl.ds(place, rows), :],
                sems.at[len(copies)],
            )
        )
        copies[-1].start()

    for core in range(2):
        for n, y in ((0, side_of), (1, 1 - side_of)):
            sub = 2 * y + core
            for z in range(NB):
                row = 2 * sub + sent_row(sub, z)
                top, left = jnp.maximum(row, z), jnp.minimum(row, z)
                fetch(core * NB + z, n * PAIR_ROWS, BLK, top, left, 0)
            for d in range(2):
                piece = core * NB + 2 * sub + d
                fetch(piece, n * PAIR_ROWS + BLK, HALF, 2 * sub + 1, 2 * sub, d * HALF)
    return copies


def chol_two_kernel(
    ids,
    block_map,
    gathered,
    near_mine,
    near_other,
    far_mine,
    far_other,
    chol,
    inverse,
    work,
    children,
    order,
    place,
    sems,
    corner_sems,
):
    side, front, sub = ids[1], ids[3], ids[4]
    copies = fetch_children(
        side, sub // 2, (near_mine, near_other, far_mine, far_other), children, sems
    )
    copies += corner_copies(sub // 2, gathered, work, corner_sems)
    counts = [
        jnp.minimum(ordered(block_map, front, child, order, place), MOST) for child in range(2)
    ]
    for copy in copies:
        copy.wait()
    add_ordered_separators(block_map, front, children, work, order, counts)
    factor_corner(work, chol, inverse)


def tail_kernel(
    ids,
    map_two,
    gathered,
    chol_in,
    inverse_in,
    rows_all,
    tail,
    near_mine,
    near_other,
    far_mine,
    far_other,
    near_late,
    far_late,
    factor,
    schur,
    chol,
    inverse,
    work,
    children,
    lower,
    solved,
    solved_high,
    solved_low,
    trail,
    slots,
    order,
    place,
    sems,
    corner_sems,
):
    side, z, front, sub = ids[1], ids[2], ids[3], ids[4]
    mine = sub // 2
    copies = fetch_children(
        side, mine, (near_mine, near_other, far_mine, far_other), children, sems
    )
    for n, (ref, child) in enumerate(((near_late, mine), (far_late, 1 - mine))):
        copies.append(
            pltpu.make_async_copy(ref, children.at[child, pl.ds(SOON, LATE)], sems.at[4 + n])
        )
        copies[-1].start()
    copies.append(
        pltpu.make_async_copy(
            gathered.at[pl.ds(side * NB, NB), 2 * PAIR_ROWS :, :],
            lower.at[:, : 2 * BLK, :],
            sems.at[8],
        )
    )
    copies[-1].start()
    factors = [
        pltpu.make_async_copy(chol_in, chol, sems.at[6]),
        pltpu.make_async_copy(inverse_in, inverse, sems.at[7]),
    ]
    for copy in factors:
        copy.start()
    counts = [ordered(map_two, front, child, order, place) for child in range(2)]
    place_of(map_two, front, 0, slots)
    place_of(map_two, front, 1, slots)
    for s in range(4):
        for b in range(2):
            lower[2 * s + b, 2 * BLK :, :] = rows_all[s, b * BLK : (b + 1) * BLK, :]
    trail[...] = tail[...]
    for copy in copies:
        copy.wait()
    wanted = (2 * sub, 2 * sub + 1, z)

    def one_child(child, carry):
        for slot, target in enumerate(wanted):
            i = slots[child, 2 * target + 1]

            def one_block(k, carry):
                col = map_two[front, child, k]
                index = block_number(place, child, i, k)

                @pl.when((col % 2 == 0) & (i > k))
                def _():
                    add_at(lower, col // 2, slot, children[child, index])

                @pl.when((col % 2 == 0) & (i < k))
                def _():
                    add_at(lower, col // 2, slot, children[child, index].T)

                return carry

            lax.fori_loop(0, jnp.where(i >= 0, NB, 0), one_block, 0)
        k = slots[child, 2 * z + 1]
        for slot in range(2):
            i = slots[child, 2 * wanted[slot] + 1]
            both = (i >= 0) & (k >= 0)
            index = block_number(place, child, jnp.maximum(i, 0), jnp.maximum(k, 0))

            @pl.when(both & (i >= k))
            def _():
                trail[slot] = trail[slot] + children[child, index]

            @pl.when(both & (i < k))
            def _():
                trail[slot] = trail[slot] + children[child, index].T

        return carry

    lax.fori_loop(0, 2, one_child, 0)
    for copy in factors:
        copy.wait()

    @pl.when(jnp.maximum(counts[0], counts[1]) > MOST)
    def _():
        for copy in corner_copies(mine, gathered, work, corner_sems):
            copy.wait()
        add_ordered_separators(map_two, front, children, work, order, counts)
        factor_corner_again(work, chol, inverse)

    solve_rows(lambda p: pair(lower, p), chol, inverse, solved, solved_high, solved_low)
    high = jnp.concatenate([solved_high[k] for k in range(NB)], 1)
    low = jnp.concatenate([solved_low[k] for k in range(NB)], 1)
    left_high, left_low = high[: 2 * BLK], low[: 2 * BLK]
    right_high, right_low = high[2 * BLK :], low[2 * BLK :]
    update = (
        dot_nt(left_high, right_high)
        + dot_nt(left_high, right_low)
        + dot_nt(left_low, right_high)
    )
    for r in range(2):
        schur[r * BLK : (r + 1) * BLK, :] = trail[r] - update[r * BLK : (r + 1) * BLK, :]
        start = pl.multiple_of((2 * sub + r) * BLK, BLK)
        factor[2 * r * BLK : (2 * r + 1) * BLK, :] = chol[z, pl.ds(start, BLK), :]
        factor[(2 * r + 1) * BLK : (2 * r + 2) * BLK, :] = solved[z, r * BLK : (r + 1) * BLK, :]


def call(kernel, name, outs, specs, args, scratch=(), flops=0, out_specs=None):
    return pl.pallas_call(
        kernel,
        name=name,
        out_shape=outs,
        in_specs=specs,
        out_specs=out_specs or [VMEM] * len(outs),
        scratch_shapes=list(scratch),
        compiler_params=PARAMS,
        cost_estimate=pl.CostEstimate(flops=flops, bytes_accessed=flops // 400, transcendentals=0)
        if flops
        else None,
    )(*args)


def swap(value, axis):
    return lax.ppermute(value, axis, [(0, 1), (1, 0)])


def per_device(
    child_updates,
    initial_one,
    initial_two,
    pattern_one,
    pattern_two,
    parent_map_one,
    parent_map_two,
):
    x, yh, yl = lax.axis_index("x"), lax.axis_index("yh"), lax.axis_index("yl")
    core, z = lax.axis_index("core"), lax.axis_index("front")
    ids = jnp.stack([x * 4 + yh * 2 + yl, core, z, x * 2 + yh, yl * 2 + core]).astype(jnp.int32)
    panel = (NB, NB * BLK, BLK)
    block = (BLK, BLK)

    (sent,) = call(
        pack_kernel,
        "pack",
        [shape(CHILD_ROWS + CORNER_ROWS, BLK)],
        [SMEM, SMEM, ANY, ANY],
        (ids, pattern_one, child_updates, initial_one),
        [
            pltpu.VMEM((NB * BLK, BLK), F32),
            pltpu.VMEM((4, *block), F32),
            pltpu.SemaphoreType.DMA((5,)),
        ],
    )
    gathered = lax.all_gather(sent, ("core", "front"), axis=0, tiled=False)
    ids_mask, _ = lax.optimization_barrier((ids, sent))
    merged, corner_two, lower_two, row_two, tail_two = call(
        mask_kernel,
        "mask",
        [
            shape(LOWER_ROWS + CORNER_ROWS, BLK),
            shape(PAIR_ROWS, BLK),
            shape(2 * BLK, BLK),
            shape(2 * BLK, BLK),
            shape(2, *block),
        ],
        [SMEM, SMEM, SMEM, VMEM, VMEM],
        (ids_mask, pattern_one, pattern_two, initial_one, initial_two),
        [pltpu.VMEM((4, *block), F32), pltpu.VMEM((2, *block), F32)],
    )
    corner_two = jnp.concatenate([corner_two, swap(corner_two, "yl"), lower_two], 0)
    rows_all = lax.all_gather(row_two, ("yl", "core"), axis=0, tiled=False)
    merged, gathered, corner_two, rows_all = lax.optimization_barrier(
        (merged, gathered, corner_two, rows_all)
    )
    merged_all = lax.all_gather(merged, ("core", "front"), axis=0, tiled=False)
    chol, pairs, lower_add, trail_add = call(
        chol_kernel,
        "chol",
        [shape(*panel), shape(4, 2 * BLK, 2 * BLK), shape(*panel), shape(36, *block)],
        [SMEM, SMEM, ANY],
        (ids, parent_map_one, gathered),
        [
            pltpu.VMEM(panel, F32),
            pltpu.VMEM((2 * NB, 5 * BLK, BLK), F32),
            pltpu.VMEM(panel, F32),
            pltpu.VMEM((36, *block), F32),
            pltpu.VMEM((NB, *block), F32),
            pltpu.SemaphoreType.DMA((64,)),
        ],
        flops=40_000_000_000,
        out_specs=[VMEM, VMEM, ANY, ANY],
    )
    gathered_two = lax.all_gather(corner_two, ("core", "front"), axis=0, tiled=False)
    places = pltpu.SMEM((2, NB), jnp.int32)
    factor_one, near_mine, near_other, near_late = call(
        rest_kernel,
        "rest",
        [
            shape(NB * BLK, BLK),
            shape(SOON // 2, *block),
            shape(SOON // 2, *block),
            shape(LATE, *block),
        ],
        [SMEM, SMEM] + [ANY] * 5,
        (ids, parent_map_two, chol, pairs, lower_add, trail_add, merged_all),
        [pltpu.VMEM(panel, F32), pltpu.VMEM((4, 2 * BLK, 2 * BLK), F32)]
        + [pltpu.VMEM(panel, F32)] * 3
        + [pltpu.VMEM(panel, BF16)] * 2
        + [pltpu.VMEM((36, *block), F32)] * 3
        + [places, places, pltpu.SemaphoreType.DMA((64,))],
        flops=15_000_000_000,
        out_specs=[VMEM, ANY, ANY, ANY],
    )
    far_mine = swap(near_mine, "yl")
    far_other = swap(far_mine, "core")
    packed = (near_mine, near_other, far_mine, far_other)
    given_late, _ = lax.optimization_barrier((near_late, far_mine))
    far_late = swap(given_late, "yl")
    children = pltpu.VMEM((2, 36, *block), F32)
    chol, inverse = call(
        chol_two_kernel,
        "chol_two",
        [shape(*panel), shape(NB, *block)],
        [SMEM, SMEM] + [ANY] * 5,
        (ids, parent_map_two, gathered_two, *packed),
        [
            pltpu.VMEM(panel, F32),
            children,
            places,
            places,
            pltpu.SemaphoreType.DMA((4,)),
            pltpu.SemaphoreType.DMA((40,)),
        ],
        flops=40_000_000_000,
    )
    rows = (NB, 3 * BLK, BLK)
    factor_two, schur_two = call(
        tail_kernel,
        "tail",
        [shape(4 * BLK, BLK), shape(2 * BLK, BLK)],
        [SMEM, SMEM, ANY, ANY, ANY] + [VMEM] * 2 + [ANY] * 6,
        (
            ids,
            parent_map_two,
            gathered_two,
            chol,
            inverse,
            rows_all,
            tail_two,
            *packed,
            near_late,
            far_late,
        ),
        [
            pltpu.VMEM(panel, F32),
            pltpu.VMEM((NB, *block), F32),
            pltpu.VMEM(panel, F32),
            children,
            pltpu.VMEM(rows, F32),
            pltpu.VMEM(rows, F32),
            pltpu.VMEM(rows, BF16),
            pltpu.VMEM(rows, BF16),
            pltpu.VMEM((2, *block), F32),
            pltpu.SMEM((2, FB), jnp.int32),
            places,
            places,
            pltpu.SemaphoreType.DMA((9,)),
            pltpu.SemaphoreType.DMA((40,)),
        ],
    )
    return factor_one, factor_two, schur_two


def solution(mesh):
    cut = Mesh(mesh.devices.reshape(4, 2, 2, 2, 8), LEAF + ("front",))
    tile = P(LEAF, "front")
    return jax.shard_map(
        per_device,
        mesh=cut,
        in_specs=(tile, tile, tile, P(), P(), P(), P()),
        out_specs=(tile, tile, tile),
        check_vma=False,
    )
```
